32 devices in a mesh: groups: 2 (over y), tile: 16 (over z, x, core).
Axes of the slice: x: 2, y: 2, z: 4, core: 2. Of those that a mesh axis runs over, the one named last changes fastest.
Arguments:
- features: bfloat16 [1024, 24, 2048], P(('groups', 'tile')), parts along dimension 0, may hold values from 0 to 64, as said below
- aerial_image: bfloat16 [3, 8192, 192], P(None, ('groups', 'tile')), parts along dimension 1, may hold values from -4 to 4
- blocks: int32 [64, 2], P('groups'), parts along dimension 0, may hold values from 0 to 127, as said below
- routes: int32 [64, 1], P('groups'), parts along dimension 0, may hold values from 0 to 15; in each aligned block of 32 rows (0 to 31, 32 to 63, ...) at most 4 rows name the same one
- w_one: bfloat16 [2048, 256], replicated, may hold values from -0.125 to 0.125
- w_depth: bfloat16 [3, 9, 2048], replicated, may hold values from -2 to 2
- w_rates: bfloat16 [3, 2048, 256], replicated, may hold values from -0.125 to 0.125
- w_pool: bfloat16 [2048, 256], replicated, may hold values from -0.125 to 0.125
- w_proj: bfloat16 [1280, 256], replicated, may hold values from -0.15625 to 0.15625
- w_first: bfloat16 [16, 9, 256, 256], P('tile'), may hold values from -0.125 to 0.125
- w_color: bfloat16 [16, 27, 256], P('tile'), may hold values from -1.25 to 1.25
- w_second: bfloat16 [16, 9, 256, 256], P('tile'), may hold values from -0.125 to 0.125
- w_head: bfloat16 [16, 6, 256], P('tile'), may hold values from -0.375 to 0.375
Outputs:
- aspp_features: bfloat16 [1024, 24, 256], P(('groups', 'tile')), parts along dimension 0
- context: float32 [512], P('groups'), parts along dimension 0
- refined: bfloat16 [64, 6, 1024], P(('groups', 'tile')), parts along dimension 0
The draws below stay inside these ranges and needn't reach their ends.
There are 2 independent parts, one for each index of `groups`. The reference program is written for one: setup_inputs(seed, part) draws one part's arguments, and reference() takes and returns one part's arrays. A program takes and returns all parts, laid end to end along the dimension named above; an argument that names none is the same for every part. Nothing has to cross between parts.
Inputs may be any that keep to these rules, and one draw needn't show every extreme that they name: `features`: Non-negative activations. Blocks are distinct; block rows lie below 128 and block columns below 6; no strip of 32 feature rows holds more than 6 blocks and one holds exactly 6. `routes`: at most 4 blocks go to one refiner and one refiner receives exactly 4; every refiner receives one or more.
All inputs are finite; a program needn't handle non-finite values.
Results may differ from the reference program's by a relative error of at most 0.0065.
Values may be sent and summed in bfloat16 or wider, within the bound.
A program may use at most 128 MiB of HBM per device.

```python
import math
import jax
import jax.numpy as jnp
import numpy as np
from jax import lax

C_IN = 2048
A = 256
REF = 256
NCLS = 6
R_DEV = 32
COLS = 24
BLK = 32
CAP = 4
OWN = 6
NB = 32
NROWS = 512
EXPERTS = 16
STRIP_BLOCK_ROWS = 8
REGION_BLOCK_COLUMNS = 6
GRID = 48


def draw_features(key, part):
    key_base, key_rows, key_cols, key_chan = jax.random.split(jax.random.fold_in(key, 11), 4)
    rows_at = jnp.arange(NROWS, dtype=jnp.float32) / max(NROWS - 1, 1)
    row_jitter = jnp.exp(jax.random.uniform(key_rows, (NROWS,), minval=-0.5, maxval=0.5))
    col_scale = jnp.exp(jax.random.uniform(key_cols, (COLS,), minval=-0.5, maxval=0.5))
    chan_scale = jnp.exp(jax.random.uniform(key_chan, (C_IN,), minval=-0.7, maxval=0.7))
    base = jnp.minimum(jnp.abs(jax.random.normal(key_base, (NROWS, COLS, C_IN))), 5.0)
    rising = 3.0 ** rows_at
    values = 0.6 * base * (rising * row_jitter)[:, None, None] * col_scale[None, :, None] * chan_scale[None, None, :]
    return values.astype(jnp.float32).astype(jnp.bfloat16)


def draw_blocks(key, part):
    key_order, key_full, key_place, key_shuffle = jax.random.split(jax.random.fold_in(key, 23), 4)
    strip_count = NROWS // R_DEV
    slot_total = strip_count * OWN
    order_perm = jax.random.permutation(key_order, slot_total)
    slot_rank = jnp.argsort(order_perm)
    full_strip = jax.random.randint(key_full, (), 0, strip_count)
    slot_ids = jnp.arange(slot_total, dtype=jnp.int32)
    score = jnp.where(slot_ids // OWN == full_strip, slot_ids - slot_total, slot_rank.astype(jnp.int32))
    chosen = jnp.argsort(score)[:NB].astype(jnp.int32)
    chosen = chosen[jax.random.permutation(key_shuffle, NB)]
    strip_index_list = chosen // OWN
    within = chosen % OWN
    spacing = GRID // OWN
    block_location = within * spacing + jax.random.randint(key_place, (NB,), 0, spacing)
    block_row_count = strip_index_list * STRIP_BLOCK_ROWS + block_location // REGION_BLOCK_COLUMNS
    block_cols = block_location % REGION_BLOCK_COLUMNS
    return jnp.stack([block_row_count, block_cols], axis=1).astype(jnp.int32)


def level_of(rng, dims, shards, smallest, high):
    def one(dim, shards_of):
        heights = jax.random.uniform(jax.random.fold_in(jax.random.fold_in(rng, 6), dim), (shards_of,), jnp.float32, smallest / len(shards), high / len(shards))
        return jnp.repeat(jnp.exp(heights), dims[dim] // shards_of).reshape((-1,) + (1,) * (len(dims) - dim - 1))

    loudness = one(*shards[0])
    for cut in shards[1:]:
        loudness = loudness * one(*cut)
    return loudness


def routed_block(own_key, own, number, rows, count, top, reach, lean):
    sequence = jax.random.permutation(own_key, count)
    heavy_load, common = load_shares(count, rows * top, reach, lean, True), load_shares(count, rows * top, reach, lean, False)
    places = jnp.arange(count)

    def named(lengths, rotation):
        used = int((lengths > 0).sum())
        fixed = max(1, used // 4)
        passed = fixed + (places - fixed + rotation * (used - fixed)) % max(1, count - fixed)
        return jnp.zeros((count,), jnp.int32).at[sequence[jnp.where(places < fixed, places, passed)]].set(jnp.asarray(lengths, jnp.int32))

    lengths = jnp.where(number % 4 == 0, named(heavy_load, number // 4), named(common, number - number // 4 - 1))
    mixed = jax.random.permutation(jax.random.fold_in(own, 3), count)
    giver, taker = mixed[0:count // 2 * 2:2], mixed[1:count // 2 * 2:2]
    room = jnp.minimum(lengths[giver] - 1, reach - lengths[taker]) // 2
    room = jnp.where((giver == sequence[0]) | (taker == sequence[0]) | (lengths[taker] == 0), 0, jnp.maximum(room, 0))
    passed = jax.random.randint(jax.random.fold_in(own, 4), (count // 2,), 0, 1 << 20) % (room + 1)
    lengths = lengths.at[giver].add(-passed).at[taker].add(passed)
    items = jnp.searchsorted(jnp.cumsum(lengths), jnp.arange(rows * top), side="right").astype(jnp.int32)
    listing = items.reshape(top, rows).T
    listing = listing[jax.random.permutation(jax.random.fold_in(own, 1), rows)]
    rotation = jax.random.randint(jax.random.fold_in(own, 2), (rows, 1), 0, top)
    return jnp.take_along_axis(listing, (jnp.arange(top)[None, :] + rotation) % top, axis=1)


def load_shares(count, total, reach, slope, full):
    loads = [(1 << 20) // math.isqrt(grade ** slope) + 1 for grade in range(1, count + 1)]
    largest = reach if full else min(reach, max(-(-total // count), total * loads[0] // sum(loads)))
    least = 1 if total - largest >= count - 1 else 0
    counts, rest = [largest] + [least] * (count - 1), total - largest - least * (count - 1)
    while rest > 0:
        candidates = [i for i in range(1, count) if counts[i] < largest] or [i for i in range(1, count) if counts[i] < reach]
        whole, budget = sum([loads[i] for i in candidates]), rest
        for i in candidates:
            more = min(reach - counts[i], max(1, budget * loads[i] // whole), rest)
            counts[i] = counts[i] + more
            rest = rest - more
    return np.array(counts)


def bell_draw(rng, extent, width, most, cuts=(), kind=jnp.bfloat16):
    factor_of = level_of(rng, extent, cuts, -0.22, 0.18) if cuts else 1.0
    array = jax.random.normal(rng, extent, jnp.float32) * width * factor_of
    return jnp.minimum(jnp.maximum(array, -most), most).astype(kind)


def setup_inputs(seed: int = 0, part: int = 0) -> dict:
    seeds = jax.random.split(jax.random.key(seed), 14)
    part_keys = jax.random.split(jax.random.fold_in(seeds[13], part), 14)
    features = draw_features(jax.random.fold_in(jax.random.fold_in(seeds[13], part), 71), part)
    aerial_image = bell_draw(part_keys[1], (3, NROWS * 8, COLS * 8), 1.0, 4.0, ((1, 16),))
    blocks = draw_blocks(jax.random.fold_in(jax.random.fold_in(seeds[13], part), 71), part)
    routes_keys = jax.random.split(jax.random.fold_in(part_keys[3], 1), NB // NB)
    routes_turns = jax.random.permutation(jax.random.fold_in(part_keys[3], 3), NB // NB)
    routes = jax.vmap(lambda own, number: routed_block(jax.random.fold_in(part_keys[3], 2), own, number, NB, EXPERTS, 1, CAP, 2))(routes_keys, routes_turns).reshape((NB, 1))
    w_one = bell_draw(seeds[4], (C_IN, A), C_IN ** -0.5, 0.125)
    w_depth = bell_draw(seeds[5], (3, 9, C_IN), 9 ** -0.5, 2.0)
    w_rates = bell_draw(seeds[6], (3, C_IN, A), C_IN ** -0.5, 0.125)
    w_pool = bell_draw(seeds[7], (C_IN, A), C_IN ** -0.5, 0.125)
    w_proj = bell_draw(seeds[8], (5 * A, A), (5 * A) ** -0.5, 0.15625)
    w_first = bell_draw(seeds[9], (EXPERTS, 9, A, REF), (9 * A) ** -0.5, 0.125, ((0, 16),))
    w_color = bell_draw(seeds[10], (EXPERTS, 27, REF), 27 ** -0.5, 1.25, ((0, 16),))
    w_second = bell_draw(seeds[11], (EXPERTS, 9, REF, REF), (9 * REF) ** -0.5, 0.125, ((0, 16),))
    w_head = bell_draw(seeds[12], (EXPERTS, NCLS, REF), REF ** -0.5, 0.375, ((0, 16),))
    return dict(features=features, aerial_image=aerial_image, blocks=blocks, routes=routes, w_one=w_one, w_depth=w_depth, w_rates=w_rates, w_pool=w_pool, w_proj=w_proj, w_first=w_first, w_color=w_color, w_second=w_second, w_head=w_head)


atrous_rates = (6, 12, 18)
reach_rows = 18


def upsample_table(block_side):
    cells = block_side // 8
    pixels = jnp.arange(block_side, dtype=jnp.float32)
    source = jnp.clip((pixels + 0.5) / 8.0 - 0.5, 0.0, float(cells - 1))
    centres = jnp.arange(cells, dtype=jnp.float32)
    weights_table = jnp.maximum(1.0 - jnp.abs(source[:, None] - centres[None, :]), 0.0)
    return (weights_table[:, None, :, None] * weights_table[None, :, None, :]).reshape(block_side * block_side, cells * cells)


def conv_taps(inputs, kernel):
    block_count, block_side = inputs.shape[0], inputs.shape[1]
    padded = jnp.pad(inputs, ((0, 0), (1, 1), (1, 1), (0, 0)))
    running = jnp.zeros((block_count * block_side * block_side, kernel.shape[2]), jnp.float32)
    for kernel_tap in range(9):
        row_off, col_off = kernel_tap // 3, kernel_tap % 3
        window = padded[:, row_off:row_off + block_side, col_off:col_off + block_side, :]
        running = running + jnp.dot(window.reshape(block_count * block_side * block_side, -1), kernel[kernel_tap], preferred_element_type=jnp.float32)
    return running


def conv_color(colors, kernel):
    block_count, block_side = colors.shape[0], colors.shape[2]
    padded = jnp.pad(colors, ((0, 0), (0, 0), (1, 1), (1, 1)))
    running = jnp.zeros((block_count, block_side, block_side, kernel.shape[1]), jnp.float32)
    for kernel_tap in range(9):
        row_off, col_off = kernel_tap // 3, kernel_tap % 3
        window = padded[:, :, row_off:row_off + block_side, col_off:col_off + block_side]
        running = running + jnp.einsum("scpq,cr->spqr", window.astype(jnp.float32), kernel[3 * kernel_tap:3 * kernel_tap + 3].astype(jnp.float32))
    return running.reshape(block_count * block_side * block_side, -1)


def refine(crop_data, colors, w_first, w_color, w_second, w_head):
    block_count, block_side = colors.shape[0], colors.shape[2]
    upsampled = jnp.einsum("pk,ska->spa", upsample_table(block_side), crop_data.astype(jnp.float32), precision=lax.Precision.HIGHEST)
    upsampled = upsampled.astype(jnp.bfloat16).reshape(block_count, block_side, block_side, -1)
    first_maps = conv_taps(upsampled, w_first) + conv_color(colors, w_color)
    first_maps = jnp.maximum(first_maps, 0.0).astype(jnp.bfloat16).reshape(block_count, block_side, block_side, -1)
    second = jnp.maximum(conv_taps(first_maps, w_second), 0.0).astype(jnp.bfloat16)
    second = second.reshape(block_count, block_side * block_side, -1)
    logits = jnp.einsum("spr,nr->snp", second.astype(jnp.float32), w_head.astype(jnp.float32))
    return logits.astype(jnp.bfloat16)


def reference(features, aerial_image, blocks, routes, w_one, w_depth, w_rates, w_pool, w_proj, w_first, w_color, w_second, w_head):
    height, col_count, channels = features.shape
    branch_width = w_one.shape[1]
    cells = BLK // 8
    running = jnp.sum(features, axis=(0, 1), dtype=jnp.float32)
    pooled = running / (height * col_count)
    context = jnp.maximum(jnp.dot(pooled, w_pool.astype(jnp.float32), precision=lax.Precision.HIGHEST), 0.0)
    offset_amount = jnp.dot(context, w_proj[4 * branch_width:].astype(jnp.float32), precision=lax.Precision.HIGHEST)
    padded = jnp.pad(features, ((reach_rows, reach_rows), (reach_rows, reach_rows), (0, 0)))
    depth_weights = w_depth.astype(jnp.float32)

    def strip_output(strip_id):
        window = lax.dynamic_slice_in_dim(padded, (strip_id * R_DEV).astype(jnp.int32), R_DEV + 2 * reach_rows, 0)
        centre_cells = window[reach_rows:reach_rows + R_DEV, reach_rows:reach_rows + col_count, :].reshape(R_DEV * col_count, channels)
        branches = [jnp.maximum(jnp.dot(centre_cells, w_one, preferred_element_type=jnp.float32), 0.0)]
        for branch_id, dilation in enumerate(atrous_rates):
            running_sum = jnp.zeros((R_DEV, col_count, channels), jnp.float32)
            for kernel_tap in range(9):
                row_at = reach_rows + (kernel_tap // 3 - 1) * dilation
                col_at = reach_rows + (kernel_tap % 3 - 1) * dilation
                running_sum = running_sum + window[row_at:row_at + R_DEV, col_at:col_at + col_count, :] * depth_weights[branch_id, kernel_tap]
            depth_map = jnp.maximum(running_sum, 0.0).astype(jnp.bfloat16)
            branches.append(jnp.maximum(jnp.dot(depth_map.reshape(R_DEV * col_count, channels), w_rates[branch_id], preferred_element_type=jnp.float32), 0.0))
        stacked = jnp.concatenate(branches, axis=1).astype(jnp.bfloat16)
        blended_sum = jnp.dot(stacked, w_proj[:4 * branch_width], preferred_element_type=jnp.float32) + offset_amount
        return jnp.maximum(blended_sum, 0.0).astype(jnp.bfloat16).reshape(R_DEV, col_count, branch_width)

    aspp_features = lax.map(strip_output, jnp.arange(height // R_DEV, dtype=jnp.int32)).reshape(height, col_count, branch_width)

    def one_block(block_id):
        row_at = blocks[block_id, 0].astype(jnp.int32)
        col_at = blocks[block_id, 1].astype(jnp.int32)
        expert_id = routes[block_id, 0].astype(jnp.int32)
        zero_index = jnp.zeros((), jnp.int32)
        crop_data = lax.dynamic_slice(aspp_features, (cells * row_at, cells * col_at, zero_index), (cells, cells, branch_width)).reshape(1, cells * cells, branch_width)
        colors = lax.dynamic_slice(aerial_image, (zero_index, row_at * BLK, col_at * BLK), (3, BLK, BLK))[None]
        return refine(crop_data, colors, w_first[expert_id], w_color[expert_id], w_second[expert_id], w_head[expert_id])[0]

    refined = lax.map(one_block, jnp.arange(NB, dtype=jnp.int32))
    return (aspp_features, context, refined)
```

```python
import functools

import jax
import jax.numpy as jnp
import numpy as np
from jax import lax
from jax.experimental import pallas as pl
from jax.experimental.pallas import tpu as pltpu
from jax.sharding import PartitionSpec as P

BLK = 32
CAP = 4
CELLS = 4
RATES = (6, 12, 18)
REACH = 18
CHUNK = 512
F32 = jnp.float32
BF16 = jnp.bfloat16


def split_three(value):
    high = value.astype(BF16)
    rest = value - high.astype(F32)
    mid = rest.astype(BF16)
    low = (rest - mid.astype(F32)).astype(BF16)
    return high, mid, low


def exact_row_dot(row, weights):
    high, mid, low = split_three(row)
    stacked = jnp.concatenate(
        [high.astype(F32), mid.astype(F32), low.astype(F32), jnp.zeros((13, row.shape[1]), F32)], axis=0
    ).astype(BF16)
    product = jnp.dot(stacked, weights, preferred_element_type=F32)
    return product[0:1] + product[1:2] + product[2:3]


def pyramid_kernel(
    tiles, rows, cols, channels, width,
    feat_hbm, w_one_hbm, w_rates_hbm, w_depth_ref, w_pool_hbm, w_proj_hbm, image_hbm, first_hbm, second_hbm,
    color_ref, head_ref, table_ref, blocks_ref, routes_ref, block_list, route_list,
    aspp_ref, context_ref, refined_ref,
    image, first, second, crops_ref, mine_ref, taps_ref, grid_b, patches, scores, back_out, back_in, colors_out, back_send, back_recv,
    own_pick, spread_pick, feat, w_one, w_rates, w_pool, w_proj, halo, grown, depth, acc, sums, sums_in, crops_out, crops_in, colors_in,
    local_sem, halo_send, halo_recv, sum_send, sum_recv, color_send, color_recv, crop_send, crop_recv,
):
    me = lax.axis_index("tile")
    chunks = channels // CHUNK
    edge = REACH * cols
    cells = rows * cols
    count = routes_ref.shape[1]
    held = count // tiles * 8

    local = [
        pltpu.make_async_copy(source, target, local_sem.at[n])
        for n, (source, target) in enumerate(
            ((feat_hbm, feat), (w_one_hbm, w_one), (w_rates_hbm, w_rates), (w_pool_hbm, w_pool), (w_proj_hbm, w_proj),
             (image_hbm, image), (first_hbm, first), (second_hbm, second))
        )
    ]
    for copy in local:
        copy.start()

    barrier = pltpu.get_barrier_semaphore()

    def greet(step, carry):
        peer = lax.rem(me + step, tiles)
        pl.semaphore_signal(barrier, inc=1, device_id={"tile": peer}, device_id_type=pl.DeviceIdType.MESH)
        return carry

    lax.fori_loop(1, tiles, greet, 0)
    pl.semaphore_wait(barrier, tiles - 1)

    def halo_copy(side, c):
        lanes = pl.ds(pl.multiple_of(c * CHUNK, CHUNK), CHUNK)
        first = cells - edge if side == 0 else 0
        return pltpu.make_async_remote_copy(
            src_ref=feat_hbm.at[pl.ds(first, edge), lanes],
            dst_ref=halo.at[side, :, lanes],
            send_sem=halo_send.at[side, c],
            recv_sem=halo_recv.at[side, c],
            device_id={"tile": lax.rem(me + 1, tiles) if side == 0 else lax.rem(me + tiles - 1, tiles)},
            device_id_type=pl.DeviceIdType.MESH,
        )

    has_next = me < tiles - 1
    has_prev = me > 0

    def send_halo(c, carry):
        @pl.when(has_next)
        def _():
            halo_copy(0, c).start()

        @pl.when(has_prev)
        def _():
            halo_copy(1, c).start()

        return carry

    lax.fori_loop(0, chunks, send_halo, 0)

    def peer_copy(step, source, target, send, recv):
        return pltpu.make_async_remote_copy(
            src_ref=source, dst_ref=target, send_sem=send.at[step], recv_sem=recv.at[step],
            device_id={"tile": lax.rem(me + step, tiles)}, device_id_type=pl.DeviceIdType.MESH,
        )

    def sum_copy(step):
        return peer_copy(step, sums, sums_in.at[step], sum_send, sum_recv)

    def color_copy(step):
        peer = lax.rem(me + step, tiles)
        return peer_copy(step, colors_out.at[pl.ds(pl.multiple_of(peer * 16, 16), 16)], colors_in.at[me], color_send, color_recv)

    def crop_copy(step):
        peer = lax.rem(me + step, tiles)
        return peer_copy(step, crops_out.at[peer], crops_in.at[me], crop_send, crop_recv)

    def back_copy(step):
        peer = lax.rem(me + step, tiles)
        return peer_copy(
            step, back_out.at[pl.ds(pl.multiple_of(peer * held, held), held)], back_in.at[me], back_send, back_recv
        )

    def each_peer(function):
        def body(step, carry):
            function(step)
            return carry

        lax.fori_loop(1, tiles, body, 0)

    local[0].wait()

    def sum_rows(n, totals):
        block = feat[pl.ds(pl.multiple_of(n * 16, 16), 16), :].astype(F32)
        return totals + block[0:8] + block[8:16]

    totals = lax.fori_loop(0, cells // 16, sum_rows, jnp.zeros((8, channels), F32))
    sums[...] = jnp.sum(totals, axis=0, keepdims=True)
    each_peer(lambda step: sum_copy(step).start())

    local[1].wait()
    local[2].wait()
    tall = 256

    @pl.loop(0, cells // tall)
    def _(m):
        span = pl.ds(pl.multiple_of(m * tall, tall), tall)
        acc[0, span, :] = jnp.dot(feat[span, :], w_one[...], preferred_element_type=F32)
        for k in range(3):
            acc[k + 1, span, :] = jnp.zeros((tall, width), F32)

    @pl.when(jnp.logical_not(has_prev))
    def _():
        grown[0:edge, :] = jnp.zeros((edge, CHUNK), F32)

    @pl.when(jnp.logical_not(has_next))
    def _():
        grown[edge + cells :, :] = jnp.zeros((edge, CHUNK), F32)

    def widen(source, start, count, lanes):
        @pl.loop(0, count // 48)
        def _(n):
            grown[pl.ds(pl.multiple_of(start + n * 48, 8), 48), :] = source[
                pl.ds(pl.multiple_of(n * 48, 16), 48), lanes
            ].astype(F32)

    experts = routes_ref[...].astype(F32)
    square = (count, count)
    down, over = lax.broadcasted_iota(jnp.int32, square, 0), lax.broadcasted_iota(jnp.int32, square, 1)
    spread = jnp.broadcast_to(experts, square)
    upright = route_list[...].astype(F32)
    rank = jnp.sum(jnp.where((upright == spread) & (down < over), 1.0, 0.0), axis=0, keepdims=True)
    slot_of = experts * CAP + rank
    strip_blocks = rows // CELLS
    local_row = blocks_ref[0:1, :].astype(F32) - lax.convert_element_type(me * strip_blocks, F32)
    is_mine = (local_row >= 0) & (local_row < strip_blocks)
    row_col = block_list[:, 0:1].astype(F32) - lax.convert_element_type(me * strip_blocks, F32)
    mine_col = (row_col >= 0) & (row_col < strip_blocks)
    base = jnp.where(is_mine, local_row * (CELLS * cols) + blocks_ref[1:2, :].astype(F32) * CELLS, -1e6)
    to_me = jnp.where(experts == lax.convert_element_type(me, F32), rank, -1.0)

    mine_rank = jnp.sum(jnp.where(mine_col & (down < over), 1.0, 0.0), axis=0, keepdims=True)
    own_row = lax.broadcasted_iota(jnp.int32, (128, 1), 0)
    hit = is_mine & (mine_rank == (own_row >> 4).astype(F32))
    own_base = jnp.max(jnp.where(hit, jnp.broadcast_to(base, (128, count)), -1e6), axis=1, keepdims=True)
    wanted_cell = own_base + (((own_row >> 2) & 3) * cols + (own_row & 3)).astype(F32)
    cell_at = lax.broadcasted_iota(jnp.int32, (128, cells), 1).astype(F32)
    own_pick[...] = (cell_at == wanted_cell).astype(F32).astype(BF16)

    own_lane = lax.broadcasted_iota(jnp.int32, (1, 128), 1)
    rank_col = jnp.sum(jnp.where(is_mine & (over < down), 1.0, 0.0), axis=1, keepdims=True)
    slot_col = upright * CAP + jnp.sum(jnp.where((upright == spread) & (over < down), 1.0, 0.0), axis=1, keepdims=True)
    hit = mine_col & (rank_col == (own_lane >> 4).astype(F32))
    own_slot = jnp.max(jnp.where(hit, jnp.broadcast_to(slot_col, (count, 128)), -1.0), axis=0, keepdims=True)

    @pl.loop(0, tiles // 4)
    def _(n):
        row = lax.broadcasted_iota(jnp.int32, (256, 1), 0) + n * 256
        hit = (own_slot == (row >> 4).astype(F32)) & ((own_lane & 15) == (row & 15))
        spread_pick[pl.ds(pl.multiple_of(n * 256, 256), 256), :] = hit.astype(F32).astype(BF16)

    def lookup(slot, values, fill):
        shape = (slot.shape[0], count)
        hit = jnp.broadcast_to(slot, shape) == jnp.broadcast_to(slot_of, shape)
        return jnp.max(jnp.where(hit, jnp.broadcast_to(values, shape), fill), axis=1, keepdims=True)

    local[5].wait()
    parts_high = image.shape[0]
    across = parts_high // 3
    group = 256
    line = lax.broadcasted_iota(jnp.int32, (group, 1), 0)
    lane = lax.broadcasted_iota(jnp.int32, (1, BLK * BLK), 1)
    source = lax.broadcasted_iota(jnp.int32, (1, parts_high), 1)
    source_channel = (source >= across).astype(jnp.int32) + (source >= 2 * across).astype(jnp.int32)
    source_block = (source - source_channel * across) // BLK
    deep = lax.broadcasted_iota(jnp.int32, (parts_high, 1), 0)
    keep = ((deep & (BLK - 1)) == (lane & (BLK - 1)))
    tall_rows = image.shape[1]
    image_row = lax.broadcasted_iota(jnp.int32, (tall_rows, 1), 0)
    colors_out[...] = jnp.zeros(colors_out.shape, BF16)

    @pl.loop(0, strip_blocks)
    def _(at):
        select = (image_row == at * BLK + (lane >> 5)).astype(F32).astype(BF16)
        strips = jnp.dot(image[...], select, preferred_element_type=F32)
        strips = jnp.where(keep, strips, 0.0).astype(BF16)

        @pl.loop(0, tiles * 16 // group)
        def _(n):
            row = line + n * group
            found = lookup((row >> 2).astype(F32), base, -1e6)
            wanted = (at * (CELLS * cols) + source_block * CELLS).astype(F32)
            chosen = ((found == wanted) & ((row & 3) == source_channel)).astype(F32).astype(BF16)
            span = pl.ds(pl.multiple_of(n * group, group), group)
            colors_out[span, :] += jnp.dot(chosen, strips, preferred_element_type=F32).astype(BF16)

    def one_chunk(c, carry):
        @pl.when(c == chunks - 2)
        def _():
            each_peer(lambda step: color_copy(step).start())

        lanes = pl.ds(pl.multiple_of(c * CHUNK, CHUNK), CHUNK)
        widen(feat, edge, cells, lanes)

        @pl.when(has_prev)
        def _():
            halo_copy(0, c).wait_recv()
            widen(halo.at[0], 0, edge, lanes)

        @pl.when(has_next)
        def _():
            halo_copy(1, c).wait_recv()
            widen(halo.at[1], edge + cells, edge, lanes)

        for half in range(CHUNK // 128):
            inner = slice(half * 128, half * 128 + 128)
            outer = pl.ds(pl.multiple_of(c * CHUNK + half * 128, 128), 128)
            for k, d in enumerate(RATES):
                taps = [
                    jnp.broadcast_to(w_depth_ref[t, k : k + 1, outer].astype(F32), (8, 128)) for t in range(9)
                ]

                def weigh(parts, column, taps=taps):
                    total = None
                    for i in range(3):
                        tap = jnp.concatenate([taps[3 * i + column]] * (parts[i].shape[0] // 8), axis=0)
                        term = parts[i] * tap
                        total = term if total is None else total + term
                    return total

                @pl.loop(0, rows // 2, unroll=4)
                def _(pair, d=d, weigh=weigh, inner=inner, k=k):
                    results = []
                    for r in range(2):
                        parts = []
                        for i in (-1, 0, 1):
                            start = pl.multiple_of((REACH + i * d + r) * cols + pair * (2 * cols), 8)
                            parts.append(grown[pl.ds(start, cols), inner])
                        low = -(-(cols - d) // 8) * 8
                        high = (d // 8) * 8
                        middle = weigh(parts, 1)
                        left = weigh([p[:low] for p in parts], 0)
                        right = weigh([p[high:] for p in parts], 2)
                        fill = jnp.zeros((d, 128), F32)
                        left = jnp.concatenate([fill, left[: cols - d]], axis=0)
                        right = jnp.concatenate([right[d - high :], fill], axis=0)
                        results.append(jnp.maximum(middle + left + right, 0.0))
                    depth[k, pl.ds(pl.multiple_of(pair * (2 * cols), 16), 2 * cols), inner] = jnp.concatenate(
                        results, axis=0
                    ).astype(BF16)

        for k in range(3):
            @pl.loop(0, cells // tall)
            def _(m, k=k):
                span = pl.ds(pl.multiple_of(m * tall, tall), tall)
                acc[k + 1, span, :] += jnp.dot(depth[k, span, :], w_rates[k, lanes, :], preferred_element_type=F32)

        return carry

    lax.fori_loop(0, chunks, one_chunk, 0)

    each_peer(lambda step: sum_copy(step).wait_recv())

    def add_sums(step, total):
        return total + sums_in[step]

    total = lax.fori_loop(1, tiles, add_sums, sums[...])
    pooled = total / (cells * tiles)
    local[3].wait()
    local[4].wait()
    context = jnp.maximum(exact_row_dot(pooled, w_pool[...]), 0.0)
    context_ref[...] = context
    offset = exact_row_dot(context, w_proj[4 * width :, :])

    @pl.loop(0, cells // tall)
    def _(m):
        span = pl.ds(pl.multiple_of(m * tall, tall), tall)
        blended = jnp.broadcast_to(offset, (tall, width))
        for k in range(4):
            branch = jnp.maximum(acc[k, span, :], 0.0).astype(BF16)
            blended += jnp.dot(branch, w_proj[k * width : (k + 1) * width, :], preferred_element_type=F32)
        aspp_ref[span, :] = jnp.maximum(blended, 0.0).astype(BF16)

    per = CAP * CELLS * CELLS
    own_crops = jnp.dot(own_pick[...], aspp_ref[...], preferred_element_type=F32).astype(BF16)

    @pl.loop(0, tiles // 4)
    def _(n):
        rows_of = pl.ds(pl.multiple_of(n * 256, 256), 256)
        found = jnp.dot(spread_pick[rows_of, :], own_crops, preferred_element_type=F32).astype(BF16)
        for t in range(4):
            crops_out[n * 4 + t] = found[t * per : (t + 1) * per]

    crops_in[me] = crops_out[me]
    each_peer(lambda step: crop_copy(step).start())
    colors_in[me] = colors_out[pl.ds(pl.multiple_of(me * 16, 16), 16), :]
    each_peer(lambda step: color_copy(step).wait_recv())

    def add_colors(n, total):
        return total + colors_in[n].astype(F32)

    mine_ref[...] = lax.fori_loop(0, tiles, add_colors, jnp.zeros(mine_ref.shape, F32))
    side, pixels = BLK, BLK * BLK
    wide = lax.broadcasted_iota(jnp.int32, (16, pixels), 1)
    row_at, col_at = wide >> 5, wide & (side - 1)
    colors = mine_ref[...]
    pieces = []
    for i in (-1, 0, 1):
        for j in (-1, 0, 1):
            moved = colors if i == 0 and j == 0 else pltpu.roll(colors, (-(side * i + j)) % pixels, 1)
            inside = (row_at + i >= 0) & (row_at + i < side) & (col_at + j >= 0) & (col_at + j < side)
            pieces.append(jnp.where(inside, moved, 0.0))
    patches[...] = jnp.concatenate(pieces, axis=0).T.astype(BF16)
    blank = jnp.zeros((side, 3 * width), BF16)
    grid_b[0:side, :] = blank
    grid_b[side + pixels :, :] = blank
    tall = 512
    local[6].wait()
    local[7].wait()
    scores[...] = jnp.zeros(scores.shape, F32)
    col = lax.broadcasted_iota(jnp.int32, (tall, width), 0) & (side - 1)

    each_peer(lambda step: crop_copy(step).wait_recv())

    def add_crops(n, total):
        return total + crops_in[n].astype(F32)

    crops_ref[...] = lax.fori_loop(0, tiles, add_crops, jnp.zeros(crops_ref.shape, F32)).astype(BF16)

    for tap in range(9):
        part = jnp.dot(crops_ref[...], first[tap * width : (tap + 1) * width, :], preferred_element_type=F32).astype(BF16)
        for block in range(CAP):
            taps_ref[block, tap * 16 : tap * 16 + 16, :] = part[block * 16 : block * 16 + 16]

    @pl.loop(0, CAP)
    def _(block):
        tap_row = lax.broadcasted_iota(jnp.int32, (144, 27), 0)
        channel = (tap_row & 15) - block * 4
        wanted_tap = (tap_row >> 4) * 3 + channel
        spread_taps = (channel >= 0) & (channel < 3) & (wanted_tap == lax.broadcasted_iota(jnp.int32, (144, 27), 1))
        tap_weights = jnp.dot(
            spread_taps.astype(F32).astype(BF16), color_ref[...], preferred_element_type=F32
        ).astype(BF16)

        @pl.loop(0, pixels // tall)
        def _(m):
            at = pl.multiple_of(m * tall, tall)
            total = jnp.dot(patches[pl.ds(at, tall), :], tap_weights, preferred_element_type=F32)
            total += jnp.dot(table_ref[pl.ds(at, tall), :], taps_ref[block], preferred_element_type=F32)
            total = jnp.maximum(total, 0.0)
            before = jnp.where(col == 0, 0.0, pltpu.roll(total, 1, 0))
            after = jnp.where(col == side - 1, 0.0, pltpu.roll(total, tall - 1, 0))
            inner = pl.ds(pl.multiple_of(side + at, side), tall)
            grid_b[inner, 0:width] = before.astype(BF16)
            grid_b[inner, width : 2 * width] = total.astype(BF16)
            grid_b[inner, 2 * width :] = after.astype(BF16)

        @pl.loop(0, pixels // tall)
        def _(m):
            at = pl.multiple_of(m * tall, tall)
            total = jnp.zeros((tall, width), F32)
            for i in range(3):
                total += jnp.dot(
                    grid_b[pl.ds(pl.multiple_of(at + side * i, side), tall), :],
                    second[3 * width * i : 3 * width * (i + 1), :],
                    preferred_element_type=F32,
                )
            total = jnp.maximum(total, 0.0).astype(BF16)
            found = lax.dot_general(
                head_ref[...], total, (((1,), (1,)), ((), ())), preferred_element_type=F32
            )
            scores[pl.ds(pl.multiple_of(block * 8, 8), head_ref.shape[0]), pl.ds(at, tall)] = found

    finished = scores[...].astype(BF16)
    step_rows = min(tiles * held, 256)
    item = lax.broadcasted_iota(jnp.int32, (step_rows, 1), 0)
    given = lax.broadcasted_iota(jnp.int32, (step_rows, 8 * CAP), 1)
    listed = lax.broadcasted_iota(jnp.int32, (step_rows, count), 1)

    @pl.loop(0, tiles * held // step_rows)
    def _(n):
        number = item + n * step_rows
        slot = jnp.max(
            jnp.where(listed == (number >> 3), jnp.broadcast_to(to_me, (step_rows, count)), -1.0), axis=1, keepdims=True
        )
        pick = ((given >> 3).astype(F32) == slot) & ((given & 7) == (number & 7))
        back_out[pl.ds(pl.multiple_of(n * step_rows, step_rows), step_rows), :] = jnp.dot(
            pick.astype(F32).astype(BF16), finished, preferred_element_type=F32
        ).astype(BF16)

    each_peer(lambda step: back_copy(step).start())
    back_in[me] = back_out[pl.ds(pl.multiple_of(me * held, held), held), :]
    each_peer(lambda step: back_copy(step).wait_recv())

    def add_back(n, total):
        return total + back_in[n].astype(F32)

    refined_ref[...] = lax.fori_loop(0, tiles, add_back, jnp.zeros(refined_ref.shape, F32)).astype(BF16)

    def drain(step):
        sum_copy(step).wait_send()
        color_copy(step).wait_send()
        crop_copy(step).wait_send()
        back_copy(step).wait_send()

    each_peer(drain)

    def drain_halo(c, carry):
        @pl.when(has_next)
        def _():
            halo_copy(0, c).wait_send()

        @pl.when(has_prev)
        def _():
            halo_copy(1, c).wait_send()

        return carry

    lax.fori_loop(0, chunks, drain_halo, 0)


def upsample_taps():
    pixels = np.arange(BLK, dtype=np.float32)
    source = np.clip((pixels + 0.5) / 8.0 - 0.5, 0.0, CELLS - 1.0)
    table = np.maximum(1.0 - np.abs(source[:, None] - np.arange(CELLS, dtype=np.float32)[None, :]), 0.0)
    moved = []
    for i in (-1, 0, 1):
        shifted = np.zeros_like(table)
        for p in range(BLK):
            if 0 <= p + i < BLK:
                shifted[p] = table[p + i]
        moved.append(shifted)
    moved = np.stack(moved)
    return np.einsum("ipa,jqb->pqijab", moved, moved).reshape(BLK * BLK, 9 * CELLS * CELLS)


def pyramid(tiles, rows, cols, features, image, blocks, routes, w_one, w_rates, w_depth, w_pool, w_proj,
            w_first, w_color, w_second, w_head):
    channels, width = w_one.shape
    cells = rows * cols
    per = CAP * CELLS * CELLS
    chunks = channels // CHUNK
    edge = REACH * cols
    held = routes.shape[0] // tiles * 8
    pixels = BLK * BLK
    whole = pl.BlockSpec(memory_space=pltpu.VMEM)
    away = pl.BlockSpec(memory_space=pl.ANY)
    dma = pltpu.SemaphoreType.DMA
    image = image.transpose(0, 2, 1).reshape(-1, image.shape[1])
    first, second = w_first.reshape(9 * width, width), w_second.reshape(9 * width, width)
    return pl.pallas_call(
        functools.partial(pyramid_kernel, tiles, rows, cols, channels, width),
        out_shape=(
            jax.ShapeDtypeStruct((cells, width), BF16),
            jax.ShapeDtypeStruct((1, width), F32),
            jax.ShapeDtypeStruct((held, pixels), BF16),
        ),
        in_specs=[away, away, away, whole, away, away, away, away, away, whole, whole, whole, whole, whole, whole, whole],
        out_specs=(whole, whole, whole),
        scratch_shapes=[
            pltpu.VMEM(image.shape, BF16),
            pltpu.VMEM(first.shape, BF16),
            pltpu.VMEM(second.shape, BF16),
            pltpu.VMEM((per, width), BF16),
            pltpu.VMEM((16, pixels), F32),
            pltpu.VMEM((CAP, 144, width), BF16),
            pltpu.VMEM((pixels + 2 * BLK, 3 * width), BF16),
            pltpu.VMEM((pixels, 144), BF16),
            pltpu.VMEM((CAP * 8, pixels), F32),
            pltpu.VMEM((tiles * held, pixels), BF16),
            pltpu.VMEM((tiles, held, pixels), BF16),
            pltpu.VMEM((tiles * 16, pixels), BF16),
            dma((tiles,)),
            dma((tiles,)),
            pltpu.VMEM((128, cells), BF16),
            pltpu.VMEM((tiles * per, 128), BF16),
            pltpu.VMEM((cells, channels), BF16),
            pltpu.VMEM(w_one.shape, BF16),
            pltpu.VMEM(w_rates.shape, BF16),
            pltpu.VMEM(w_pool.shape, BF16),
            pltpu.VMEM(w_proj.shape, BF16),
            pltpu.VMEM((2, edge, channels), BF16),
            pltpu.VMEM((cells + 2 * edge, CHUNK), F32),
            pltpu.VMEM((3, cells, CHUNK), BF16),
            pltpu.VMEM((4, cells, width), F32),
            pltpu.VMEM((1, channels), F32),
            pltpu.VMEM((tiles, 1, channels), F32),
            pltpu.VMEM((tiles, per, width), BF16),
            pltpu.VMEM((tiles, per, width), BF16),
            pltpu.VMEM((tiles, 16, pixels), BF16),
            dma((8,)),
            dma((2, chunks)),
            dma((2, chunks)),
            dma((tiles,)),
            dma((tiles,)),
            dma((tiles,)),
            dma((tiles,)),
            dma((tiles,)),
            dma((tiles,)),
        ],
        compiler_params=pltpu.CompilerParams(collective_id=0, has_side_effects=True, vmem_limit_bytes=60 << 20),
        name="pyramid",
    )(
        features.reshape(cells, channels), w_one, w_rates, w_depth.transpose(1, 0, 2), w_pool, w_proj, image, first, second,
        w_color, w_head, jnp.asarray(upsample_taps(), BF16), blocks.T, routes.T, blocks, routes,
    )


def shards(
    tiles,
    features,
    aerial_image,
    blocks,
    routes,
    w_one,
    w_depth,
    w_rates,
    w_pool,
    w_proj,
    w_first,
    w_color,
    w_second,
    w_head,
):
    rows, cols, channels = features.shape
    width = w_one.shape[1]
    aspp, context, refined = pyramid(
        tiles, rows, cols, features, aerial_image, blocks, routes, w_one, w_rates, w_depth, w_pool, w_proj,
        w_first[0], w_color[0], w_second[0], w_head[0],
    )
    refined = refined.reshape(-1, 8, BLK * BLK)[:, : w_head.shape[1], :]
    return aspp.reshape(rows, cols, width), context.reshape(width), refined


def solution(mesh):
    return jax.shard_map(
        functools.partial(shards, mesh.shape["tile"]),
        mesh=mesh,
        in_specs=(
            P(("groups", "tile"), None, None),
            P(None, ("groups", "tile"), None),
            P("groups", None),
            P("groups", None),
            P(),
            P(),
            P(),
            P(),
            P(),
            P("tile", None, None, None),
            P("tile", None, None),
            P("tile", None, None, None),
            P("tile", None, None),
        ),
        out_specs=(
            P(("groups", "tile"), None, None),
            P("groups"),
            P(("groups", "tile"), None, None),
        ),
        check_vma=False,
    )
```

```python
import functools

import jax
import jax.numpy as jnp
import numpy as np
from jax import lax
from jax.experimental import pallas as pl
from jax.experimental.pallas import tpu as pltpu
from jax.sharding import PartitionSpec as P

BLK = 32
CAP = 4
CELLS = 4
RATES = (6, 12, 18)
REACH = 18
CHUNK = 256
HIGH = 4
QUARTERS = 4
AHEAD = 4
F32 = jnp.float32
BF16 = jnp.bfloat16


def split_three(value):
    high = value.astype(BF16)
    rest = value - high.astype(F32)
    mid = rest.astype(BF16)
    low = (rest - mid.astype(F32)).astype(BF16)
    return high, mid, low


def exact_row_dot(row, weights):
    high, mid, low = split_three(row)
    stacked = jnp.concatenate(
        [high.astype(F32), mid.astype(F32), low.astype(F32), jnp.zeros((13, row.shape[1]), F32)], axis=0
    ).astype(BF16)
    product = jnp.dot(stacked, weights, preferred_element_type=F32)
    return product[0:1] + product[1:2] + product[2:3]


def pyramid_kernel(
    tiles, rows, cols, channels, width,
    feat_hbm, w_one_hbm, w_rates_hbm, w_depth_hbm, w_pool_hbm, w_proj_hbm, image_hbm, first_hbm, second_hbm,
    color_hbm, head_hbm, table_hbm, blocks_hbm, routes_hbm,
    aspp_ref, context_ref, refined_ref,
    feat, w_one, w_rates, w_depth_ref, w_pool, w_proj, image, first, second, color_ref, head_ref, table_ref, blocks_ref, routes_ref,
    halo, grown, depth, acc, sums, sums_in, own_colors, own_pick, crop_pick, back_pick, mine_ref, crops_ref, offset_ref,
    taps_ref, grid_b, patches, scores,
    colors_out, colors_in0, colors_in1, colors_in2, crops_out, crops_in0, crops_in1, crops_in2,
    back_out, back_in0, back_in1, back_in2,
    local_sem, halo_send, halo_recv, sum_send, sum_recv, color_send, color_recv, crop_send, crop_recv, back_send, back_recv,
):
    me = lax.axis_index("tile")
    chunks = channels // CHUNK
    edge = REACH * cols
    cells = rows * cols
    count = routes_ref.shape[1]
    classes = head_ref.shape[0]
    half, low_count = tiles // 2, tiles // (2 * HIGH)
    core = lax.rem(me, 2)
    low = lax.rem(me // 2, low_count)
    high = me // (2 * low_count)

    local = [
        pltpu.make_async_copy(source, target, local_sem.at[n])
        for n, (source, target) in enumerate(
            ((feat_hbm, feat), (blocks_hbm, blocks_ref), (routes_hbm, routes_ref), (w_one_hbm, w_one), (image_hbm, image),
             (w_depth_hbm, w_depth_ref), (w_rates_hbm, w_rates), (w_pool_hbm, w_pool), (w_proj_hbm, w_proj),
             (color_hbm, color_ref), (head_hbm, head_ref), (table_hbm, table_ref), (first_hbm, first), (second_hbm, second))
        )
    ]
    for copy in local:
        copy.start()

    mate = me + 1 - 2 * core

    def low_peer(step):
        return (high * low_count + lax.rem(low + step, low_count)) * 2 + core

    def high_peer(step):
        return (lax.rem(high + step, HIGH) * low_count + low) * 2 + core

    has_next = me < tiles - 1
    has_prev = me > 0
    barrier = pltpu.get_barrier_semaphore()

    def greet(peer):
        pl.semaphore_signal(barrier, inc=1, device_id={"tile": peer}, device_id_type=pl.DeviceIdType.MESH)

    def greet_low(step, carry):
        greet(low_peer(step))
        return carry

    outward = jnp.where(core == 1, me + 1, me - 1)
    has_outward = (outward >= 0) & (outward < tiles)

    @pl.when(has_outward)
    def _():
        greet(outward)

    greet(mate)
    lax.fori_loop(1, low_count, greet_low, 0)
    for step in range(1, HIGH):
        greet(high_peer(step))
    pl.semaphore_wait(barrier, low_count - 1 + HIGH + has_outward.astype(jnp.int32))

    def send(source, target, send_sem, recv_sem, peer):
        return pltpu.make_async_remote_copy(
            src_ref=source, dst_ref=target, send_sem=send_sem, recv_sem=recv_sem,
            device_id={"tile": peer}, device_id_type=pl.DeviceIdType.MESH,
        )

    def halo_copy(side, c):
        lanes = pl.ds(pl.multiple_of(c * CHUNK, CHUNK), CHUNK)
        return send(
            feat_hbm.at[pl.ds(cells - edge if side == 0 else 0, edge), lanes], halo.at[side, :, lanes],
            halo_send.at[side, c], halo_recv.at[side, c],
            lax.rem(me + 1, tiles) if side == 0 else lax.rem(me + tiles - 1, tiles),
        )

    def send_halo(c):
        @pl.when(has_next)
        def _():
            halo_copy(0, c).start()

        @pl.when(has_prev)
        def _():
            halo_copy(1, c).start()

    def steps(number, function):
        def body(step, carry):
            function(step)
            return carry

        lax.fori_loop(1, number, body, 0)

    def exchange(out, in0, in1, in2, sems, middle, last):
        (n1, at1, peer1), (n2, at2, peer2) = middle, last
        mine = out.at[core]

        def copy0():
            return send(out.at[1 - core], in0, sems[0].at[0], sems[1].at[0], mate)

        def copy1(step):
            return send(mine.at[lax.rem(at1 + step, n1)], in1.at[step - 1], sems[0].at[step], sems[1].at[step], peer1(step))

        def copy2(step):
            slot = n1 + step
            return send(
                mine.at[at1, lax.rem(at2 + step, n2)], in2.at[step - 1], sems[0].at[slot], sems[1].at[slot], peer2(step)
            )

        def start():
            copy0().start()

        def pass_middle():
            copy0().wait_recv()

            def add(n, carry):
                mine[n] = (mine[n].astype(F32) + in0[n].astype(F32)).astype(BF16)
                return carry

            lax.fori_loop(0, n1, add, 0)
            steps(n1, lambda step: copy1(step).start())

        def pass_last():
            steps(n1, lambda step: copy1(step).wait_recv())

            def add(step, total):
                return total + in1[step - 1].astype(F32)

            mine[at1] = lax.fori_loop(1, n1, add, mine[at1].astype(F32)).astype(BF16)
            steps(n2, lambda step: copy2(step).start())

        def finish():
            steps(n2, lambda step: copy2(step).wait_recv())

            def add(step, total):
                return total + in2[step - 1].astype(F32)

            return lax.fori_loop(1, n2, add, mine[at1, at2].astype(F32))

        def drain():
            copy0().wait_send()
            steps(n1, lambda step: copy1(step).wait_send())
            steps(n2, lambda step: copy2(step).wait_send())

        return start, pass_middle, pass_last, finish, drain

    by_low, by_high = (low_count, low, low_peer), (HIGH, high, high_peer)
    colors_start, colors_middle, colors_last, colors_finish, colors_drain = exchange(
        colors_out, colors_in0, colors_in1, colors_in2, (color_send, color_recv), by_high, by_low
    )
    crops_start, crops_middle, crops_last, crops_finish, crops_drain = exchange(
        crops_out, crops_in0, crops_in1, crops_in2, (crop_send, crop_recv), by_low, by_high
    )
    back_start, back_middle, back_last, back_finish, back_drain = exchange(
        back_out, back_in0, back_in1, back_in2, (back_send, back_recv), by_low, by_high
    )

    def sum_low(step):
        return send(sums.at[0], sums_in.at[step - 1], sum_send.at[step], sum_recv.at[step], low_peer(step))

    def sum_high(step):
        slot = low_count + step
        return send(sums.at[1], sums_in.at[slot - 2], sum_send.at[slot], sum_recv.at[slot], high_peer(step))

    def sum_mate():
        return send(sums.at[2], sums_in.at[low_count + HIGH - 2], sum_send.at[0], sum_recv.at[0], mate)

    def add_sums(start, number, total):
        return lax.fori_loop(0, number, lambda n, value: value + sums_in[start + n], total)

    send_halo(0)
    local[0].wait()

    def sum_rows(n, totals):
        block = feat[pl.ds(pl.multiple_of(n * 16, 16), 16), :].astype(F32)
        return totals + block[0:8] + block[8:16]

    totals = lax.fori_loop(0, cells // 16, sum_rows, jnp.zeros((8, channels), F32))
    sums[0] = jnp.sum(totals, axis=0, keepdims=True)
    steps(low_count, lambda step: sum_low(step).start())
    send_halo(1)

    tall = 256
    local[3].wait()

    @pl.loop(0, cells // tall)
    def _(m):
        span = pl.ds(pl.multiple_of(m * tall, tall), tall)
        acc[0, span, :] = jnp.dot(feat[span, :], w_one[...], preferred_element_type=F32)
        for k in range(3):
            acc[k + 1, span, :] = jnp.zeros((tall, width), F32)

    @pl.when(jnp.logical_not(has_prev))
    def _():
        grown[0:edge, :] = jnp.zeros((edge, CHUNK), F32)

    @pl.when(jnp.logical_not(has_next))
    def _():
        grown[edge + cells :, :] = jnp.zeros((edge, CHUNK), F32)

    def widen(source, start, count, lanes):
        @pl.loop(0, count // 48)
        def _(n):
            grown[pl.ds(pl.multiple_of(start + n * 48, 8), 48), :] = source[
                pl.ds(pl.multiple_of(n * 48, 16), 48), lanes
            ].astype(F32)

    local[1].wait()
    local[2].wait()
    experts = routes_ref[...].astype(F32)
    square = (count, count)
    down, over = lax.broadcasted_iota(jnp.int32, square, 0), lax.broadcasted_iota(jnp.int32, square, 1)
    spread = jnp.broadcast_to(experts, square)

    def stand(row):
        return jnp.sum(jnp.where(down == over, jnp.broadcast_to(row, square), 0.0), axis=1, keepdims=True)

    upright = stand(experts)
    rank = jnp.sum(jnp.where((upright == spread) & (down < over), 1.0, 0.0), axis=0, keepdims=True)
    strip_blocks = rows // CELLS
    local_row = blocks_ref[0:1, :].astype(F32) - lax.convert_element_type(me * strip_blocks, F32)
    block_col = blocks_ref[1:2, :].astype(F32)
    is_mine = (local_row >= 0) & (local_row < strip_blocks)
    row_col = stand(local_row)
    mine_col = (row_col >= 0) & (row_col < strip_blocks)
    to_me = jnp.where(experts == lax.convert_element_type(me, F32), rank, -1.0)
    mine_rank = jnp.sum(jnp.where(mine_col & (down < over), 1.0, 0.0), axis=0, keepdims=True)
    rank_col = jnp.sum(jnp.where(is_mine & (over < down), 1.0, 0.0), axis=1, keepdims=True)
    slot_col = upright * CAP + jnp.sum(jnp.where((upright == spread) & (over < down), 1.0, 0.0), axis=1, keepdims=True)

    def own_values(index, values):
        shape = (index.shape[0], count)
        hit = jnp.broadcast_to(is_mine & (mine_rank == index), shape)
        return jnp.max(jnp.where(hit, jnp.broadcast_to(values, shape), -1e6), axis=1, keepdims=True)

    own_row = lax.broadcasted_iota(jnp.int32, (128, 1), 0)
    own_base = own_values((own_row >> 4).astype(F32), local_row * (CELLS * cols) + block_col * CELLS)
    wanted_cell = own_base + (((own_row >> 2) & 3) * cols + (own_row & 3)).astype(F32)
    cell_at = lax.broadcasted_iota(jnp.int32, (128, cells), 1).astype(F32)
    own_pick[...] = (cell_at == wanted_cell).astype(F32).astype(BF16)

    own_lane = lax.broadcasted_iota(jnp.int32, (1, 128), 1)

    def own_slots(index):
        hit = mine_col & (rank_col == index.astype(F32))
        return jnp.max(jnp.where(hit, jnp.broadcast_to(slot_col, (count, 128)), -1.0), axis=0, keepdims=True)

    own_slot = own_slots(own_lane >> 4)
    per = CAP * CELLS * CELLS

    @pl.loop(0, tiles)
    def _(n):
        rest = lax.rem(n, half)
        tile = (lax.rem(rest, HIGH) * low_count + rest // HIGH) * 2 + n // half
        row = lax.broadcasted_iota(jnp.int32, (per, 1), 0)
        hit = (own_slot == (tile * CAP + (row >> 4)).astype(F32)) & ((own_lane & 15) == (row & 15))
        crop_pick[pl.ds(pl.multiple_of(n * per, per), per), :] = hit.astype(F32).astype(BF16)

        item = back_pick.shape[0] // tiles
        span = item // QUARTERS
        line = lax.broadcasted_iota(jnp.int32, (item, 1), 0)
        quarter = sum((line >= q * span).astype(jnp.int32) for q in range(1, QUARTERS))
        line = line - quarter * span
        place = sum((line >= p * classes).astype(jnp.int32) for p in range(1, span // classes)) + jnp.zeros_like(line)
        kind = line - place * classes
        listed = lax.broadcasted_iota(jnp.int32, (item, count), 1)
        wanted = listed == tile * (span // classes) + place
        slot = jnp.max(jnp.where(wanted, jnp.broadcast_to(to_me, (item, count)), -1.0), axis=1, keepdims=True)
        given = lax.broadcasted_iota(jnp.int32, (item, 128), 1)
        pick = (((given >> 3) & 3).astype(F32) == slot) & ((given & 7) == kind) & ((given >> 5) == quarter)
        back_pick[pl.ds(pl.multiple_of(n * item, 16), item), :] = pick.astype(F32).astype(BF16)

    steps(low_count, lambda step: sum_low(step).wait_recv())
    sums[1] = add_sums(0, low_count - 1, sums[0])
    steps(HIGH, lambda step: sum_high(step).start())
    for c in range(2, AHEAD):
        send_halo(c)

    local[4].wait()
    parts_high = image.shape[0]
    across = parts_high // 3
    line = lax.broadcasted_iota(jnp.int32, (32, 1), 0)
    lane = lax.broadcasted_iota(jnp.int32, (1, BLK * BLK), 1)
    source = lax.broadcasted_iota(jnp.int32, (1, parts_high), 1)
    source_channel = (source >= across).astype(jnp.int32) + (source >= 2 * across).astype(jnp.int32)
    source_block = ((source - source_channel * across) // BLK).astype(F32)
    deep = lax.broadcasted_iota(jnp.int32, (parts_high, 1), 0)
    keep = ((deep & (BLK - 1)) == (lane & (BLK - 1)))
    tall_rows = image.shape[1]
    image_row = lax.broadcasted_iota(jnp.int32, (tall_rows, 1), 0)
    own_colors[...] = jnp.zeros(own_colors.shape, F32)
    color_slot = (line >> 2).astype(F32)
    color_row, color_block = own_values(color_slot, local_row), own_values(color_slot, block_col)

    @pl.loop(0, strip_blocks)
    def _(at):
        select = (image_row == at * BLK + (lane >> 5)).astype(F32).astype(BF16)
        strips = jnp.dot(image[...], select, preferred_element_type=F32)
        strips = jnp.where(keep, strips, 0.0).astype(BF16)
        chosen = (color_row == at.astype(F32)) & (color_block == source_block) & ((line & 3) == source_channel)
        own_colors[...] += jnp.dot(chosen.astype(F32).astype(BF16), strips, preferred_element_type=F32)

    color_values = own_colors[...].astype(BF16)
    lane_slot = own_slots(own_lane >> 2)[:, 0:32]

    @pl.loop(0, tiles)
    def _(n):
        row = lax.broadcasted_iota(jnp.int32, (16, 1), 0)
        tile = lax.rem(n, half) * 2 + n // half
        hit = (lane_slot == (tile * CAP + (row >> 2)).astype(F32)) & ((own_lane[:, 0:32] & 3) == (row & 3))
        found = jnp.dot(hit.astype(F32).astype(BF16), color_values, preferred_element_type=F32).astype(BF16)
        rest = lax.rem(n, half)
        colors_out[n // half, rest // low_count, lax.rem(rest, low_count)] = found

    colors_start()
    local[5].wait()
    local[6].wait()

    def one_chunk(c, carry):
        @pl.when(c < chunks - AHEAD)
        def _():
            send_halo(c + AHEAD)

        @pl.when(c == 2)
        def _():
            colors_middle()

        @pl.when(c == 3)
        def _():
            steps(HIGH, lambda step: sum_high(step).wait_recv())
            sums[2] = add_sums(low_count - 1, HIGH - 1, sums[1])
            sum_mate().start()

        @pl.when(c == chunks - 3)
        def _():
            sum_mate().wait_recv()
            local[7].wait()
            local[8].wait()
            pooled = add_sums(low_count + HIGH - 2, 1, sums[2]) / (cells * tiles)
            context = jnp.maximum(exact_row_dot(pooled, w_pool[...]), 0.0)
            context_ref[...] = context
            offset_ref[...] = exact_row_dot(context, w_proj[4 * width :, :])

        @pl.when(c == chunks - 2)
        def _():
            colors_last()

        lanes = pl.ds(pl.multiple_of(c * CHUNK, CHUNK), CHUNK)
        widen(feat, edge, cells, lanes)

        @pl.when(has_prev)
        def _():
            halo_copy(0, c).wait_recv()
            widen(halo.at[0], 0, edge, lanes)

        @pl.when(has_next)
        def _():
            halo_copy(1, c).wait_recv()
            widen(halo.at[1], edge + cells, edge, lanes)

        for half in range(CHUNK // 128):
            inner = slice(half * 128, half * 128 + 128)
            outer = pl.ds(pl.multiple_of(c * CHUNK + half * 128, 128), 128)
            for k, d in enumerate(RATES):
                taps = [
                    jnp.broadcast_to(w_depth_ref[t, k : k + 1, outer].astype(F32), (8, 128)) for t in range(9)
                ]

                def weigh(parts, column, taps=taps):
                    total = None
                    for i in range(3):
                        tap = jnp.concatenate([taps[3 * i + column]] * (parts[i].shape[0] // 8), axis=0)
                        term = parts[i] * tap
                        total = term if total is None else total + term
                    return total

                @pl.loop(0, rows // 2, unroll=4)
                def _(pair, d=d, weigh=weigh, inner=inner, k=k):
                    results = []
                    for r in range(2):
                        parts = []
                        for i in (-1, 0, 1):
                            start = pl.multiple_of((REACH + i * d + r) * cols + pair * (2 * cols), 8)
                            parts.append(grown[pl.ds(start, cols), inner])
                        low = -(-(cols - d) // 8) * 8
                        high = (d // 8) * 8
                        middle = weigh(parts, 1)
                        left = weigh([p[:low] for p in parts], 0)
                        right = weigh([p[high:] for p in parts], 2)
                        fill = jnp.zeros((d, 128), F32)
                        left = jnp.concatenate([fill, left[: cols - d]], axis=0)
                        right = jnp.concatenate([right[d - high :], fill], axis=0)
                        results.append(jnp.maximum(middle + left + right, 0.0))
                    depth[k, pl.ds(pl.multiple_of(pair * (2 * cols), 16), 2 * cols), inner] = jnp.concatenate(
                        results, axis=0
                    ).astype(BF16)

        for k in range(3):
            @pl.loop(0, cells // tall)
            def _(m, k=k):
                span = pl.ds(pl.multiple_of(m * tall, tall), tall)
                acc[k + 1, span, :] += jnp.dot(depth[k, span, :], w_rates[k, lanes, :], preferred_element_type=F32)

        return carry

    lax.fori_loop(0, chunks, one_chunk, 0)

    @pl.loop(0, cells // tall)
    def _(m):
        span = pl.ds(pl.multiple_of(m * tall, tall), tall)
        blended = jnp.broadcast_to(offset_ref[...], (tall, width))
        for k in range(4):
            branch = jnp.maximum(acc[k, span, :], 0.0).astype(BF16)
            blended += jnp.dot(branch, w_proj[k * width : (k + 1) * width, :], preferred_element_type=F32)
        aspp_ref[span, :] = jnp.maximum(blended, 0.0).astype(BF16)

    own_crops = jnp.dot(own_pick[...], aspp_ref[...], preferred_element_type=F32).astype(BF16)

    @pl.loop(0, tiles // 4)
    def _(n):
        rows_of = pl.ds(pl.multiple_of(n * (4 * per), 4 * per), 4 * per)
        found = jnp.dot(crop_pick[rows_of, :], own_crops, preferred_element_type=F32).astype(BF16)
        for t in range(4):
            at = n * 4 + t
            rest = lax.rem(at, half)
            crops_out[at // half, rest // HIGH, lax.rem(rest, HIGH)] = found[t * per : (t + 1) * per]

    crops_start()
    crops_middle()

    mine_ref[...] = colors_finish()
    side, pixels = BLK, BLK * BLK
    wide = lax.broadcasted_iota(jnp.int32, (16, pixels), 1)
    row_at, col_at = wide >> 5, wide & (side - 1)
    colors = mine_ref[...]
    pieces = []
    for i in (-1, 0, 1):
        for j in (-1, 0, 1):
            moved = colors if i == 0 and j == 0 else pltpu.roll(colors, (-(side * i + j)) % pixels, 1)
            inside = (row_at + i >= 0) & (row_at + i < side) & (col_at + j >= 0) & (col_at + j < side)
            pieces.append(jnp.where(inside, moved, 0.0))
    patches[...] = jnp.concatenate(pieces, axis=0).T.astype(BF16)

    crops_last()
    blank = jnp.zeros((side, 3 * width), BF16)
    grid_b[0:side, :] = blank
    grid_b[side + pixels :, :] = blank
    tall = 512
    for n in range(9, 14):
        local[n].wait()
    scores[...] = jnp.zeros(scores.shape, F32)
    col = lax.broadcasted_iota(jnp.int32, (tall, width), 0) & (side - 1)

    crops_ref[...] = crops_finish().astype(BF16)

    for tap in range(9):
        part = jnp.dot(crops_ref[...], first[tap * width : (tap + 1) * width, :], preferred_element_type=F32).astype(BF16)
        for block in range(CAP):
            taps_ref[block, tap * 16 : tap * 16 + 16, :] = part[block * 16 : block * 16 + 16]

    @pl.loop(0, CAP)
    def _(block):
        tap_row = lax.broadcasted_iota(jnp.int32, (144, 27), 0)
        channel = (tap_row & 15) - block * 4
        wanted_tap = (tap_row >> 4) * 3 + channel
        spread_taps = (channel >= 0) & (channel < 3) & (wanted_tap == lax.broadcasted_iota(jnp.int32, (144, 27), 1))
        tap_weights = jnp.dot(
            spread_taps.astype(F32).astype(BF16), color_ref[...], preferred_element_type=F32
        ).astype(BF16)

        @pl.loop(0, pixels // tall)
        def _(m):
            at = pl.multiple_of(m * tall, tall)
            total = jnp.dot(patches[pl.ds(at, tall), :], tap_weights, preferred_element_type=F32)
            total += jnp.dot(table_ref[pl.ds(at, tall), :], taps_ref[block], preferred_element_type=F32)
            total = jnp.maximum(total, 0.0)
            before = jnp.where(col == 0, 0.0, pltpu.roll(total, 1, 0))
            after = jnp.where(col == side - 1, 0.0, pltpu.roll(total, tall - 1, 0))
            inner = pl.ds(pl.multiple_of(side + at, side), tall)
            grid_b[inner, 0:width] = before.astype(BF16)
            grid_b[inner, width : 2 * width] = total.astype(BF16)
            grid_b[inner, 2 * width :] = after.astype(BF16)

        @pl.loop(0, pixels // tall)
        def _(m):
            at = pl.multiple_of(m * tall, tall)
            total = jnp.zeros((tall, width), F32)
            for i in range(3):
                total += jnp.dot(
                    grid_b[pl.ds(pl.multiple_of(at + side * i, side), tall), :],
                    second[3 * width * i : 3 * width * (i + 1), :],
                    preferred_element_type=F32,
                )
            total = jnp.maximum(total, 0.0).astype(BF16)
            found = lax.dot_general(
                head_ref[...], total, (((1,), (1,)), ((), ())), preferred_element_type=F32
            )
            wide_part = pixels // QUARTERS
            for q in range(tall // wide_part):
                quarter = m * (tall // wide_part) + q
                scores[pl.ds(pl.multiple_of(quarter * (8 * CAP) + block * 8, 8), classes), :] = found[
                    :, q * wide_part : (q + 1) * wide_part
                ]

    finished = scores[...].astype(BF16)
    item = back_pick.shape[0] // tiles

    @pl.loop(0, tiles // 4)
    def _(n):
        rows_of = pl.ds(pl.multiple_of(n * (4 * item), 16), 4 * item)
        found = jnp.dot(back_pick[rows_of, :], finished, preferred_element_type=F32).astype(BF16)
        for t in range(4):
            at = n * 4 + t
            rest = lax.rem(at, half)
            back_out[at // half, rest // HIGH, lax.rem(rest, HIGH)] = found[t * item : (t + 1) * item]

    back_start()
    back_middle()
    back_last()
    result = back_finish()
    span = item // QUARTERS
    wide_part = pixels // QUARTERS
    for q in range(QUARTERS):
        for p in range(span // classes):
            start = q * span + p * classes
            refined_ref[p, :, q * wide_part : (q + 1) * wide_part] = result[start : start + classes].astype(BF16)

    steps(low_count, lambda step: sum_low(step).wait_send())
    steps(HIGH, lambda step: sum_high(step).wait_send())
    sum_mate().wait_send()
    colors_drain()
    crops_drain()
    back_drain()

    def drain_halo(c, carry):
        @pl.when(has_next)
        def _():
            halo_copy(0, c).wait_send()

        @pl.when(has_prev)
        def _():
            halo_copy(1, c).wait_send()

        return carry

    lax.fori_loop(0, chunks, drain_halo, 0)


def upsample_taps():
    pixels = np.arange(BLK, dtype=np.float32)
    source = np.clip((pixels + 0.5) / 8.0 - 0.5, 0.0, CELLS - 1.0)
    table = np.maximum(1.0 - np.abs(source[:, None] - np.arange(CELLS, dtype=np.float32)[None, :]), 0.0)
    moved = []
    for i in (-1, 0, 1):
        shifted = np.zeros_like(table)
        for p in range(BLK):
            if 0 <= p + i < BLK:
                shifted[p] = table[p + i]
        moved.append(shifted)
    moved = np.stack(moved)
    return np.einsum("ipa,jqb->pqijab", moved, moved).reshape(BLK * BLK, 9 * CELLS * CELLS)


def pyramid(tiles, rows, cols, features, image, blocks, routes, w_one, w_rates, w_depth, w_pool, w_proj,
            w_first, w_color, w_second, w_head):
    channels, width = w_one.shape
    cells = rows * cols
    per = CAP * CELLS * CELLS
    chunks = channels // CHUNK
    edge = REACH * cols
    places = routes.shape[0] // tiles
    classes = w_head.shape[0]
    pixels = BLK * BLK
    item = places * classes * QUARTERS
    low_count = tiles // (2 * HIGH)
    part = pixels // QUARTERS
    whole = pl.BlockSpec(memory_space=pltpu.VMEM)
    away = pl.BlockSpec(memory_space=pl.ANY)
    dma = pltpu.SemaphoreType.DMA
    image = image.transpose(0, 2, 1).reshape(-1, image.shape[1])
    first, second = w_first.reshape(9 * width, width), w_second.reshape(9 * width, width)
    operands = (
        features.reshape(cells, channels), w_one, w_rates, w_depth.transpose(1, 0, 2), w_pool, w_proj, image, first, second,
        w_color, w_head, jnp.asarray(upsample_taps(), BF16), blocks.T, routes.T,
    )

    def exchange_buffers(shape, middle, last):
        return [
            pltpu.VMEM((2, middle, last, *shape), BF16),
            pltpu.VMEM((middle, last, *shape), BF16),
            pltpu.VMEM((middle - 1, last, *shape), BF16),
            pltpu.VMEM((last - 1, *shape), BF16),
        ]

    links = low_count + HIGH
    return pl.pallas_call(
        functools.partial(pyramid_kernel, tiles, rows, cols, channels, width),
        out_shape=(
            jax.ShapeDtypeStruct((cells, width), BF16),
            jax.ShapeDtypeStruct((1, width), F32),
            jax.ShapeDtypeStruct((places, classes, pixels), BF16),
        ),
        in_specs=[away] * len(operands),
        out_specs=(whole, whole, whole),
        scratch_shapes=[
            *(pltpu.VMEM(operand.shape, operand.dtype) for operand in operands),
            pltpu.VMEM((2, edge, channels), BF16),
            pltpu.VMEM((cells + 2 * edge, CHUNK), F32),
            pltpu.VMEM((3, cells, CHUNK), BF16),
            pltpu.VMEM((4, cells, width), F32),
            pltpu.VMEM((3, 1, channels), F32),
            pltpu.VMEM((links - 1, 1, channels), F32),
            pltpu.VMEM((32, pixels), F32),
            pltpu.VMEM((128, cells), BF16),
            pltpu.VMEM((tiles * per, 128), BF16),
            pltpu.VMEM((tiles * item, 128), BF16),
            pltpu.VMEM((16, pixels), F32),
            pltpu.VMEM((per, width), BF16),
            pltpu.VMEM((1, width), F32),
            pltpu.VMEM((CAP, 144, width), BF16),
            pltpu.VMEM((pixels + 2 * BLK, 3 * width), BF16),
            pltpu.VMEM((pixels, 144), BF16),
            pltpu.VMEM((QUARTERS * CAP * 8, part), F32),
            *exchange_buffers((16, pixels), HIGH, low_count),
            *exchange_buffers((per, width), low_count, HIGH),
            *exchange_buffers((item, part), low_count, HIGH),
            dma((len(operands),)),
            dma((2, chunks)),
            dma((2, chunks)),
            *(dma((links,)) for _ in range(8)),
        ],
        compiler_params=pltpu.CompilerParams(collective_id=0, has_side_effects=True, vmem_limit_bytes=60 << 20),
        name="pyramid",
    )(*operands)


def shards(
    tiles,
    features,
    aerial_image,
    blocks,
    routes,
    w_one,
    w_depth,
    w_rates,
    w_pool,
    w_proj,
    w_first,
    w_color,
    w_second,
    w_head,
):
    rows, cols, channels = features.shape
    width = w_one.shape[1]
    aspp, context, refined = pyramid(
        tiles, rows, cols, features, aerial_image, blocks, routes, w_one, w_rates, w_depth, w_pool, w_proj,
        w_first[0], w_color[0], w_second[0], w_head[0],
    )
    return aspp.reshape(rows, cols, width), context.reshape(width), refined


def solution(mesh):
    return jax.shard_map(
        functools.partial(shards, mesh.shape["tile"]),
        mesh=mesh,
        in_specs=(
            P(("groups", "tile"), None, None),
            P(None, ("groups", "tile"), None),
            P("groups", None),
            P("groups", None),
            P(),
            P(),
            P(),
            P(),
            P(),
            P("tile", None, None, None),
            P("tile", None, None),
            P("tile", None, None, None),
            P("tile", None, None),
        ),
        out_specs=(
            P(("groups", "tile"), None, None),
            P("groups"),
            P(("groups", "tile"), None, None),
        ),
        check_vma=False,
    )
```

```python
import functools

import jax
import jax.numpy as jnp
import numpy as np
from jax import lax
from jax.experimental import pallas as pl
from jax.experimental.pallas import tpu as pltpu
from jax.sharding import PartitionSpec as P

BLK = 32
CAP = 4
CELLS = 4
RATES = (6, 12, 18)
REACH = 18
CHUNK = 256
HIGH = 4
QUARTERS = 4
AHEAD = 4
OWN = 6
F32 = jnp.float32
BF16 = jnp.bfloat16


def split_three(value):
    high = value.astype(BF16)
    rest = value - high.astype(F32)
    mid = rest.astype(BF16)
    low = (rest - mid.astype(F32)).astype(BF16)
    return high, mid, low


def exact_row_dot(row, weights):
    high, mid, low = split_three(row)
    stacked = jnp.concatenate(
        [high.astype(F32), mid.astype(F32), low.astype(F32), jnp.zeros((13, row.shape[1]), F32)], axis=0
    ).astype(BF16)
    product = jnp.dot(stacked, weights, preferred_element_type=F32)
    return product[0:1] + product[1:2] + product[2:3]


def pyramid_kernel(
    tiles, rows, cols, channels, width,
    feat_hbm, w_one_hbm, w_rates_hbm, w_depth_hbm, w_pool_hbm, w_proj_hbm, image_hbm, first_hbm, second_hbm,
    color_hbm, head_hbm, table_hbm, blocks_hbm, routes_hbm,
    aspp_ref, context_ref, refined_ref,
    feat, w_one, w_rates, w_depth_ref, w_pool, w_proj, image, first, second, color_ref, head_ref, table_ref, blocks_ref, routes_ref,
    halo, grown, depth, acc, sums, sums_in, own_colors, own_pick, crop_pick, back_pick, mine_ref, offset_ref,
    taps_ref, grid_b, patches, scores,
    colors_both, colors_out, colors_high, colors_low, crops_both, crops_out, crops_in, scores_both, back_out, back_in,
    local_sem, halo_send, halo_recv, sum_send, sum_recv, color_send, color_recv, crop_send, crop_recv, back_send, back_recv,
    mate_send, mate_recv,
):
    me = lax.axis_index("tile")
    chunks = channels // CHUNK
    edge = REACH * cols
    cells = rows * cols
    count = routes_ref.shape[1]
    classes = head_ref.shape[0]
    half, low_count = tiles // 2, tiles // (2 * HIGH)
    core = lax.rem(me, 2)
    low = lax.rem(me // 2, low_count)
    high = me // (2 * low_count)
    chip = me // 2

    local = [
        pltpu.make_async_copy(source, target, local_sem.at[n])
        for n, (source, target) in enumerate(
            ((feat_hbm, feat), (blocks_hbm, blocks_ref), (routes_hbm, routes_ref), (w_one_hbm, w_one), (image_hbm, image),
             (w_depth_hbm, w_depth_ref), (w_rates_hbm, w_rates), (w_pool_hbm, w_pool), (w_proj_hbm, w_proj),
             (color_hbm, color_ref), (head_hbm, head_ref), (table_hbm, table_ref), (first_hbm, first), (second_hbm, second))
        )
    ]
    for copy in local:
        copy.start()

    mate = me + 1 - 2 * core

    def low_peer(step):
        return (high * low_count + lax.rem(low + step, low_count)) * 2 + core

    def high_peer(step):
        return (lax.rem(high + step, HIGH) * low_count + low) * 2 + core

    has_next = me < tiles - 1
    has_prev = me > 0
    barrier = pltpu.get_barrier_semaphore()

    def greet(peer):
        pl.semaphore_signal(barrier, inc=1, device_id={"tile": peer}, device_id_type=pl.DeviceIdType.MESH)

    def chip_peer(step):
        return lax.rem(chip + step, half) * 2 + core

    def greet_chip(step, carry):
        greet(chip_peer(step))
        return carry

    outward = jnp.where(core == 1, me + 1, me - 1)
    has_outward = (outward >= 0) & (outward < tiles)

    @pl.when(has_outward)
    def _():
        greet(outward)

    greet(mate)
    lax.fori_loop(1, half, greet_chip, 0)
    pl.semaphore_wait(barrier, half + has_outward.astype(jnp.int32))

    def send(source, target, send_sem, recv_sem, peer):
        return pltpu.make_async_remote_copy(
            src_ref=source, dst_ref=target, send_sem=send_sem, recv_sem=recv_sem,
            device_id={"tile": peer}, device_id_type=pl.DeviceIdType.MESH,
        )

    def halo_copy(side, c):
        lanes = pl.ds(pl.multiple_of(c * CHUNK, CHUNK), CHUNK)
        return send(
            feat_hbm.at[pl.ds(cells - edge if side == 0 else 0, edge), lanes], halo.at[side, :, lanes],
            halo_send.at[side, c], halo_recv.at[side, c],
            lax.rem(me + 1, tiles) if side == 0 else lax.rem(me + tiles - 1, tiles),
        )

    def send_halo(c):
        @pl.when(has_next)
        def _():
            halo_copy(0, c).start()

        @pl.when(has_prev)
        def _():
            halo_copy(1, c).start()

    def steps(number, function):
        def body(step, carry):
            function(step)
            return carry

        lax.fori_loop(1, number, body, 0)

    def mate_copy(number, both):
        return send(both.at[core], both.at[core], mate_send.at[number], mate_recv.at[number], mate)

    def color_high(step):
        rows_of = pl.ds(pl.multiple_of(lax.rem(high + step, HIGH) * (low_count * 16), 16), low_count * 16)
        return send(colors_out.at[rows_of], colors_high.at[step - 1], color_send.at[step], color_recv.at[step], high_peer(step))

    def color_low(step):
        rows_of = pl.ds(pl.multiple_of((high * low_count + lax.rem(low + step, low_count)) * 16, 16), 16)
        slot = HIGH + step
        return send(colors_out.at[rows_of], colors_low.at[step - 1], color_send.at[slot], color_recv.at[slot], low_peer(step))

    def crop_rows(block, to_chip):
        return pl.ds(pl.multiple_of((block * half + to_chip) * 16, 16), 16)

    def crop_copy(block, step):
        return send(
            crops_out.at[crop_rows(block, lax.rem(chip + step, half))], crops_in.at[block, step - 1],
            crop_send.at[block, step], crop_recv.at[block, step], chip_peer(step),
        )

    item = back_pick.shape[0] // half

    def back_rows(to_chip):
        return pl.ds(pl.multiple_of(to_chip * item, 16), item)

    def back_copy(step):
        return send(
            back_out.at[back_rows(lax.rem(chip + step, half))], back_in.at[step - 1],
            back_send.at[step], back_recv.at[step], chip_peer(step),
        )

    def sum_low(step):
        return send(sums.at[0], sums_in.at[step - 1], sum_send.at[step], sum_recv.at[step], low_peer(step))

    def sum_high(step):
        slot = low_count + step
        return send(sums.at[1], sums_in.at[slot - 2], sum_send.at[slot], sum_recv.at[slot], high_peer(step))

    def sum_mate():
        return send(sums.at[2], sums_in.at[low_count + HIGH - 2], sum_send.at[0], sum_recv.at[0], mate)

    def add_sums(start, number, total):
        return lax.fori_loop(0, number, lambda n, value: value + sums_in[start + n], total)

    send_halo(0)
    local[0].wait()

    def sum_rows(n, totals):
        block = feat[pl.ds(pl.multiple_of(n * 16, 16), 16), :].astype(F32)
        return totals + block[0:8] + block[8:16]

    totals = lax.fori_loop(0, cells // 16, sum_rows, jnp.zeros((8, channels), F32))
    sums[0] = jnp.sum(totals, axis=0, keepdims=True)
    steps(low_count, lambda step: sum_low(step).start())
    send_halo(1)

    tall = 256
    local[3].wait()

    @pl.loop(0, cells // tall)
    def _(m):
        span = pl.ds(pl.multiple_of(m * tall, tall), tall)
        acc[0, span, :] = jnp.dot(feat[span, :], w_one[...], preferred_element_type=F32)

    @pl.when(jnp.logical_not(has_prev))
    def _():
        grown[0:edge, :] = jnp.zeros((edge, CHUNK), F32)

    @pl.when(jnp.logical_not(has_next))
    def _():
        grown[edge + cells :, :] = jnp.zeros((edge, CHUNK), F32)

    def widen(source, start, count, lanes):
        @pl.loop(0, count // 48)
        def _(n):
            grown[pl.ds(pl.multiple_of(start + n * 48, 8), 48), :] = source[
                pl.ds(pl.multiple_of(n * 48, 16), 48), lanes
            ].astype(F32)

    local[1].wait()
    local[2].wait()
    experts = routes_ref[...].astype(F32)
    square = (count, count)
    down, over = lax.broadcasted_iota(jnp.int32, square, 0), lax.broadcasted_iota(jnp.int32, square, 1)
    spread = jnp.broadcast_to(experts, square)

    def stand(row):
        return jnp.sum(jnp.where(down == over, jnp.broadcast_to(row, square), 0.0), axis=1, keepdims=True)

    upright = stand(experts)
    rank = jnp.sum(jnp.where((upright == spread) & (down < over), 1.0, 0.0), axis=0, keepdims=True)
    strip_blocks = rows // CELLS
    block_row, block_col = blocks_ref[0:1, :].astype(F32), blocks_ref[1:2, :].astype(F32)
    strip_row = (blocks_ref[0:1, :] // strip_blocks).astype(F32)
    strip_col = stand(strip_row)
    beside = jnp.broadcast_to(strip_row, square) == strip_col
    first_strip = lax.convert_element_type(chip * 2, F32)

    def listed_at(strip, place):
        within = strip - first_strip
        return jnp.where((within >= 0) & (within < 2), within * 8 + place, -1.0)

    own_row_index = listed_at(strip_row, jnp.sum(jnp.where(beside & (down < over), 1.0, 0.0), axis=0, keepdims=True))
    own_col_index = listed_at(strip_col, jnp.sum(jnp.where(beside & (over < down), 1.0, 0.0), axis=1, keepdims=True))
    slot_col = upright * CAP + jnp.sum(jnp.where((upright == spread) & (over < down), 1.0, 0.0), axis=1, keepdims=True)
    local_row = block_row - lax.convert_element_type(me * strip_blocks, F32)

    def own_values(index, values):
        shape = (index.shape[0], count)
        hit = jnp.broadcast_to(own_row_index, shape) == (index + core * 8).astype(F32)
        return jnp.max(jnp.where(hit, jnp.broadcast_to(values, shape), -1e6), axis=1, keepdims=True)

    own_row = lax.broadcasted_iota(jnp.int32, (128, 1), 0)
    own_base = own_values(own_row >> 4, local_row * (CELLS * cols) + block_col * CELLS)
    wanted_cell = own_base + (((own_row >> 2) & 3) * cols + (own_row & 3)).astype(F32)
    cell_at = lax.broadcasted_iota(jnp.int32, (128, cells), 1).astype(F32)
    own_pick[...] = (cell_at == wanted_cell).astype(F32).astype(BF16)

    own_lane = lax.broadcasted_iota(jnp.int32, (1, 256), 1)

    def own_slots(index):
        hit = own_col_index == index.astype(F32)
        return jnp.max(jnp.where(hit, jnp.broadcast_to(slot_col, (count, 256)), -1.0), axis=0, keepdims=True)

    own_slot = own_slots(own_lane >> 4)
    @pl.loop(0, CAP * half // 8)
    def _(n):
        row = lax.broadcasted_iota(jnp.int32, (128, 1), 0) + n * 128
        index = row >> 4
        tile = (index % half) * 2 + core
        hit = (own_slot == (tile * CAP + index // half).astype(F32)) & ((own_lane & 15) == (row & 15))
        crop_pick[pl.ds(pl.multiple_of(n * 128, 128), 128), :] = hit.astype(F32).astype(BF16)

    def to_expert(expert):
        return jnp.where(experts == lax.convert_element_type(expert, F32), rank, -1.0)

    to_first, to_second = to_expert(2 * chip), to_expert(2 * chip + 1)

    @pl.loop(0, half)
    def _(n):
        tile = n * 2 + core
        span = item // QUARTERS
        line = lax.broadcasted_iota(jnp.int32, (item, 1), 0)
        quarter = sum((line >= q * span).astype(jnp.int32) for q in range(1, QUARTERS))
        line = line - quarter * span
        place = sum((line >= p * classes).astype(jnp.int32) for p in range(1, span // classes)) + jnp.zeros_like(line)
        kind = line - place * classes
        listed = lax.broadcasted_iota(jnp.int32, (item, count), 1)
        wanted = listed == tile * (span // classes) + place
        given = lax.broadcasted_iota(jnp.int32, (item, 128), 1)
        right_place = ((given & 7) == kind) & ((given >> 5) == quarter)
        for s, values in enumerate((to_first, to_second)):
            slot = jnp.max(jnp.where(wanted, jnp.broadcast_to(values, (item, count)), -1.0), axis=1, keepdims=True)
            pick = (((given >> 3) & 3).astype(F32) == slot) & right_place
            back_pick[back_rows(n), s * 128 : s * 128 + 128] = pick.astype(F32).astype(BF16)

    steps(low_count, lambda step: sum_low(step).wait_recv())
    sums[1] = add_sums(0, low_count - 1, sums[0])
    steps(HIGH, lambda step: sum_high(step).start())
    for c in range(2, AHEAD):
        send_halo(c)

    local[4].wait()
    parts_high = image.shape[0]
    across = parts_high // 3
    group = 2 * 3 * BLK
    line = lax.broadcasted_iota(jnp.int32, (group, 1), 0)
    line_own = (line >= 3 * BLK).astype(jnp.int32)
    line_channel = (line - line_own * (3 * BLK)) // BLK
    lane = lax.broadcasted_iota(jnp.int32, (1, BLK * BLK), 1)
    source = lax.broadcasted_iota(jnp.int32, (1, parts_high), 1).astype(F32)
    keep = (line & (BLK - 1)) == (lane & (BLK - 1))
    tall_rows = image.shape[1]
    image_row = lax.broadcasted_iota(jnp.int32, (tall_rows, 1), 0)
    image_lane = (lax.broadcasted_iota(jnp.int32, (1, tall_rows), 1) // BLK).astype(F32)
    fold = ((image_row & (BLK - 1)) == (lane >> 5)).astype(F32).astype(BF16)
    own_colors[...] = jnp.zeros(own_colors.shape, F32)

    for n in range(OWN // 2):
        index = line_own + 2 * n
        at = own_values(index, local_row)
        wanted = own_values(index, block_col) * BLK + (line_channel * across + (line & (BLK - 1))).astype(F32)
        chosen = (source == wanted).astype(F32).astype(BF16)
        columns = jnp.dot(chosen, image[...], preferred_element_type=F32)
        columns = jnp.where(image_lane == at, columns, 0.0).astype(BF16)
        strips = jnp.where(keep, jnp.dot(columns, fold, preferred_element_type=F32), 0.0)
        for p in range(6):
            to = (2 * n + p // 3) * 4 + p % 3
            own_colors[to : to + 1, :] = jnp.sum(strips[p * BLK : (p + 1) * BLK], axis=0, keepdims=True)

    colors_both[core] = own_colors[...].astype(BF16)
    mate_copy(0, colors_both).start()

    local[5].wait()
    local[6].wait()

    def one_chunk(c, carry):
        @pl.when(c < chunks - AHEAD)
        def _():
            send_halo(c + AHEAD)

        @pl.when(c == 1)
        def _():
            mate_copy(0, colors_both).wait_recv()
            lane_of = own_lane[:, 0:32]
            for s in range(2):
                lane_slot = own_slots((own_lane & 31) // 4 + 8 * s)[:, 0:32]

                @pl.loop(0, half)
                def _(n, s=s, lane_slot=lane_slot):
                    row = lax.broadcasted_iota(jnp.int32, (16, 1), 0)
                    hit = (lane_slot == ((n * 2 + core) * CAP + (row >> 2)).astype(F32)) & ((lane_of & 3) == (row & 3))
                    found = jnp.dot(hit.astype(F32).astype(BF16), colors_both[s], preferred_element_type=F32)
                    rows_of = pl.ds(pl.multiple_of(n * 16, 16), 16)
                    if s == 0:
                        colors_out[rows_of, :] = found.astype(BF16)
                    else:
                        colors_out[rows_of, :] = (colors_out[rows_of, :].astype(F32) + found).astype(BF16)

            steps(HIGH, lambda step: color_high(step).start())

        @pl.when(c == 3)
        def _():
            steps(HIGH, lambda step: sum_high(step).wait_recv())
            sums[2] = add_sums(low_count - 1, HIGH - 1, sums[1])
            sum_mate().start()

        @pl.when(c == chunks - 3)
        def _():
            sum_mate().wait_recv()
            local[7].wait()
            local[8].wait()
            pooled = add_sums(low_count + HIGH - 2, 1, sums[2]) / (cells * tiles)
            context = jnp.maximum(exact_row_dot(pooled, w_pool[...]), 0.0)
            context_ref[...] = context
            offset_ref[...] = exact_row_dot(context, w_proj[4 * width :, :])

        @pl.when(c == chunks - 2)
        def _():
            steps(HIGH, lambda step: color_high(step).wait_recv())
            rows_of = pl.ds(pl.multiple_of(high * (low_count * 16), 16), low_count * 16)

            def add(n, total):
                return total + colors_high[n].astype(F32)

            colors_out[rows_of, :] = lax.fori_loop(0, HIGH - 1, add, colors_out[rows_of, :].astype(F32)).astype(BF16)
            steps(low_count, lambda step: color_low(step).start())

        for at, (start, stop) in ((chunks // 2, (0, chunks // 2)), (chunks - 1, (chunks // 2, chunks - 1))):
            @pl.when(c == at)
            def _(start=start * CHUNK, stop=stop * CHUNK):
                for k in range(3):
                    @pl.loop(0, cells // tall)
                    def _(m, k=k):
                        span = pl.ds(pl.multiple_of(m * tall, tall), tall)
                        part = jnp.dot(depth[k, span, start:stop], w_rates[k, start:stop, :], preferred_element_type=F32)
                        acc[k + 1, span, :] = part if start == 0 else acc[k + 1, span, :] + part

        lanes = pl.ds(pl.multiple_of(c * CHUNK, CHUNK), CHUNK)
        widen(feat, edge, cells, lanes)

        @pl.when(has_prev)
        def _():
            halo_copy(0, c).wait_recv()
            widen(halo.at[0], 0, edge, lanes)

        @pl.when(has_next)
        def _():
            halo_copy(1, c).wait_recv()
            widen(halo.at[1], edge + cells, edge, lanes)

        for part in range(CHUNK // 128):
            inner = slice(part * 128, part * 128 + 128)
            outer = pl.ds(pl.multiple_of(c * CHUNK + part * 128, 128), 128)
            for k, d in enumerate(RATES):
                taps = [
                    jnp.broadcast_to(w_depth_ref[t, k : k + 1, outer].astype(F32), (8, 128)) for t in range(9)
                ]

                def weigh(parts, column, taps=taps):
                    total = None
                    for i in range(3):
                        tap = jnp.concatenate([taps[3 * i + column]] * (parts[i].shape[0] // 8), axis=0)
                        term = parts[i] * tap
                        total = term if total is None else total + term
                    return total

                @pl.loop(0, rows // 2, unroll=4)
                def _(pair, d=d, weigh=weigh, inner=inner, outer=outer, k=k):
                    results = []
                    for r in range(2):
                        parts = []
                        for i in (-1, 0, 1):
                            start = pl.multiple_of((REACH + i * d + r) * cols + pair * (2 * cols), 8)
                            parts.append(grown[pl.ds(start, cols), inner])
                        low = -(-(cols - d) // 8) * 8
                        high = (d // 8) * 8
                        middle = weigh(parts, 1)
                        left = weigh([p[:low] for p in parts], 0)
                        right = weigh([p[high:] for p in parts], 2)
                        fill = jnp.zeros((d, 128), F32)
                        left = jnp.concatenate([fill, left[: cols - d]], axis=0)
                        right = jnp.concatenate([right[d - high :], fill], axis=0)
                        results.append(jnp.maximum(middle + left + right, 0.0))
                    depth[k, pl.ds(pl.multiple_of(pair * (2 * cols), 16), 2 * cols), outer] = jnp.concatenate(
                        results, axis=0
                    ).astype(BF16)

        return carry

    lax.fori_loop(0, chunks, one_chunk, 0)

    @pl.loop(0, cells // tall)
    def _(m):
        span = pl.ds(pl.multiple_of(m * tall, tall), tall)
        blended = jnp.broadcast_to(offset_ref[...], (tall, width))
        for k in range(4):
            branch = acc[k, span, :]
            if k:
                branch += jnp.dot(
                    depth[k - 1, span, channels - CHUNK :], w_rates[k - 1, channels - CHUNK :, :], preferred_element_type=F32
                )
            branch = jnp.maximum(branch, 0.0).astype(BF16)
            blended += jnp.dot(branch, w_proj[k * width : (k + 1) * width, :], preferred_element_type=F32)
        aspp_ref[span, :] = jnp.maximum(blended, 0.0).astype(BF16)

    crops_both[core] = jnp.dot(own_pick[...], aspp_ref[...], preferred_element_type=F32).astype(BF16)
    mate_copy(1, crops_both).start()
    mate_copy(1, crops_both).wait_recv()

    @pl.loop(0, CAP * half // 8)
    def _(n):
        rows_of = pl.ds(pl.multiple_of(n * 128, 128), 128)
        found = jnp.dot(crop_pick[rows_of, 0:128], crops_both[0], preferred_element_type=F32)
        found += jnp.dot(crop_pick[rows_of, 128:256], crops_both[1], preferred_element_type=F32)
        crops_out[rows_of, :] = found.astype(BF16)

    def crop_sends(block, carry):
        steps(half, lambda step: crop_copy(block, step).start())
        return carry

    lax.fori_loop(0, CAP, crop_sends, 0)
    steps(low_count, lambda step: color_low(step).wait_recv())

    def add_low(n, total):
        return total + colors_low[n].astype(F32)

    mine_ref[...] = lax.fori_loop(
        0, low_count - 1, add_low, colors_out[pl.ds(pl.multiple_of(chip * 16, 16), 16), :].astype(F32)
    )
    side, pixels = BLK, BLK * BLK
    wide = lax.broadcasted_iota(jnp.int32, (16, pixels), 1)
    row_at, col_at = wide >> 5, wide & (side - 1)
    colors = mine_ref[...]
    pieces = []
    for i in (-1, 0, 1):
        for j in (-1, 0, 1):
            moved = colors if i == 0 and j == 0 else pltpu.roll(colors, (-(side * i + j)) % pixels, 1)
            inside = (row_at + i >= 0) & (row_at + i < side) & (col_at + j >= 0) & (col_at + j < side)
            pieces.append(jnp.where(inside, moved, 0.0))
    patches[...] = jnp.concatenate(pieces, axis=0).T.astype(BF16)

    blank = jnp.zeros((side, 3 * width), BF16)
    grid_b[0:side, :] = blank
    grid_b[side + pixels :, :] = blank
    tall = 512
    for n in range(9, 14):
        local[n].wait()
    scores[...] = jnp.zeros(scores.shape, F32)
    col = lax.broadcasted_iota(jnp.int32, (tall, width), 0) & (side - 1)

    @pl.loop(0, CAP)
    def _(block):
        steps(half, lambda step: crop_copy(block, step).wait_recv())

        def add_crop(n, total):
            return total + crops_in[block, n].astype(F32)

        crop = lax.fori_loop(0, half - 1, add_crop, crops_out[crop_rows(block, chip), :].astype(F32)).astype(BF16)
        for tap in range(9):
            part = jnp.dot(crop, first[tap * width : (tap + 1) * width, :], preferred_element_type=F32)
            taps_ref[tap * 16 : tap * 16 + 16, :] = part.astype(BF16)

        tap_row = lax.broadcasted_iota(jnp.int32, (144, 27), 0)
        channel = (tap_row & 15) - block * 4
        wanted_tap = (tap_row >> 4) * 3 + channel
        spread_taps = (channel >= 0) & (channel < 3) & (wanted_tap == lax.broadcasted_iota(jnp.int32, (144, 27), 1))
        tap_weights = jnp.dot(
            spread_taps.astype(F32).astype(BF16), color_ref[...], preferred_element_type=F32
        ).astype(BF16)

        @pl.loop(0, pixels // tall)
        def _(m):
            at = pl.multiple_of(m * tall, tall)
            total = jnp.dot(patches[pl.ds(at, tall), :], tap_weights, preferred_element_type=F32)
            total += jnp.dot(table_ref[pl.ds(at, tall), :], taps_ref[...], preferred_element_type=F32)
            total = jnp.maximum(total, 0.0)
            before = jnp.where(col == 0, 0.0, pltpu.roll(total, 1, 0))
            after = jnp.where(col == side - 1, 0.0, pltpu.roll(total, tall - 1, 0))
            inner = pl.ds(pl.multiple_of(side + at, side), tall)
            grid_b[inner, 0:width] = before.astype(BF16)
            grid_b[inner, width : 2 * width] = total.astype(BF16)
            grid_b[inner, 2 * width :] = after.astype(BF16)

        @pl.loop(0, pixels // tall)
        def _(m):
            at = pl.multiple_of(m * tall, tall)
            total = jnp.zeros((tall, width), F32)
            for i in range(3):
                total += jnp.dot(
                    grid_b[pl.ds(pl.multiple_of(at + side * i, side), tall), :],
                    second[3 * width * i : 3 * width * (i + 1), :],
                    preferred_element_type=F32,
                )
            total = jnp.maximum(total, 0.0).astype(BF16)
            found = lax.dot_general(
                head_ref[...], total, (((1,), (1,)), ((), ())), preferred_element_type=F32
            )
            wide_part = pixels // QUARTERS
            for q in range(tall // wide_part):
                quarter = m * (tall // wide_part) + q
                scores[pl.ds(pl.multiple_of(quarter * (8 * CAP) + block * 8, 8), classes), :] = found[
                    :, q * wide_part : (q + 1) * wide_part
                ]

    scores_both[core] = scores[...].astype(BF16)
    mate_copy(2, scores_both).start()
    mate_copy(2, scores_both).wait_recv()

    @pl.loop(0, half // 2)
    def _(n):
        rows_of = pl.ds(pl.multiple_of(n * (2 * item), 16), 2 * item)
        found = jnp.dot(back_pick[rows_of, 0:128], scores_both[0], preferred_element_type=F32)
        found += jnp.dot(back_pick[rows_of, 128:256], scores_both[1], preferred_element_type=F32)
        back_out[rows_of, :] = found.astype(BF16)

    steps(half, lambda step: back_copy(step).start())
    steps(half, lambda step: back_copy(step).wait_recv())

    def add_back(n, total):
        return total + back_in[n].astype(F32)

    result = lax.fori_loop(0, half - 1, add_back, back_out[back_rows(chip), :].astype(F32))
    span = item // QUARTERS
    wide_part = pixels // QUARTERS
    for q in range(QUARTERS):
        for p in range(span // classes):
            start = q * span + p * classes
            refined_ref[p, :, q * wide_part : (q + 1) * wide_part] = result[start : start + classes].astype(BF16)

    steps(low_count, lambda step: sum_low(step).wait_send())
    steps(HIGH, lambda step: sum_high(step).wait_send())
    sum_mate().wait_send()
    steps(HIGH, lambda step: color_high(step).wait_send())
    steps(low_count, lambda step: color_low(step).wait_send())
    steps(half, lambda step: back_copy(step).wait_send())
    for number, both in enumerate((colors_both, crops_both, scores_both)):
        mate_copy(number, both).wait_send()

    def drain_crops(block, carry):
        steps(half, lambda step: crop_copy(block, step).wait_send())
        return carry

    lax.fori_loop(0, CAP, drain_crops, 0)

    def drain_halo(c, carry):
        @pl.when(has_next)
        def _():
            halo_copy(0, c).wait_send()

        @pl.when(has_prev)
        def _():
            halo_copy(1, c).wait_send()

        return carry

    lax.fori_loop(0, chunks, drain_halo, 0)


def upsample_taps():
    pixels = np.arange(BLK, dtype=np.float32)
    source = np.clip((pixels + 0.5) / 8.0 - 0.5, 0.0, CELLS - 1.0)
    table = np.maximum(1.0 - np.abs(source[:, None] - np.arange(CELLS, dtype=np.float32)[None, :]), 0.0)
    moved = []
    for i in (-1, 0, 1):
        shifted = np.zeros_like(table)
        for p in range(BLK):
            if 0 <= p + i < BLK:
                shifted[p] = table[p + i]
        moved.append(shifted)
    moved = np.stack(moved)
    return np.einsum("ipa,jqb->pqijab", moved, moved).reshape(BLK * BLK, 9 * CELLS * CELLS)


def pyramid(tiles, rows, cols, features, image, blocks, routes, w_one, w_rates, w_depth, w_pool, w_proj,
            w_first, w_color, w_second, w_head):
    channels, width = w_one.shape
    cells = rows * cols
    per = CAP * CELLS * CELLS
    chunks = channels // CHUNK
    edge = REACH * cols
    places = routes.shape[0] // tiles
    classes = w_head.shape[0]
    pixels = BLK * BLK
    item = places * classes * QUARTERS
    low_count = tiles // (2 * HIGH)
    part = pixels // QUARTERS
    whole = pl.BlockSpec(memory_space=pltpu.VMEM)
    away = pl.BlockSpec(memory_space=pl.ANY)
    dma = pltpu.SemaphoreType.DMA
    image = image.transpose(0, 2, 1).reshape(-1, image.shape[1])
    first, second = w_first.reshape(9 * width, width), w_second.reshape(9 * width, width)
    operands = (
        features.reshape(cells, channels), w_one, w_rates, w_depth.transpose(1, 0, 2), w_pool, w_proj, image, first, second,
        w_color, w_head, jnp.asarray(upsample_taps(), BF16), blocks.T, routes.T,
    )

    links = low_count + HIGH
    half = tiles // 2
    return pl.pallas_call(
        functools.partial(pyramid_kernel, tiles, rows, cols, channels, width),
        out_shape=(
            jax.ShapeDtypeStruct((cells, width), BF16),
            jax.ShapeDtypeStruct((1, width), F32),
            jax.ShapeDtypeStruct((places, classes, pixels), BF16),
        ),
        in_specs=[away] * len(operands),
        out_specs=(whole, whole, whole),
        scratch_shapes=[
            *(pltpu.VMEM(operand.shape, operand.dtype) for operand in operands),
            pltpu.VMEM((2, edge, channels), BF16),
            pltpu.VMEM((cells + 2 * edge, CHUNK), F32),
            pltpu.VMEM((3, cells, channels), BF16),
            pltpu.VMEM((4, cells, width), F32),
            pltpu.VMEM((3, 1, channels), F32),
            pltpu.VMEM((links - 1, 1, channels), F32),
            pltpu.VMEM((32, pixels), F32),
            pltpu.VMEM((128, cells), BF16),
            pltpu.VMEM((half * per, 256), BF16),
            pltpu.VMEM((half * item, 256), BF16),
            pltpu.VMEM((16, pixels), F32),
            pltpu.VMEM((1, width), F32),
            pltpu.VMEM((144, width), BF16),
            pltpu.VMEM((pixels + 2 * BLK, 3 * width), BF16),
            pltpu.VMEM((pixels, 144), BF16),
            pltpu.VMEM((QUARTERS * CAP * 8, part), F32),
            pltpu.VMEM((2, 32, pixels), BF16),
            pltpu.VMEM((half * 16, pixels), BF16),
            pltpu.VMEM((HIGH - 1, low_count * 16, pixels), BF16),
            pltpu.VMEM((low_count - 1, 16, pixels), BF16),
            pltpu.VMEM((2, 128, width), BF16),
            pltpu.VMEM((half * per, width), BF16),
            pltpu.VMEM((CAP, half - 1, 16, width), BF16),
            pltpu.VMEM((2, QUARTERS * CAP * 8, part), BF16),
            pltpu.VMEM((half * item, part), BF16),
            pltpu.VMEM((half - 1, item, part), BF16),
            dma((len(operands),)),
            dma((2, chunks)),
            dma((2, chunks)),
            *(dma((links,)) for _ in range(4)),
            *(dma((CAP, half)) for _ in range(2)),
            *(dma((half,)) for _ in range(2)),
            *(dma((3,)) for _ in range(2)),
        ],
        compiler_params=pltpu.CompilerParams(collective_id=0, has_side_effects=True, vmem_limit_bytes=60 << 20),
        name="pyramid",
    )(*operands)


def shards(
    tiles,
    features,
    aerial_image,
    blocks,
    routes,
    w_one,
    w_depth,
    w_rates,
    w_pool,
    w_proj,
    w_first,
    w_color,
    w_second,
    w_head,
):
    rows, cols, channels = features.shape
    width = w_one.shape[1]
    aspp, context, refined = pyramid(
        tiles, rows, cols, features, aerial_image, blocks, routes, w_one, w_rates, w_depth, w_pool, w_proj,
        w_first[0], w_color[0], w_second[0], w_head[0],
    )
    return aspp.reshape(rows, cols, width), context.reshape(width), refined


def solution(mesh):
    return jax.shard_map(
        functools.partial(shards, mesh.shape["tile"]),
        mesh=mesh,
        in_specs=(
            P(("groups", "tile"), None, None),
            P(None, ("groups", "tile"), None),
            P("groups", None),
            P("groups", None),
            P(),
            P(),
            P(),
            P(),
            P(),
            P("tile", None, None, None),
            P("tile", None, None),
            P("tile", None, None, None),
            P("tile", None, None),
        ),
        out_specs=(
            P(("groups", "tile"), None, None),
            P("groups"),
            P(("groups", "tile"), None, None),
        ),
        check_vma=False,
    )
```

```python
import functools

import jax
import jax.numpy as jnp
import numpy as np
from jax import lax
from jax.experimental import pallas as pl
from jax.experimental.pallas import tpu as pltpu
from jax.sharding import PartitionSpec as P

BLK = 32
CAP = 4
CELLS = 4
RATES = (6, 12, 18)
REACH = 18
CHUNK = 256
HIGH = 4
QUARTERS = 4
AHEAD = 4
OWN = 6
F32 = jnp.float32
BF16 = jnp.bfloat16


def split_three(value):
    high = value.astype(BF16)
    rest = value - high.astype(F32)
    mid = rest.astype(BF16)
    low = (rest - mid.astype(F32)).astype(BF16)
    return high, mid, low


def exact_row_dot(row, weights):
    high, mid, low = split_three(row)
    stacked = jnp.concatenate(
        [high.astype(F32), mid.astype(F32), low.astype(F32), jnp.zeros((13, row.shape[1]), F32)], axis=0
    ).astype(BF16)
    product = jnp.dot(stacked, weights, preferred_element_type=F32)
    return product[0:1] + product[1:2] + product[2:3]


def pyramid_kernel(
    tiles, rows, cols, channels, width,
    feat_hbm, w_one_hbm, w_rates_hbm, w_depth_hbm, w_pool_hbm, w_proj_hbm, image_hbm, first_hbm, second_hbm,
    color_hbm, head_hbm, table_hbm, blocks_hbm, routes_hbm,
    aspp_ref, context_ref, refined_ref,
    feat, w_one, w_rates, w_depth_ref, w_pool, w_proj, image, first, second, color_ref, head_ref, table_ref, blocks_ref, routes_ref,
    halo, grown, depth, acc, sums, sums_in, own_colors, own_pick, crop_pick, back_pick, mine_ref, offset_ref,
    taps_ref, grid_b, patches, scores,
    colors_both, colors_out, colors_high, colors_low, crops_both, crops_out, crops_in, scores_both, back_out, back_in,
    local_sem, halo_send, halo_recv, sum_send, sum_recv, color_send, color_recv, crop_send, crop_recv, back_send, back_recv,
    mate_send, mate_recv, relay, relay_send, relay_recv,
):
    me = lax.axis_index("tile")
    chunks = channels // CHUNK
    edge = REACH * cols
    cells = rows * cols
    count = routes_ref.shape[1]
    classes = head_ref.shape[0]
    half, low_count = tiles // 2, tiles // (2 * HIGH)
    core = lax.rem(me, 2)
    low = lax.rem(me // 2, low_count)
    high = me // (2 * low_count)
    chip = me // 2

    local = [
        pltpu.make_async_copy(source, target, local_sem.at[n])
        for n, (source, target) in enumerate(
            ((feat_hbm, feat), (blocks_hbm, blocks_ref), (routes_hbm, routes_ref), (w_one_hbm, w_one), (image_hbm, image),
             (w_depth_hbm, w_depth_ref), (w_rates_hbm, w_rates), (w_pool_hbm, w_pool), (w_proj_hbm, w_proj),
             (color_hbm, color_ref), (head_hbm, head_ref), (table_hbm, table_ref), (first_hbm, first), (second_hbm, second))
        )
    ]
    for copy in local:
        copy.start()

    mate = me + 1 - 2 * core

    def low_peer(step):
        return (high * low_count + lax.rem(low + step, low_count)) * 2 + core

    def high_peer(step):
        return (lax.rem(high + step, HIGH) * low_count + low) * 2 + core

    has_next = me < tiles - 1
    has_prev = me > 0
    barrier = pltpu.get_barrier_semaphore()

    def greet(peer):
        pl.semaphore_signal(barrier, inc=1, device_id={"tile": peer}, device_id_type=pl.DeviceIdType.MESH)

    def chip_peer(step):
        return lax.rem(chip + step, half) * 2 + core

    def greet_chip(step, carry):
        greet(chip_peer(step))
        return carry

    outward = jnp.where(core == 1, me + 1, me - 1)
    has_outward = (outward >= 0) & (outward < tiles)

    slanted = jnp.where(core == 1, me + 3, me - 3)
    has_slanted = (slanted >= 0) & (slanted < tiles) if low_count == 2 else False
    relayed = jnp.where(core == 1, 2 * (HIGH - 1 - high), 2 * high) if low_count == 2 else 0
    gives = low == core
    first_relayed = chunks - relayed

    @pl.when(has_outward)
    def _():
        greet(outward)

    if low_count == 2:
        @pl.when(has_slanted)
        def _():
            greet(slanted)

    greet(mate)
    lax.fori_loop(1, half, greet_chip, 0)
    expected = half + has_outward.astype(jnp.int32)
    pl.semaphore_wait(barrier, expected + has_slanted.astype(jnp.int32) if low_count == 2 else expected)

    def send(source, target, send_sem, recv_sem, peer):
        return pltpu.make_async_remote_copy(
            src_ref=source, dst_ref=target, send_sem=send_sem, recv_sem=recv_sem,
            device_id={"tile": peer}, device_id_type=pl.DeviceIdType.MESH,
        )

    def halo_copy(side, c):
        lanes = pl.ds(pl.multiple_of(c * CHUNK, CHUNK), CHUNK)
        return send(
            feat_hbm.at[pl.ds(cells - edge if side == 0 else 0, edge), lanes], halo.at[side, :, lanes],
            halo_send.at[side, c], halo_recv.at[side, c],
            lax.rem(me + 1, tiles) if side == 0 else lax.rem(me + tiles - 1, tiles),
        )

    def relay_copy(side, c):
        lanes = pl.ds(pl.multiple_of(c * CHUNK, CHUNK), CHUNK)
        return send(
            feat_hbm.at[pl.ds(cells - edge if side == 0 else 0, edge), lanes], relay.at[c - first_relayed],
            halo_send.at[side, c], relay_recv.at[c - first_relayed], low_peer(1),
        )

    def pass_copy(side, c):
        lanes = pl.ds(pl.multiple_of(c * CHUNK, CHUNK), CHUNK)
        slot = c - first_relayed
        return send(relay.at[slot], halo.at[side, :, lanes], relay_send.at[slot], halo_recv.at[side, c], slanted)

    def send_halo(c):
        for side, present in ((0, has_next), (1, has_prev)):
            if low_count == 2:
                given = present & (core == 1 - side) & gives & (c >= first_relayed)

                @pl.when(given)
                def _(side=side):
                    relay_copy(side, c).start()

                present = present & jnp.logical_not(given)

            @pl.when(present)
            def _(side=side):
                halo_copy(side, c).start()

    def pass_halo(c):
        if low_count == 2:
            for side in range(2):
                @pl.when((core == 1 - side) & jnp.logical_not(gives) & (c >= first_relayed) & (c < chunks))
                def _(side=side):
                    relay_copy(side, c).wait_recv()
                    pass_copy(side, c).start()

    def steps(number, function):
        def body(step, carry):
            function(step)
            return carry

        lax.fori_loop(1, number, body, 0)

    def mate_copy(number, both):
        return send(both.at[core], both.at[core], mate_send.at[number], mate_recv.at[number], mate)

    def color_high(step):
        rows_of = pl.ds(pl.multiple_of(lax.rem(high + step, HIGH) * (low_count * 16), 16), low_count * 16)
        return send(colors_out.at[rows_of], colors_high.at[step - 1], color_send.at[step], color_recv.at[step], high_peer(step))

    def color_low(step):
        rows_of = pl.ds(pl.multiple_of((high * low_count + lax.rem(low + step, low_count)) * 16, 16), 16)
        slot = HIGH + step
        return send(colors_out.at[rows_of], colors_low.at[step - 1], color_send.at[slot], color_recv.at[slot], low_peer(step))

    def crop_rows(block, to_chip):
        return pl.ds(pl.multiple_of((block * half + to_chip) * 16, 16), 16)

    def crop_copy(block, step):
        return send(
            crops_out.at[crop_rows(block, lax.rem(chip + step, half))], crops_in.at[block, step - 1],
            crop_send.at[block, step], crop_recv.at[block, step], chip_peer(step),
        )

    item = back_pick.shape[0] // half

    def back_rows(to_chip):
        return pl.ds(pl.multiple_of(to_chip * item, 16), item)

    def back_copy(step):
        return send(
            back_out.at[back_rows(lax.rem(chip + step, half))], back_in.at[step - 1],
            back_send.at[step], back_recv.at[step], chip_peer(step),
        )

    def sum_low(step):
        return send(sums.at[0], sums_in.at[step - 1], sum_send.at[step], sum_recv.at[step], low_peer(step))

    def sum_high(step):
        slot = low_count + step
        return send(sums.at[1], sums_in.at[slot - 2], sum_send.at[slot], sum_recv.at[slot], high_peer(step))

    def sum_mate():
        return send(sums.at[2], sums_in.at[low_count + HIGH - 2], sum_send.at[0], sum_recv.at[0], mate)

    def add_sums(start, number, total):
        return lax.fori_loop(0, number, lambda n, value: value + sums_in[start + n], total)

    send_halo(0)
    local[0].wait()

    def sum_rows(n, totals):
        block = feat[pl.ds(pl.multiple_of(n * 16, 16), 16), :].astype(F32)
        return totals + block[0:8] + block[8:16]

    totals = lax.fori_loop(0, cells // 16, sum_rows, jnp.zeros((8, channels), F32))
    sums[0] = jnp.sum(totals, axis=0, keepdims=True)
    steps(low_count, lambda step: sum_low(step).start())
    for c in range(1, AHEAD):
        send_halo(c)

    tall = 768
    local[3].wait()

    @pl.loop(0, cells // tall)
    def _(m):
        span = pl.ds(pl.multiple_of(m * tall, tall), tall)
        acc[0, span, :] = jnp.dot(feat[span, :], w_one[...], preferred_element_type=F32)

    @pl.when(jnp.logical_not(has_prev))
    def _():
        grown[0:edge, :] = jnp.zeros((edge, CHUNK), F32)

    @pl.when(jnp.logical_not(has_next))
    def _():
        grown[edge + cells :, :] = jnp.zeros((edge, CHUNK), F32)

    def widen(source, start, count, lanes):
        @pl.loop(0, count // 48)
        def _(n):
            grown[pl.ds(pl.multiple_of(start + n * 48, 8), 48), :] = source[
                pl.ds(pl.multiple_of(n * 48, 16), 48), lanes
            ].astype(F32)

    local[1].wait()
    local[2].wait()
    experts = routes_ref[...].astype(F32)
    square = (count, count)
    down, over = lax.broadcasted_iota(jnp.int32, square, 0), lax.broadcasted_iota(jnp.int32, square, 1)
    spread = jnp.broadcast_to(experts, square)

    def stand(row):
        return jnp.sum(jnp.where(down == over, jnp.broadcast_to(row, square), 0.0), axis=1, keepdims=True)

    upright = stand(experts)
    rank = jnp.sum(jnp.where((upright == spread) & (down < over), 1.0, 0.0), axis=0, keepdims=True)
    strip_blocks = rows // CELLS
    block_row, block_col = blocks_ref[0:1, :].astype(F32), blocks_ref[1:2, :].astype(F32)
    strip_row = (blocks_ref[0:1, :] // strip_blocks).astype(F32)
    strip_col = stand(strip_row)
    beside = jnp.broadcast_to(strip_row, square) == strip_col
    first_strip = lax.convert_element_type(chip * 2, F32)

    def listed_at(strip, place):
        within = strip - first_strip
        return jnp.where((within >= 0) & (within < 2), within * 8 + place, -1.0)

    own_row_index = listed_at(strip_row, jnp.sum(jnp.where(beside & (down < over), 1.0, 0.0), axis=0, keepdims=True))
    own_col_index = listed_at(strip_col, jnp.sum(jnp.where(beside & (over < down), 1.0, 0.0), axis=1, keepdims=True))
    slot_col = upright * CAP + jnp.sum(jnp.where((upright == spread) & (over < down), 1.0, 0.0), axis=1, keepdims=True)
    local_row = block_row - lax.convert_element_type(me * strip_blocks, F32)

    def own_values(index, values):
        shape = (index.shape[0], count)
        hit = jnp.broadcast_to(own_row_index, shape) == (index + core * 8).astype(F32)
        return jnp.max(jnp.where(hit, jnp.broadcast_to(values, shape), -1e6), axis=1, keepdims=True)

    own_row = lax.broadcasted_iota(jnp.int32, (128, 1), 0)
    own_base = own_values(own_row >> 4, local_row * (CELLS * cols) + block_col * CELLS)
    wanted_cell = own_base + (((own_row >> 2) & 3) * cols + (own_row & 3)).astype(F32)
    cell_at = lax.broadcasted_iota(jnp.int32, (128, cells), 1).astype(F32)
    own_pick[...] = (cell_at == wanted_cell).astype(F32).astype(BF16)

    own_lane = lax.broadcasted_iota(jnp.int32, (1, 256), 1)

    def own_slots(index):
        hit = own_col_index == index.astype(F32)
        return jnp.max(jnp.where(hit, jnp.broadcast_to(slot_col, (count, 256)), -1.0), axis=0, keepdims=True)

    own_slot = own_slots(own_lane >> 4)
    @pl.loop(0, CAP * half // 8)
    def _(n):
        row = lax.broadcasted_iota(jnp.int32, (128, 1), 0) + n * 128
        index = row >> 4
        tile = (index % half) * 2 + core
        hit = (own_slot == (tile * CAP + index // half).astype(F32)) & ((own_lane & 15) == (row & 15))
        crop_pick[pl.ds(pl.multiple_of(n * 128, 128), 128), :] = hit.astype(F32).astype(BF16)

    def to_expert(expert):
        return jnp.where(experts == lax.convert_element_type(expert, F32), rank, -1.0)

    to_first, to_second = to_expert(2 * chip), to_expert(2 * chip + 1)

    @pl.loop(0, half)
    def _(n):
        tile = n * 2 + core
        span = item // QUARTERS
        line = lax.broadcasted_iota(jnp.int32, (item, 1), 0)
        quarter = sum((line >= q * span).astype(jnp.int32) for q in range(1, QUARTERS))
        line = line - quarter * span
        place = sum((line >= p * classes).astype(jnp.int32) for p in range(1, span // classes)) + jnp.zeros_like(line)
        kind = line - place * classes
        listed = lax.broadcasted_iota(jnp.int32, (item, count), 1)
        wanted = listed == tile * (span // classes) + place
        given = lax.broadcasted_iota(jnp.int32, (item, 128), 1)
        right_place = ((given & 7) == kind) & ((given >> 5) == quarter)
        for s, values in enumerate((to_first, to_second)):
            slot = jnp.max(jnp.where(wanted, jnp.broadcast_to(values, (item, count)), -1.0), axis=1, keepdims=True)
            pick = (((given >> 3) & 3).astype(F32) == slot) & right_place
            back_pick[back_rows(n), s * 128 : s * 128 + 128] = pick.astype(F32).astype(BF16)

    local[4].wait()
    parts_high = image.shape[0]
    across = parts_high // 3
    group = 2 * 3 * BLK
    line = lax.broadcasted_iota(jnp.int32, (group, 1), 0)
    line_own = (line >= 3 * BLK).astype(jnp.int32)
    line_channel = (line - line_own * (3 * BLK)) // BLK
    lane = lax.broadcasted_iota(jnp.int32, (1, BLK * BLK), 1)
    source = lax.broadcasted_iota(jnp.int32, (1, parts_high), 1).astype(F32)
    keep = (line & (BLK - 1)) == (lane & (BLK - 1))
    tall_rows = image.shape[1]
    image_row = lax.broadcasted_iota(jnp.int32, (tall_rows, 1), 0)
    image_lane = (lax.broadcasted_iota(jnp.int32, (1, tall_rows), 1) // BLK).astype(F32)
    fold = ((image_row & (BLK - 1)) == (lane >> 5)).astype(F32).astype(BF16)
    own_colors[...] = jnp.zeros(own_colors.shape, F32)

    for n in range(OWN // 2):
        index = line_own + 2 * n
        at = own_values(index, local_row)
        wanted = own_values(index, block_col) * BLK + (line_channel * across + (line & (BLK - 1))).astype(F32)
        chosen = (source == wanted).astype(F32).astype(BF16)
        columns = jnp.dot(chosen, image[...], preferred_element_type=F32)
        columns = jnp.where(image_lane == at, columns, 0.0).astype(BF16)
        strips = jnp.where(keep, jnp.dot(columns, fold, preferred_element_type=F32), 0.0)
        for p in range(6):
            to = (2 * n + p // 3) * 4 + p % 3
            own_colors[to : to + 1, :] = jnp.sum(strips[p * BLK : (p + 1) * BLK], axis=0, keepdims=True)

    colors_both[core] = own_colors[...].astype(BF16)
    mate_copy(0, colors_both).start()

    local[5].wait()
    local[6].wait()

    def one_chunk(c, carry):
        @pl.when(c < chunks - AHEAD)
        def _():
            send_halo(c + AHEAD)

        @pl.when(c == 1)
        def _():
            steps(low_count, lambda step: sum_low(step).wait_recv())
            sums[1] = add_sums(0, low_count - 1, sums[0])
            steps(HIGH, lambda step: sum_high(step).start())

        @pl.when(c == 2)
        def _():
            mate_copy(0, colors_both).wait_recv()
            lane_of = own_lane[:, 0:32]
            for s in range(2):
                lane_slot = own_slots((own_lane & 31) // 4 + 8 * s)[:, 0:32]

                @pl.loop(0, half)
                def _(n, s=s, lane_slot=lane_slot):
                    row = lax.broadcasted_iota(jnp.int32, (16, 1), 0)
                    hit = (lane_slot == ((n * 2 + core) * CAP + (row >> 2)).astype(F32)) & ((lane_of & 3) == (row & 3))
                    found = jnp.dot(hit.astype(F32).astype(BF16), colors_both[s], preferred_element_type=F32)
                    rows_of = pl.ds(pl.multiple_of(n * 16, 16), 16)
                    if s == 0:
                        colors_out[rows_of, :] = found.astype(BF16)
                    else:
                        colors_out[rows_of, :] = (colors_out[rows_of, :].astype(F32) + found).astype(BF16)

            steps(HIGH, lambda step: color_high(step).start())

        @pl.when(c == chunks - 4)
        def _():
            steps(HIGH, lambda step: sum_high(step).wait_recv())
            sums[2] = add_sums(low_count - 1, HIGH - 1, sums[1])
            sum_mate().start()

        @pl.when(c == chunks - 2)
        def _():
            sum_mate().wait_recv()
            local[7].wait()
            local[8].wait()
            pooled = add_sums(low_count + HIGH - 2, 1, sums[2]) / (cells * tiles)
            context = jnp.maximum(exact_row_dot(pooled, w_pool[...]), 0.0)
            context_ref[...] = context
            offset_ref[...] = exact_row_dot(context, w_proj[4 * width :, :])

        @pl.when(c == chunks - 2)
        def _():
            steps(HIGH, lambda step: color_high(step).wait_recv())
            rows_of = pl.ds(pl.multiple_of(high * (low_count * 16), 16), low_count * 16)

            def add(n, total):
                return total + colors_high[n].astype(F32)

            colors_out[rows_of, :] = lax.fori_loop(0, HIGH - 1, add, colors_out[rows_of, :].astype(F32)).astype(BF16)
            steps(low_count, lambda step: color_low(step).start())

        for at, (start, stop) in ((chunks // 2, (0, chunks // 2)), (chunks - 1, (chunks // 2, chunks - 1))):
            @pl.when(c == at)
            def _(start=start * CHUNK, stop=stop * CHUNK):
                for k in range(3):
                    @pl.loop(0, cells // tall)
                    def _(m, k=k):
                        span = pl.ds(pl.multiple_of(m * tall, tall), tall)
                        part = jnp.dot(depth[k, span, start:stop], w_rates[k, start:stop, :], preferred_element_type=F32)
                        acc[k + 1, span, :] = part if start == 0 else acc[k + 1, span, :] + part

        lanes = pl.ds(pl.multiple_of(c * CHUNK, CHUNK), CHUNK)
        widen(feat, edge, cells, lanes)

        @pl.when(has_prev)
        def _():
            halo_copy(0, c).wait_recv()
            widen(halo.at[0], 0, edge, lanes)

        @pl.when(has_next)
        def _():
            halo_copy(1, c).wait_recv()
            widen(halo.at[1], edge + cells, edge, lanes)

        pass_halo(c + 1)

        for part in range(CHUNK // 128):
            inner = slice(part * 128, part * 128 + 128)
            outer = pl.ds(pl.multiple_of(c * CHUNK + part * 128, 128), 128)
            for k, d in enumerate(RATES):
                taps = [
                    jnp.broadcast_to(w_depth_ref[t, k : k + 1, outer].astype(F32), (8, 128)) for t in range(9)
                ]

                def weigh(parts, column, taps=taps):
                    total = None
                    for i in range(3):
                        tap = jnp.concatenate([taps[3 * i + column]] * (parts[i].shape[0] // 8), axis=0)
                        term = parts[i] * tap
                        total = term if total is None else total + term
                    return total

                @pl.loop(0, rows // 2, unroll=4)
                def _(pair, d=d, weigh=weigh, inner=inner, outer=outer, k=k):
                    results = []
                    for r in range(2):
                        parts = []
                        for i in (-1, 0, 1):
                            start = pl.multiple_of((REACH + i * d + r) * cols + pair * (2 * cols), 8)
                            parts.append(grown[pl.ds(start, cols), inner])
                        low = -(-(cols - d) // 8) * 8
                        high = (d // 8) * 8
                        middle = weigh(parts, 1)
                        left = weigh([p[:low] for p in parts], 0)
                        right = weigh([p[high:] for p in parts], 2)
                        fill = jnp.zeros((d, 128), F32)
                        left = jnp.concatenate([fill, left[: cols - d]], axis=0)
                        right = jnp.concatenate([right[d - high :], fill], axis=0)
                        results.append(jnp.maximum(middle + left + right, 0.0))
                    depth[k, pl.ds(pl.multiple_of(pair * (2 * cols), 16), 2 * cols), outer] = jnp.concatenate(
                        results, axis=0
                    ).astype(BF16)

        return carry

    lax.fori_loop(0, chunks, one_chunk, 0)

    @pl.loop(0, cells // tall)
    def _(m):
        span = pl.ds(pl.multiple_of(m * tall, tall), tall)
        blended = jnp.broadcast_to(offset_ref[...], (tall, width))
        for k in range(4):
            branch = acc[k, span, :]
            if k:
                branch += jnp.dot(
                    depth[k - 1, span, channels - CHUNK :], w_rates[k - 1, channels - CHUNK :, :], preferred_element_type=F32
                )
            branch = jnp.maximum(branch, 0.0).astype(BF16)
            blended += jnp.dot(branch, w_proj[k * width : (k + 1) * width, :], preferred_element_type=F32)
        aspp_ref[span, :] = jnp.maximum(blended, 0.0).astype(BF16)

    crops_both[core] = jnp.dot(own_pick[...], aspp_ref[...], preferred_element_type=F32).astype(BF16)
    mate_copy(1, crops_both).start()
    mate_copy(1, crops_both).wait_recv()

    @pl.loop(0, CAP * half // 8)
    def _(n):
        rows_of = pl.ds(pl.multiple_of(n * 128, 128), 128)
        found = jnp.dot(crop_pick[rows_of, 0:128], crops_both[0], preferred_element_type=F32)
        found += jnp.dot(crop_pick[rows_of, 128:256], crops_both[1], preferred_element_type=F32)
        crops_out[rows_of, :] = found.astype(BF16)

    def crop_sends(block, carry):
        steps(half, lambda step: crop_copy(block, step).start())
        return carry

    lax.fori_loop(0, CAP, crop_sends, 0)
    steps(low_count, lambda step: color_low(step).wait_recv())

    def add_low(n, total):
        return total + colors_low[n].astype(F32)

    mine_ref[...] = lax.fori_loop(
        0, low_count - 1, add_low, colors_out[pl.ds(pl.multiple_of(chip * 16, 16), 16), :].astype(F32)
    )
    side, pixels = BLK, BLK * BLK
    wide = lax.broadcasted_iota(jnp.int32, (16, pixels), 1)
    row_at, col_at = wide >> 5, wide & (side - 1)
    colors = mine_ref[...]
    pieces = []
    for i in (-1, 0, 1):
        for j in (-1, 0, 1):
            moved = colors if i == 0 and j == 0 else pltpu.roll(colors, (-(side * i + j)) % pixels, 1)
            inside = (row_at + i >= 0) & (row_at + i < side) & (col_at + j >= 0) & (col_at + j < side)
            pieces.append(jnp.where(inside, moved, 0.0))
    patches[...] = jnp.concatenate(pieces, axis=0).T.astype(BF16)

    blank = jnp.zeros((side, 3 * width), BF16)
    grid_b[0:side, :] = blank
    grid_b[side + pixels :, :] = blank
    tall, whole_tall = 512, 1024
    for n in range(9, 14):
        local[n].wait()
    scores[...] = jnp.zeros(scores.shape, F32)
    col = lax.broadcasted_iota(jnp.int32, (tall, width), 0) & (side - 1)

    @pl.loop(0, CAP)
    def _(block):
        steps(half, lambda step: crop_copy(block, step).wait_recv())

        def add_crop(n, total):
            return total + crops_in[block, n].astype(F32)

        crop = lax.fori_loop(0, half - 1, add_crop, crops_out[crop_rows(block, chip), :].astype(F32)).astype(BF16)
        for tap in range(9):
            part = jnp.dot(crop, first[tap * width : (tap + 1) * width, :], preferred_element_type=F32)
            taps_ref[tap * 16 : tap * 16 + 16, :] = part.astype(BF16)

        tap_row = lax.broadcasted_iota(jnp.int32, (144, 27), 0)
        channel = (tap_row & 15) - block * 4
        wanted_tap = (tap_row >> 4) * 3 + channel
        spread_taps = (channel >= 0) & (channel < 3) & (wanted_tap == lax.broadcasted_iota(jnp.int32, (144, 27), 1))
        tap_weights = jnp.dot(
            spread_taps.astype(F32).astype(BF16), color_ref[...], preferred_element_type=F32
        ).astype(BF16)

        @pl.loop(0, pixels // tall)
        def _(m):
            at = pl.multiple_of(m * tall, tall)
            total = jnp.dot(patches[pl.ds(at, tall), :], tap_weights, preferred_element_type=F32)
            total += jnp.dot(table_ref[pl.ds(at, tall), :], taps_ref[...], preferred_element_type=F32)
            total = jnp.maximum(total, 0.0)
            before = jnp.where(col == 0, 0.0, pltpu.roll(total, 1, 0))
            after = jnp.where(col == side - 1, 0.0, pltpu.roll(total, tall - 1, 0))
            inner = pl.ds(pl.multiple_of(side + at, side), tall)
            grid_b[inner, 0:width] = before.astype(BF16)
            grid_b[inner, width : 2 * width] = total.astype(BF16)
            grid_b[inner, 2 * width :] = after.astype(BF16)

        @pl.loop(0, pixels // whole_tall)
        def _(m, tall=whole_tall):
            at = pl.multiple_of(m * tall, tall)
            total = jnp.zeros((tall, width), F32)
            for i in range(3):
                total += jnp.dot(
                    grid_b[pl.ds(pl.multiple_of(at + side * i, side), tall), :],
                    second[3 * width * i : 3 * width * (i + 1), :],
                    preferred_element_type=F32,
                )
            total = jnp.maximum(total, 0.0).astype(BF16)
            found = lax.dot_general(
                head_ref[...], total, (((1,), (1,)), ((), ())), preferred_element_type=F32
            )
            wide_part = pixels // QUARTERS
            for q in range(tall // wide_part):
                quarter = m * (tall // wide_part) + q
                scores[pl.ds(pl.multiple_of(quarter * (8 * CAP) + block * 8, 8), classes), :] = found[
                    :, q * wide_part : (q + 1) * wide_part
                ]

    scores_both[core] = scores[...].astype(BF16)
    mate_copy(2, scores_both).start()
    mate_copy(2, scores_both).wait_recv()

    @pl.loop(0, half // 2)
    def _(n):
        rows_of = pl.ds(pl.multiple_of(n * (2 * item), 16), 2 * item)
        found = jnp.dot(back_pick[rows_of, 0:128], scores_both[0], preferred_element_type=F32)
        found += jnp.dot(back_pick[rows_of, 128:256], scores_both[1], preferred_element_type=F32)
        back_out[rows_of, :] = found.astype(BF16)

    steps(half, lambda step: back_copy(step).start())
    steps(half, lambda step: back_copy(step).wait_recv())

    def add_back(n, total):
        return total + back_in[n].astype(F32)

    result = lax.fori_loop(0, half - 1, add_back, back_out[back_rows(chip), :].astype(F32))
    span = item // QUARTERS
    wide_part = pixels // QUARTERS
    for q in range(QUARTERS):
        for p in range(span // classes):
            start = q * span + p * classes
            refined_ref[:, p, q * wide_part : (q + 1) * wide_part] = result[start : start + classes].astype(BF16)

    steps(low_count, lambda step: sum_low(step).wait_send())
    steps(HIGH, lambda step: sum_high(step).wait_send())
    sum_mate().wait_send()
    steps(HIGH, lambda step: color_high(step).wait_send())
    steps(low_count, lambda step: color_low(step).wait_send())
    steps(half, lambda step: back_copy(step).wait_send())
    for number, both in enumerate((colors_both, crops_both, scores_both)):
        mate_copy(number, both).wait_send()

    def drain_crops(block, carry):
        steps(half, lambda step: crop_copy(block, step).wait_send())
        return carry

    lax.fori_loop(0, CAP, drain_crops, 0)

    def drain_halo(c, carry):
        @pl.when(has_next)
        def _():
            halo_copy(0, c).wait_send()

        @pl.when(has_prev)
        def _():
            halo_copy(1, c).wait_send()

        return carry

    lax.fori_loop(0, chunks, drain_halo, 0)
    if low_count == 2:
        def drain_relay(c, carry):
            pass_copy(0, first_relayed + c).wait_send()
            return carry

        lax.fori_loop(0, jnp.where(gives, 0, relayed), drain_relay, 0)


def upsample_taps():
    pixels = np.arange(BLK, dtype=np.float32)
    source = np.clip((pixels + 0.5) / 8.0 - 0.5, 0.0, CELLS - 1.0)
    table = np.maximum(1.0 - np.abs(source[:, None] - np.arange(CELLS, dtype=np.float32)[None, :]), 0.0)
    moved = []
    for i in (-1, 0, 1):
        shifted = np.zeros_like(table)
        for p in range(BLK):
            if 0 <= p + i < BLK:
                shifted[p] = table[p + i]
        moved.append(shifted)
    moved = np.stack(moved)
    return np.einsum("ipa,jqb->pqijab", moved, moved).reshape(BLK * BLK, 9 * CELLS * CELLS)


def pyramid(tiles, rows, cols, features, image, blocks, routes, w_one, w_rates, w_depth, w_pool, w_proj,
            w_first, w_color, w_second, w_head):
    channels, width = w_one.shape
    cells = rows * cols
    per = CAP * CELLS * CELLS
    chunks = channels // CHUNK
    edge = REACH * cols
    places = routes.shape[0] // tiles
    classes = w_head.shape[0]
    pixels = BLK * BLK
    item = places * classes * QUARTERS
    low_count = tiles // (2 * HIGH)
    part = pixels // QUARTERS
    whole = pl.BlockSpec(memory_space=pltpu.VMEM)
    away = pl.BlockSpec(memory_space=pl.ANY)
    dma = pltpu.SemaphoreType.DMA
    image = image.transpose(0, 2, 1).reshape(-1, image.shape[1])
    first, second = w_first.reshape(9 * width, width), w_second.reshape(9 * width, width)
    operands = (
        features.reshape(cells, channels), w_one, w_rates, w_depth.transpose(1, 0, 2), w_pool, w_proj, image, first, second,
        w_color, w_head, jnp.asarray(upsample_taps(), BF16), blocks.T, routes.T,
    )

    links = low_count + HIGH
    half = tiles // 2
    return pl.pallas_call(
        functools.partial(pyramid_kernel, tiles, rows, cols, channels, width),
        out_shape=(
            jax.ShapeDtypeStruct((cells, width), BF16),
            jax.ShapeDtypeStruct((1, width), F32),
            jax.ShapeDtypeStruct((classes, places, pixels), BF16),
        ),
        in_specs=[away] * len(operands),
        out_specs=(whole, whole, whole),
        scratch_shapes=[
            *(pltpu.VMEM(operand.shape, operand.dtype) for operand in operands),
            pltpu.VMEM((2, edge, channels), BF16),
            pltpu.VMEM((cells + 2 * edge, CHUNK), F32),
            pltpu.VMEM((3, cells, channels), BF16),
            pltpu.VMEM((4, cells, width), F32),
            pltpu.VMEM((3, 1, channels), F32),
            pltpu.VMEM((links - 1, 1, channels), F32),
            pltpu.VMEM((32, pixels), F32),
            pltpu.VMEM((128, cells), BF16),
            pltpu.VMEM((half * per, 256), BF16),
            pltpu.VMEM((half * item, 256), BF16),
            pltpu.VMEM((16, pixels), F32),
            pltpu.VMEM((1, width), F32),
            pltpu.VMEM((144, width), BF16),
            pltpu.VMEM((pixels + 2 * BLK, 3 * width), BF16),
            pltpu.VMEM((pixels, 144), BF16),
            pltpu.VMEM((QUARTERS * CAP * 8, part), F32),
            pltpu.VMEM((2, 32, pixels), BF16),
            pltpu.VMEM((half * 16, pixels), BF16),
            pltpu.VMEM((HIGH - 1, low_count * 16, pixels), BF16),
            pltpu.VMEM((low_count - 1, 16, pixels), BF16),
            pltpu.VMEM((2, 128, width), BF16),
            pltpu.VMEM((half * per, width), BF16),
            pltpu.VMEM((CAP, half - 1, 16, width), BF16),
            pltpu.VMEM((2, QUARTERS * CAP * 8, part), BF16),
            pltpu.VMEM((half * item, part), BF16),
            pltpu.VMEM((half - 1, item, part), BF16),
            dma((len(operands),)),
            dma((2, chunks)),
            dma((2, chunks)),
            *(dma((links,)) for _ in range(4)),
            *(dma((CAP, half)) for _ in range(2)),
            *(dma((half,)) for _ in range(2)),
            *(dma((3,)) for _ in range(2)),
            pltpu.VMEM((2 * (HIGH - 1), edge, CHUNK), BF16),
            *(dma((2 * (HIGH - 1),)) for _ in range(2)),
        ],
        compiler_params=pltpu.CompilerParams(collective_id=0, has_side_effects=True, vmem_limit_bytes=60 << 20),
        name="pyramid",
    )(*operands)


def settle_kernel(*refs):
    half = len(refs) // 2
    for source, target in zip(refs[:half], refs[half:]):
        target[...] = source[...]


def settle(*arrays):
    return pl.pallas_call(
        settle_kernel,
        out_shape=tuple(jax.ShapeDtypeStruct(a.shape, a.dtype) for a in arrays),
        name="settle",
    )(*arrays)


def shards(
    tiles,
    features,
    aerial_image,
    blocks,
    routes,
    w_one,
    w_depth,
    w_rates,
    w_pool,
    w_proj,
    w_first,
    w_color,
    w_second,
    w_head,
):
    rows, cols, channels = features.shape
    width = w_one.shape[1]
    aspp, context, refined = pyramid(
        tiles, rows, cols, features, aerial_image, blocks, routes, w_one, w_rates, w_depth, w_pool, w_proj,
        w_first[0], w_color[0], w_second[0], w_head[0],
    )
    aspp, context, refined = settle(aspp, context, refined)
    return aspp.reshape(rows, cols, width), context.reshape(width), refined.transpose(1, 0, 2)


def solution(mesh):
    return jax.shard_map(
        functools.partial(shards, mesh.shape["tile"]),
        mesh=mesh,
        in_specs=(
            P(("groups", "tile"), None, None),
            P(None, ("groups", "tile"), None),
            P("groups", None),
            P("groups", None),
            P(),
            P(),
            P(),
            P(),
            P(),
            P("tile", None, None, None),
            P("tile", None, None),
            P("tile", None, None, None),
            P("tile", None, None),
        ),
        out_specs=(
            P(("groups", "tile"), None, None),
            P("groups"),
            P(("groups", "tile"), None, None),
        ),
        check_vma=False,
    )
```

```python
import functools

import jax
import jax.numpy as jnp
import numpy as np
from jax import lax
from jax.experimental import pallas as pl
from jax.experimental.pallas import tpu as pltpu
from jax.sharding import PartitionSpec as P

BLK = 32
CAP = 4
CELLS = 4
RATES = (6, 12, 18)
REACH = 18
CHUNK = 256
HIGH = 4
QUARTERS = 4
COLOR_ROWS = 112
AHEAD = 4
RELAY_AHEAD = 6
PARTS = 2
OWN = 6
F32 = jnp.float32
BF16 = jnp.bfloat16


def split_three(value):
    high = value.astype(BF16)
    rest = value - high.astype(F32)
    mid = rest.astype(BF16)
    low = (rest - mid.astype(F32)).astype(BF16)
    return high, mid, low


def exact_row_dot(row, weights):
    high, mid, low = split_three(row)
    stacked = jnp.concatenate(
        [high.astype(F32), mid.astype(F32), low.astype(F32), jnp.zeros((13, row.shape[1]), F32)], axis=0
    ).astype(BF16)
    product = jnp.dot(stacked, weights, preferred_element_type=F32)
    return product[0:1] + product[1:2] + product[2:3]


def pyramid_kernel(
    tiles, rows, cols, channels, width,
    feat_hbm, w_one_hbm, w_rates_hbm, w_depth_hbm, w_pool_hbm, w_proj_hbm, image_hbm, first_hbm, second_hbm,
    color_hbm, head_hbm, table_hbm, blocks_hbm, routes_hbm,
    aspp_ref, context_ref, refined_ref,
    feat, w_one, w_rates, w_depth_ref, w_pool, w_proj, image, first, second, color_ref, head_ref, table_ref, blocks_ref, routes_ref,
    halo, grown, depth, acc, sums, sums_in, own_colors, own_pick, crop_pick, back_pick, mine_ref, offset_ref,
    taps_ref, grids, scores,
    colors_both, colors_out, colors_high, colors_low, crops_both, crops_out, crops_in, scores_both, back_out, back_in,
    local_sem, halo_send, halo_recv, sum_send, sum_recv, color_send, color_recv, crop_send, crop_recv, back_send, back_recv,
    mate_send, mate_recv, relay, relay_send, relay_recv,
):
    me = lax.axis_index("tile")
    chunks = channels // CHUNK
    edge = REACH * cols
    cells = rows * cols
    count = routes_ref.shape[1]
    classes = head_ref.shape[0]
    half, low_count = tiles // 2, tiles // (2 * HIGH)
    core = lax.rem(me, 2)
    low = lax.rem(me // 2, low_count)
    high = me // (2 * low_count)
    chip = me // 2

    local = [
        pltpu.make_async_copy(source, target, local_sem.at[n])
        for n, (source, target) in enumerate(
            ((feat_hbm, feat), (blocks_hbm, blocks_ref), (routes_hbm, routes_ref), (w_one_hbm, w_one), (image_hbm, image),
             (w_depth_hbm, w_depth_ref), (w_rates_hbm, w_rates), (w_pool_hbm, w_pool), (w_proj_hbm, w_proj),
             (color_hbm, color_ref), (head_hbm, head_ref), (table_hbm, table_ref), (first_hbm, first), (second_hbm, second))
        )
    ]
    for copy in local:
        copy.start()

    mate = me + 1 - 2 * core

    def low_peer(step):
        return (high * low_count + lax.rem(low + step, low_count)) * 2 + core

    def high_peer(step):
        return (lax.rem(high + step, HIGH) * low_count + low) * 2 + core

    has_next = me < tiles - 1
    has_prev = me > 0
    barrier = pltpu.get_barrier_semaphore()

    def greet(peer):
        pl.semaphore_signal(barrier, inc=1, device_id={"tile": peer}, device_id_type=pl.DeviceIdType.MESH)

    def chip_peer(step):
        return lax.rem(chip + step, half) * 2 + core

    def greet_chip(step, carry):
        greet(chip_peer(step))
        return carry

    outward = jnp.where(core == 1, me + 1, me - 1)
    has_outward = (outward >= 0) & (outward < tiles)

    slanted = jnp.where(core == 1, me + 3, me - 3)
    has_slanted = (slanted >= 0) & (slanted < tiles) if low_count == 2 else False
    forward = jnp.where(high < HIGH - 1, 2 * (HIGH - 1 - high) + 1, 0)
    relayed = jnp.where(core == 1, forward, 2 * high) if low_count == 2 else 0
    gives = low == core
    first_relayed = chunks - relayed

    @pl.when(has_outward)
    def _():
        greet(outward)

    if low_count == 2:
        @pl.when(has_slanted)
        def _():
            greet(slanted)

    greet(mate)
    lax.fori_loop(1, half, greet_chip, 0)
    local[0].wait()

    def sum_rows(n, totals):
        block = feat[pl.ds(pl.multiple_of(n * 16, 16), 16), :].astype(F32)
        return totals + block[0:8] + block[8:16]

    totals = lax.fori_loop(0, cells // 16, sum_rows, jnp.zeros((8, channels), F32))
    sums[0] = jnp.sum(totals, axis=0, keepdims=True)

    expected = half + has_outward.astype(jnp.int32)
    pl.semaphore_wait(barrier, expected + has_slanted.astype(jnp.int32) if low_count == 2 else expected)

    def send(source, target, send_sem, recv_sem, peer):
        return pltpu.make_async_remote_copy(
            src_ref=source, dst_ref=target, send_sem=send_sem, recv_sem=recv_sem,
            device_id={"tile": peer}, device_id_type=pl.DeviceIdType.MESH,
        )

    def halo_copy(side, c):
        lanes = pl.ds(pl.multiple_of(c * CHUNK, CHUNK), CHUNK)
        return send(
            feat_hbm.at[pl.ds(cells - edge if side == 0 else 0, edge), lanes], halo.at[side, :, lanes],
            halo_send.at[side, c], halo_recv.at[side, c],
            lax.rem(me + 1, tiles) if side == 0 else lax.rem(me + tiles - 1, tiles),
        )

    def relay_copy(side, c):
        lanes = pl.ds(pl.multiple_of(c * CHUNK, CHUNK), CHUNK)
        return send(
            feat_hbm.at[pl.ds(cells - edge if side == 0 else 0, edge), lanes], relay.at[c - first_relayed],
            halo_send.at[side, c], relay_recv.at[c - first_relayed], low_peer(1),
        )

    def pass_copy(side, c):
        lanes = pl.ds(pl.multiple_of(c * CHUNK, CHUNK), CHUNK)
        slot = c - first_relayed
        return send(relay.at[slot], halo.at[side, :, lanes], relay_send.at[slot], halo_recv.at[side, c], slanted)

    def relays(side, c):
        return (core == 1 - side) & gives & (c >= first_relayed)

    def send_direct(c):
        for side, present in ((0, has_next), (1, has_prev)):
            if low_count == 2:
                present = present & jnp.logical_not(relays(side, c))

            @pl.when(present)
            def _(side=side):
                halo_copy(side, c).start()

    def send_relay(c):
        if low_count == 2:
            for side in range(2):
                @pl.when(relays(side, c))
                def _(side=side):
                    relay_copy(side, c).start()

    def pass_halo(c):
        if low_count == 2:
            for side in range(2):
                @pl.when((core == 1 - side) & jnp.logical_not(gives) & (c >= first_relayed) & (c < chunks))
                def _(side=side):
                    relay_copy(side, c).wait_recv()
                    pass_copy(side, c).start()

    def steps(number, function):
        def body(step, carry):
            function(step)
            return carry

        lax.fori_loop(1, number, body, 0)

    def mate_copy(number, both):
        return send(both.at[core], both.at[core], mate_send.at[number], mate_recv.at[number], mate)

    def color_high(step):
        rows_of = pl.ds(pl.multiple_of(lax.rem(high + step, HIGH) * (low_count * 16), 16), low_count * 16)
        return send(colors_out.at[rows_of], colors_high.at[step - 1], color_send.at[step], color_recv.at[step], high_peer(step))

    def color_low(step):
        rows_of = pl.ds(pl.multiple_of((high * low_count + lax.rem(low + step, low_count)) * 16, 16), 16)
        slot = HIGH + step
        return send(colors_out.at[rows_of], colors_low.at[step - 1], color_send.at[slot], color_recv.at[slot], low_peer(step))

    def crop_rows(block, to_chip):
        return pl.ds(pl.multiple_of((block * half + to_chip) * 16, 16), 16)

    def crop_copy(block, step):
        return send(
            crops_out.at[crop_rows(block, lax.rem(chip + step, half))], crops_in.at[block, step - 1],
            crop_send.at[block, step], crop_recv.at[block, step], chip_peer(step),
        )

    item = back_pick.shape[0] // half

    def back_rows(to_chip):
        return pl.ds(pl.multiple_of(to_chip * item, 16), item)

    def back_copy(m, step):
        return send(
            back_out.at[m, back_rows(lax.rem(chip + step, half))], back_in.at[m, step - 1],
            back_send.at[m, step], back_recv.at[m, step], chip_peer(step),
        )

    def sum_low(step):
        return send(sums.at[0], sums_in.at[step - 1], sum_send.at[step], sum_recv.at[step], low_peer(step))

    def sum_high(step):
        slot = low_count + step
        return send(sums.at[1], sums_in.at[slot - 2], sum_send.at[slot], sum_recv.at[slot], high_peer(step))

    def sum_mate():
        return send(sums.at[2], sums_in.at[low_count + HIGH - 2], sum_send.at[0], sum_recv.at[0], mate)

    def add_sums(start, number, total):
        return lax.fori_loop(0, number, lambda n, value: value + sums_in[start + n], total)

    steps(low_count, lambda step: sum_low(step).start())
    send_direct(0)
    for c in range(1, AHEAD):
        send_direct(c)
    for c in range(RELAY_AHEAD):
        send_relay(c)

    tall = 768
    local[3].wait()

    @pl.loop(0, cells // tall)
    def _(m):
        span = pl.ds(pl.multiple_of(m * tall, tall), tall)
        acc[0, span, :] = jnp.dot(feat[span, :], w_one[...], preferred_element_type=F32)

    @pl.when(jnp.logical_not(has_prev))
    def _():
        grown[0:edge, :] = jnp.zeros((edge, CHUNK), F32)

    @pl.when(jnp.logical_not(has_next))
    def _():
        grown[edge + cells :, :] = jnp.zeros((edge, CHUNK), F32)

    def widen(source, start, count, lanes):
        @pl.loop(0, count // 48)
        def _(n):
            grown[pl.ds(pl.multiple_of(start + n * 48, 8), 48), :] = source[
                pl.ds(pl.multiple_of(n * 48, 16), 48), lanes
            ].astype(F32)

    local[1].wait()
    local[2].wait()
    experts = routes_ref[...].astype(F32)
    square = (count, count)
    down, over = lax.broadcasted_iota(jnp.int32, square, 0), lax.broadcasted_iota(jnp.int32, square, 1)
    spread = jnp.broadcast_to(experts, square)

    def stand(row):
        return jnp.sum(jnp.where(down == over, jnp.broadcast_to(row, square), 0.0), axis=1, keepdims=True)

    upright = stand(experts)
    rank = jnp.sum(jnp.where((upright == spread) & (down < over), 1.0, 0.0), axis=0, keepdims=True)
    strip_blocks = rows // CELLS
    block_row, block_col = blocks_ref[0:1, :].astype(F32), blocks_ref[1:2, :].astype(F32)
    strip_row = (blocks_ref[0:1, :] // strip_blocks).astype(F32)
    strip_col = stand(strip_row)
    beside = jnp.broadcast_to(strip_row, square) == strip_col
    first_strip = lax.convert_element_type(chip * 2, F32)

    def listed_at(strip, place):
        within = strip - first_strip
        return jnp.where((within >= 0) & (within < 2), within * 8 + place, -1.0)

    own_row_index = listed_at(strip_row, jnp.sum(jnp.where(beside & (down < over), 1.0, 0.0), axis=0, keepdims=True))
    own_col_index = listed_at(strip_col, jnp.sum(jnp.where(beside & (over < down), 1.0, 0.0), axis=1, keepdims=True))
    slot_col = upright * CAP + jnp.sum(jnp.where((upright == spread) & (over < down), 1.0, 0.0), axis=1, keepdims=True)
    local_row = block_row - lax.convert_element_type(me * strip_blocks, F32)

    def own_values(index, values):
        shape = (index.shape[0], count)
        hit = jnp.broadcast_to(own_row_index, shape) == (index + core * 8).astype(F32)
        return jnp.max(jnp.where(hit, jnp.broadcast_to(values, shape), -1e6), axis=1, keepdims=True)

    own_row = lax.broadcasted_iota(jnp.int32, (128, 1), 0)
    own_base = own_values(own_row >> 4, local_row * (CELLS * cols) + block_col * CELLS)
    wanted_cell = own_base + (((own_row >> 2) & 3) * cols + (own_row & 3)).astype(F32)
    cell_at = lax.broadcasted_iota(jnp.int32, (128, cells), 1).astype(F32)
    own_pick[...] = (cell_at == wanted_cell).astype(F32).astype(BF16)

    own_lane = lax.broadcasted_iota(jnp.int32, (1, 256), 1)

    def own_slots(index):
        hit = own_col_index == index.astype(F32)
        return jnp.max(jnp.where(hit, jnp.broadcast_to(slot_col, (count, 256)), -1.0), axis=0, keepdims=True)

    own_slot = own_slots(own_lane >> 4)
    @pl.loop(0, CAP * half // 8)
    def _(n):
        row = lax.broadcasted_iota(jnp.int32, (128, 1), 0) + n * 128
        index = row >> 4
        tile = (index % half) * 2 + core
        hit = (own_slot == (tile * CAP + index // half).astype(F32)) & ((own_lane & 15) == (row & 15))
        crop_pick[pl.ds(pl.multiple_of(n * 128, 128), 128), :] = hit.astype(F32).astype(BF16)

    def to_expert(expert):
        return jnp.where(experts == lax.convert_element_type(expert, F32), rank, -1.0)

    to_first, to_second = to_expert(2 * chip), to_expert(2 * chip + 1)

    @pl.loop(0, half)
    def _(n):
        tile = n * 2 + core
        span = item // QUARTERS
        line = lax.broadcasted_iota(jnp.int32, (item, 1), 0)
        quarter = sum((line >= q * span).astype(jnp.int32) for q in range(1, QUARTERS))
        line = line - quarter * span
        place = sum((line >= p * classes).astype(jnp.int32) for p in range(1, span // classes)) + jnp.zeros_like(line)
        kind = line - place * classes
        listed = lax.broadcasted_iota(jnp.int32, (item, count), 1)
        wanted = listed == tile * (span // classes) + place
        given = lax.broadcasted_iota(jnp.int32, (item, 128), 1)
        right_place = ((given & 7) == kind) & ((given >> 5) == quarter)
        for s, values in enumerate((to_first, to_second)):
            slot = jnp.max(jnp.where(wanted, jnp.broadcast_to(values, (item, count)), -1.0), axis=1, keepdims=True)
            pick = (((given >> 3) & 3).astype(F32) == slot) & right_place
            back_pick[back_rows(n), s * 128 : s * 128 + 128] = pick.astype(F32).astype(BF16)

    steps(low_count, lambda step: sum_low(step).wait_recv())
    sums[1] = add_sums(0, low_count - 1, sums[0])
    steps(HIGH, lambda step: sum_high(step).start())

    local[4].wait()
    parts_high = image.shape[0]
    across = parts_high // 3
    group = 2 * 3 * BLK
    line = lax.broadcasted_iota(jnp.int32, (group, 1), 0)
    line_own = (line >= 3 * BLK).astype(jnp.int32)
    line_channel = (line - line_own * (3 * BLK)) // BLK
    lane = lax.broadcasted_iota(jnp.int32, (1, BLK * BLK), 1)
    source = lax.broadcasted_iota(jnp.int32, (1, parts_high), 1).astype(F32)
    keep = (line & (BLK - 1)) == (lane & (BLK - 1))
    tall_rows = image.shape[1]
    image_row = lax.broadcasted_iota(jnp.int32, (tall_rows, 1), 0)
    image_lane = (lax.broadcasted_iota(jnp.int32, (1, tall_rows), 1) // BLK).astype(F32)
    fold = ((image_row & (BLK - 1)) == (lane >> 5)).astype(F32).astype(BF16)
    own_colors[...] = jnp.zeros(own_colors.shape, F32)

    for n in range(OWN // 2):
        index = line_own + 2 * n
        at = own_values(index, local_row)
        wanted = own_values(index, block_col) * BLK + (line_channel * across + (line & (BLK - 1))).astype(F32)
        chosen = (source == wanted).astype(F32).astype(BF16)
        columns = jnp.dot(chosen, image[...], preferred_element_type=F32)
        columns = jnp.where(image_lane == at, columns, 0.0).astype(BF16)
        strips = jnp.where(keep, jnp.dot(columns, fold, preferred_element_type=F32), 0.0)
        for p in range(6):
            to = (2 * n + p // 3) * 4 + p % 3
            own_colors[to : to + 1, :] = jnp.sum(strips[p * BLK : (p + 1) * BLK], axis=0, keepdims=True)

    colors_both[core] = own_colors[...].astype(BF16)
    mate_copy(0, colors_both).start()

    local[5].wait()
    local[6].wait()

    def one_chunk(c, carry):
        @pl.when(c < chunks - AHEAD)
        def _():
            send_direct(c + AHEAD)

        @pl.when(c < chunks - RELAY_AHEAD)
        def _():
            send_relay(c + RELAY_AHEAD)

        @pl.when(c == 2)
        def _():
            mate_copy(0, colors_both).wait_recv()
            lane_of = own_lane[:, 0:32]
            for s in range(2):
                lane_slot = own_slots((own_lane & 31) // 4 + 8 * s)[:, 0:32]

                @pl.loop(0, half)
                def _(n, s=s, lane_slot=lane_slot):
                    row = lax.broadcasted_iota(jnp.int32, (16, 1), 0)
                    hit = (lane_slot == ((n * 2 + core) * CAP + (row >> 2)).astype(F32)) & ((lane_of & 3) == (row & 3))
                    found = jnp.dot(hit.astype(F32).astype(BF16), colors_both[s], preferred_element_type=F32)
                    rows_of = pl.ds(pl.multiple_of(n * 16, 16), 16)
                    if s == 0:
                        colors_out[rows_of, :] = found.astype(BF16)
                    else:
                        colors_out[rows_of, :] = (colors_out[rows_of, :].astype(F32) + found).astype(BF16)

            steps(HIGH, lambda step: color_high(step).start())

        @pl.when(c == 1)
        def _():
            steps(HIGH, lambda step: sum_high(step).wait_recv())
            sums[2] = add_sums(low_count - 1, HIGH - 1, sums[1])
            sum_mate().start()

        @pl.when(c == 3)
        def _():
            sum_mate().wait_recv()
            local[7].wait()
            local[8].wait()
            pooled = add_sums(low_count + HIGH - 2, 1, sums[2]) / (cells * tiles)
            context = jnp.maximum(exact_row_dot(pooled, w_pool[...]), 0.0)
            context_ref[...] = context
            offset_ref[...] = exact_row_dot(context, w_proj[4 * width :, :])

        @pl.when(c == chunks - 2)
        def _():
            steps(HIGH, lambda step: color_high(step).wait_recv())
            rows_of = pl.ds(pl.multiple_of(high * (low_count * 16), 16), low_count * 16)

            def add(n, total):
                return total + colors_high[n].astype(F32)

            colors_out[rows_of, :] = lax.fori_loop(0, HIGH - 1, add, colors_out[rows_of, :].astype(F32)).astype(BF16)
            steps(low_count, lambda step: color_low(step).start())

        for at, (start, stop) in ((chunks // 2, (0, chunks // 2)), (chunks - 1, (chunks // 2, chunks - 1))):
            @pl.when(c == at)
            def _(start=start * CHUNK, stop=stop * CHUNK):
                for k in range(3):
                    @pl.loop(0, cells // tall)
                    def _(m, k=k):
                        span = pl.ds(pl.multiple_of(m * tall, tall), tall)
                        part = jnp.dot(depth[k, span, start:stop], w_rates[k, start:stop, :], preferred_element_type=F32)
                        acc[k + 1, span, :] = part if start == 0 else acc[k + 1, span, :] + part

        lanes = pl.ds(pl.multiple_of(c * CHUNK, CHUNK), CHUNK)
        widen(feat, edge, cells, lanes)

        def take(side, present):
            @pl.when(present)
            def _():
                halo_copy(side, c).wait_recv()
                widen(halo.at[side], 0 if side == 0 else edge + cells, edge, lanes)

        def map_rows(late):
            for part in range(CHUNK // 128):
                inner = slice(part * 128, part * 128 + 128)
                outer = pl.ds(pl.multiple_of(c * CHUNK + part * 128, 128), 128)
                for k, d in enumerate(RATES):
                    taps = [
                        jnp.broadcast_to(w_depth_ref[t, k : k + 1, outer].astype(F32), (8, 128)) for t in range(9)
                    ]

                    def weigh(parts, column, taps=taps):
                        total = None
                        for i in range(3):
                            tap = jnp.concatenate([taps[3 * i + column]] * (parts[i].shape[0] // 8), axis=0)
                            term = parts[i] * tap
                            total = term if total is None else total + term
                        return total

                    def two_rows(pair, d=d, weigh=weigh, inner=inner, outer=outer, k=k):
                        results = []
                        for r in range(2):
                            parts = []
                            for i in (-1, 0, 1):
                                start = pl.multiple_of((REACH + i * d + r) * cols + pair * (2 * cols), 8)
                                parts.append(grown[pl.ds(start, cols), inner])
                            low = -(-(cols - d) // 8) * 8
                            high = (d // 8) * 8
                            middle = weigh(parts, 1)
                            left = weigh([p[:low] for p in parts], 0)
                            right = weigh([p[high:] for p in parts], 2)
                            fill = jnp.zeros((d, 128), F32)
                            left = jnp.concatenate([fill, left[: cols - d]], axis=0)
                            right = jnp.concatenate([right[d - high :], fill], axis=0)
                            results.append(jnp.maximum(middle + left + right, 0.0))
                        depth[k, pl.ds(pl.multiple_of(pair * (2 * cols), 16), 2 * cols), outer] = jnp.concatenate(
                            results, axis=0
                        ).astype(BF16)

                    pairs = d // 2 if late else (rows - d) // 2
                    after = core == 1 if late else core == 0
                    first_pair = jnp.where(after, rows // 2 - pairs, 0)
                    unroll = max(u for u in (3, 4, 5) if pairs % u == 0 or pairs % u == 1)
                    for n in range(pairs % unroll):
                        two_rows(first_pair + n)
                    first_pair += pairs % unroll

                    @pl.loop(0, pairs // unroll)
                    def _(n, two_rows=two_rows, first_pair=first_pair, unroll=unroll):
                        for u in range(unroll):
                            two_rows(first_pair + n * unroll + u)

        take(1, has_next & (core == 0))
        take(0, has_prev & (core == 1))
        map_rows(False)
        pass_halo(c + 1)
        take(0, has_prev & (core == 0))
        take(1, has_next & (core == 1))
        map_rows(True)
        return carry

    lax.fori_loop(0, chunks, one_chunk, 0)

    @pl.loop(0, cells // tall)
    def _(m):
        span = pl.ds(pl.multiple_of(m * tall, tall), tall)
        blended = jnp.broadcast_to(offset_ref[...], (tall, width))
        for k in range(4):
            branch = acc[k, span, :]
            if k:
                branch += jnp.dot(
                    depth[k - 1, span, channels - CHUNK :], w_rates[k - 1, channels - CHUNK :, :], preferred_element_type=F32
                )
            branch = jnp.maximum(branch, 0.0).astype(BF16)
            blended += jnp.dot(branch, w_proj[k * width : (k + 1) * width, :], preferred_element_type=F32)
        aspp_ref[span, :] = jnp.maximum(blended, 0.0).astype(BF16)

    crops_both[core] = jnp.dot(own_pick[...], aspp_ref[...], preferred_element_type=F32).astype(BF16)
    mate_copy(1, crops_both).start()
    steps(low_count, lambda step: color_low(step).wait_recv())

    def add_low(n, total):
        return total + colors_low[n].astype(F32)

    mine_ref[...] = lax.fori_loop(
        0, low_count - 1, add_low, colors_out[pl.ds(pl.multiple_of(chip * 16, 16), 16), :].astype(F32)
    )
    side, pixels = BLK, BLK * BLK
    wide = lax.broadcasted_iota(jnp.int32, (3 * CAP, pixels), 1)
    row_at, col_at = wide >> 5, wide & (side - 1)
    received = mine_ref[...]
    colors = jnp.concatenate([received[4 * n : 4 * n + 3] for n in range(CAP)], axis=0)
    local[11].wait()
    pieces = []
    for i in (-1, 0, 1):
        for j in (-1, 0, 1):
            moved = colors if i == 0 and j == 0 else pltpu.roll(colors, (-(side * i + j)) % pixels, 1)
            inside = (row_at + i >= 0) & (row_at + i < side) & (col_at + j >= 0) & (col_at + j < side)
            pieces.append(jnp.where(inside, moved, 0.0))
    pieces.append(jnp.zeros((128 - 9 * 3 * CAP, pixels), F32))
    spread_colors = jnp.concatenate(pieces, axis=0).T.astype(BF16)
    table_ref[:, 0:128] = (table_ref[:, 0:128].astype(F32) + spread_colors.astype(F32)).astype(BF16)

    mate_copy(1, crops_both).wait_recv()

    @pl.loop(0, CAP)
    def _(block):
        @pl.loop(0, half // 8)
        def _(n):
            rows_of = pl.ds(pl.multiple_of((block * (half // 8) + n) * 128, 128), 128)
            found = jnp.dot(crop_pick[rows_of, 0:128], crops_both[0], preferred_element_type=F32)
            found += jnp.dot(crop_pick[rows_of, 128:256], crops_both[1], preferred_element_type=F32)
            crops_out[rows_of, :] = found.astype(BF16)

        steps(half, lambda step: crop_copy(block, step).start())

    blank = jnp.zeros((side, 3 * width), BF16)
    for block in range(CAP):
        grids[block, 0:side, :] = blank
        grids[block, side + pixels :, :] = blank
    for n in (9, 10, 12, 13):
        local[n].wait()
    tap_row = lax.broadcasted_iota(jnp.int32, (COLOR_ROWS, 27), 0)
    pixel_tap = lax.broadcasted_iota(jnp.int32, (COLOR_ROWS, 27), 1)
    tap_of = sum((pixel_tap >= 3 * n).astype(jnp.int32) for n in range(1, 9))
    for block in range(CAP):
        wanted = tap_of * (3 * CAP) + 3 * block + pixel_tap - 3 * tap_of
        spread_taps = (tap_row == wanted).astype(F32).astype(BF16)
        taps_ref[block, 0:COLOR_ROWS, :] = jnp.dot(spread_taps, color_ref[...], preferred_element_type=F32).astype(BF16)
    scores[...] = jnp.zeros(scores.shape, F32)
    tall = pixels // PARTS
    col = lax.broadcasted_iota(jnp.int32, (tall, width), 0) & (side - 1)

    def open_block(block):
        steps(half, lambda step: crop_copy(block, step).wait_recv())

        def add_crop(n, total):
            return total + crops_in[block, n].astype(F32)

        crop = lax.fori_loop(0, half - 1, add_crop, crops_out[crop_rows(block, chip), :].astype(F32)).astype(BF16)
        for tap in range(9):
            part = jnp.dot(crop, first[tap * width : (tap + 1) * width, :], preferred_element_type=F32)
            taps_ref[block, COLOR_ROWS + tap * 16 : COLOR_ROWS + tap * 16 + 16, :] = part.astype(BF16)

    def first_conv(block):
        @pl.loop(0, PARTS)
        def _(m):
            at = pl.multiple_of(m * tall, tall)
            total = jnp.dot(table_ref[pl.ds(at, tall), :], taps_ref[block], preferred_element_type=F32)
            total = jnp.maximum(total, 0.0)
            before = jnp.where(col == 0, 0.0, pltpu.roll(total, 1, 0))
            after = jnp.where(col == side - 1, 0.0, pltpu.roll(total, tall - 1, 0))
            inner = pl.ds(pl.multiple_of(side + at, side), tall)
            grids[block, inner, 0:width] = before.astype(BF16)
            grids[block, inner, width : 2 * width] = total.astype(BF16)
            grids[block, inner, 2 * width :] = after.astype(BF16)

    def second_conv(pair, m):
        at = m * tall
        total = None
        for i in range(3):
            rows_of = slice(at + side * i, at + side * i + tall)
            both = jnp.concatenate([grids[2 * pair, rows_of, :], grids[2 * pair + 1, rows_of, :]], axis=0)
            term = jnp.dot(both, second[3 * width * i : 3 * width * (i + 1), :], preferred_element_type=F32)
            total = term if total is None else total + term
        total = jnp.maximum(total, 0.0).astype(BF16)
        found = lax.dot_general(head_ref[...], total, (((1,), (1,)), ((), ())), preferred_element_type=F32)
        wide_part = tall // QUARTERS
        for b in range(2):
            for q in range(QUARTERS):
                start = pl.multiple_of(q * (8 * CAP) + (2 * pair + b) * 8, 8)
                left = b * tall + q * wide_part
                scores[m, pl.ds(start, classes), :] = found[:, left : left + wide_part]

    def back_swap(m):
        scores_both[m, core] = scores[m].astype(BF16)
        mate_copy(2 + m, scores_both.at[m]).start()

    def back_spread(m):
        mate_copy(2 + m, scores_both.at[m]).wait_recv()

        @pl.loop(0, half // 2)
        def _(n):
            rows_of = pl.ds(pl.multiple_of(n * (2 * item), 16), 2 * item)
            found = jnp.dot(back_pick[rows_of, 0:128], scores_both[m, 0], preferred_element_type=F32)
            found += jnp.dot(back_pick[rows_of, 128:256], scores_both[m, 1], preferred_element_type=F32)
            back_out[m, rows_of, :] = found.astype(BF16)

        steps(half, lambda step: back_copy(m, step).start())

    def back_finish(m):
        steps(half, lambda step: back_copy(m, step).wait_recv())

        def add_back(n, total):
            return total + back_in[m, n].astype(F32)

        result = lax.fori_loop(0, half - 1, add_back, back_out[m, back_rows(chip), :].astype(F32))
        span = item // QUARTERS
        wide_part = pixels // (PARTS * QUARTERS)
        for q in range(QUARTERS):
            for p in range(span // classes):
                start = q * span + p * classes
                left = (m * QUARTERS + q) * wide_part
                refined_ref[:, p, left : left + wide_part] = result[start : start + classes].astype(BF16)

    @pl.loop(0, CAP // 2)
    def _(pair):
        @pl.loop(0, 2)
        def _(n):
            open_block(2 * pair + n)
            first_conv(2 * pair + n)

        second_conv(pair, 0)

    for m in range(1, PARTS):
        back_swap(m - 1)
        second_conv(0, m)
        back_spread(m - 1)

        @pl.loop(1, CAP // 2)
        def _(pair, m=m):
            second_conv(pair, m)

    back_swap(PARTS - 1)
    back_spread(PARTS - 1)
    steps(low_count, lambda step: sum_low(step).wait_send())
    steps(HIGH, lambda step: sum_high(step).wait_send())
    sum_mate().wait_send()
    steps(HIGH, lambda step: color_high(step).wait_send())
    steps(low_count, lambda step: color_low(step).wait_send())
    for number, both in enumerate((colors_both, crops_both)):
        mate_copy(number, both).wait_send()

    def drain_crops(block, carry):
        steps(half, lambda step: crop_copy(block, step).wait_send())
        return carry

    lax.fori_loop(0, CAP, drain_crops, 0)

    def drain_halo(c, carry):
        @pl.when(has_next)
        def _():
            halo_copy(0, c).wait_send()

        @pl.when(has_prev)
        def _():
            halo_copy(1, c).wait_send()

        return carry

    lax.fori_loop(0, chunks, drain_halo, 0)
    if low_count == 2:
        def drain_relay(c, carry):
            pass_copy(0, first_relayed + c).wait_send()
            return carry

        lax.fori_loop(0, jnp.where(gives, 0, relayed), drain_relay, 0)

    for m in range(PARTS):
        back_finish(m)

    for m in range(PARTS):
        steps(half, lambda step, m=m: back_copy(m, step).wait_send())
        mate_copy(2 + m, scores_both.at[m]).wait_send()


def upsample_taps():
    pixels = np.arange(BLK, dtype=np.float32)
    source = np.clip((pixels + 0.5) / 8.0 - 0.5, 0.0, CELLS - 1.0)
    table = np.maximum(1.0 - np.abs(source[:, None] - np.arange(CELLS, dtype=np.float32)[None, :]), 0.0)
    moved = []
    for i in (-1, 0, 1):
        shifted = np.zeros_like(table)
        for p in range(BLK):
            if 0 <= p + i < BLK:
                shifted[p] = table[p + i]
        moved.append(shifted)
    moved = np.stack(moved)
    table = np.einsum("ipa,jqb->pqijab", moved, moved).reshape(BLK * BLK, 9 * CELLS * CELLS)
    return np.pad(table, ((0, 0), (COLOR_ROWS, 0)))


def pyramid(tiles, rows, cols, features, image, blocks, routes, w_one, w_rates, w_depth, w_pool, w_proj,
            w_first, w_color, w_second, w_head):
    channels, width = w_one.shape
    cells = rows * cols
    per = CAP * CELLS * CELLS
    chunks = channels // CHUNK
    edge = REACH * cols
    places = routes.shape[0] // tiles
    classes = w_head.shape[0]
    pixels = BLK * BLK
    item = places * classes * QUARTERS
    low_count = tiles // (2 * HIGH)
    part = pixels // (PARTS * QUARTERS)
    whole = pl.BlockSpec(memory_space=pltpu.VMEM)
    away = pl.BlockSpec(memory_space=pl.ANY)
    dma = pltpu.SemaphoreType.DMA
    image = image.transpose(0, 2, 1).reshape(-1, image.shape[1])
    first, second = w_first.reshape(9 * width, width), w_second.reshape(9 * width, width)
    operands = (
        features.reshape(cells, channels), w_one, w_rates, w_depth.transpose(1, 0, 2), w_pool, w_proj, image, first, second,
        w_color, w_head, jnp.asarray(upsample_taps(), BF16), blocks.T, routes.T,
    )

    links = low_count + HIGH
    half = tiles // 2
    return pl.pallas_call(
        functools.partial(pyramid_kernel, tiles, rows, cols, channels, width),
        out_shape=(
            jax.ShapeDtypeStruct((cells, width), BF16),
            jax.ShapeDtypeStruct((1, width), F32),
            jax.ShapeDtypeStruct((classes, places, pixels), BF16),
        ),
        in_specs=[away] * len(operands),
        out_specs=(whole, whole, whole),
        scratch_shapes=[
            *(pltpu.VMEM(operand.shape, operand.dtype) for operand in operands),
            pltpu.VMEM((2, edge, channels), BF16),
            pltpu.VMEM((cells + 2 * edge, CHUNK), F32),
            pltpu.VMEM((3, cells, channels), BF16),
            pltpu.VMEM((4, cells, width), F32),
            pltpu.VMEM((3, 1, channels), F32),
            pltpu.VMEM((links - 1, 1, channels), F32),
            pltpu.VMEM((32, pixels), F32),
            pltpu.VMEM((128, cells), BF16),
            pltpu.VMEM((half * per, 256), BF16),
            pltpu.VMEM((half * item, 256), BF16),
            pltpu.VMEM((16, pixels), F32),
            pltpu.VMEM((1, width), F32),
            pltpu.VMEM((CAP, COLOR_ROWS + 144, width), BF16),
            pltpu.VMEM((CAP, pixels + 2 * BLK, 3 * width), BF16),
            pltpu.VMEM((PARTS, QUARTERS * CAP * 8, part), F32),
            pltpu.VMEM((2, 32, pixels), BF16),
            pltpu.VMEM((half * 16, pixels), BF16),
            pltpu.VMEM((HIGH - 1, low_count * 16, pixels), BF16),
            pltpu.VMEM((low_count - 1, 16, pixels), BF16),
            pltpu.VMEM((2, 128, width), BF16),
            pltpu.VMEM((half * per, width), BF16),
            pltpu.VMEM((CAP, half - 1, 16, width), BF16),
            pltpu.VMEM((PARTS, 2, QUARTERS * CAP * 8, part), BF16),
            pltpu.VMEM((PARTS, half * item, part), BF16),
            pltpu.VMEM((PARTS, half - 1, item, part), BF16),
            dma((len(operands),)),
            dma((2, chunks)),
            dma((2, chunks)),
            *(dma((links,)) for _ in range(4)),
            *(dma((CAP, half)) for _ in range(2)),
            *(dma((PARTS, half)) for _ in range(2)),
            *(dma((2 + PARTS,)) for _ in range(2)),
            pltpu.VMEM((2 * HIGH - 1, edge, CHUNK), BF16),
            *(dma((2 * HIGH - 1,)) for _ in range(2)),
        ],
        compiler_params=pltpu.CompilerParams(collective_id=0, has_side_effects=True, vmem_limit_bytes=60 << 20),
        name="pyramid",
    )(*operands)


def settle_kernel(*refs):
    half = len(refs) // 2
    for source, target in zip(refs[:half], refs[half:]):
        target[...] = source[...]


def settle(*arrays):
    return pl.pallas_call(
        settle_kernel,
        out_shape=tuple(jax.ShapeDtypeStruct(a.shape, a.dtype) for a in arrays),
        name="settle",
    )(*arrays)


def shards(
    tiles,
    features,
    aerial_image,
    blocks,
    routes,
    w_one,
    w_depth,
    w_rates,
    w_pool,
    w_proj,
    w_first,
    w_color,
    w_second,
    w_head,
):
    rows, cols, channels = features.shape
    width = w_one.shape[1]
    aspp, context, refined = pyramid(
        tiles, rows, cols, features, aerial_image, blocks, routes, w_one, w_rates, w_depth, w_pool, w_proj,
        w_first[0], w_color[0], w_second[0], w_head[0],
    )
    aspp, context, refined = settle(aspp, context, refined)
    return aspp.reshape(rows, cols, width), context.reshape(width), refined.transpose(1, 0, 2)


def solution(mesh):
    return jax.shard_map(
        functools.partial(shards, mesh.shape["tile"]),
        mesh=mesh,
        in_specs=(
            P(("groups", "tile"), None, None),
            P(None, ("groups", "tile"), None),
            P("groups", None),
            P("groups", None),
            P(),
            P(),
            P(),
            P(),
            P(),
            P("tile", None, None, None),
            P("tile", None, None),
            P("tile", None, None, None),
            P("tile", None, None),
        ),
        out_specs=(
            P(("groups", "tile"), None, None),
            P("groups"),
            P(("groups", "tile"), None, None),
        ),
        check_vma=False,
    )
```

```python
import functools

import jax
import jax.numpy as jnp
import numpy as np
from jax import lax
from jax.experimental import pallas as pl
from jax.experimental.pallas import tpu as pltpu
from jax.sharding import PartitionSpec as P

BLK = 32
CAP = 4
CELLS = 4
RATES = (6, 12, 18)
REACH = 18
CHUNK = 256
HIGH = 4
QUARTERS = 4
COLOR_ROWS = 112
AHEAD = 4
RELAY_AHEAD = 6
PARTS = 2
OWN = 6
F32 = jnp.float32
BF16 = jnp.bfloat16


def split_three(value):
    high = value.astype(BF16)
    rest = value - high.astype(F32)
    mid = rest.astype(BF16)
    low = (rest - mid.astype(F32)).astype(BF16)
    return high, mid, low


def exact_row_dot(row, weights):
    high, mid, low = split_three(row)
    stacked = jnp.concatenate(
        [high.astype(F32), mid.astype(F32), low.astype(F32), jnp.zeros((13, row.shape[1]), F32)], axis=0
    ).astype(BF16)
    product = jnp.dot(stacked, weights, preferred_element_type=F32)
    return product[0:1] + product[1:2] + product[2:3]


def pyramid_kernel(
    tiles, rows, cols, channels, width,
    feat_hbm, w_one_hbm, w_rates_hbm, w_depth_hbm, w_pool_hbm, w_proj_hbm, image_hbm, first_hbm, second_hbm,
    color_hbm, head_hbm, table_hbm, blocks_hbm, routes_hbm,
    aspp_hbm, context_hbm, refined_hbm,
    aspp_ref, context_ref, refined_ref, out_sem,
    feat, w_one, w_rates, w_depth_ref, w_pool, w_proj, image, first, second, color_ref, head_ref, table_ref, blocks_ref, routes_ref,
    halo, grown, depth, acc, sums, sums_in, own_colors, own_pick, crop_pick, back_pick, mine_ref, offset_ref,
    taps_ref, grids, scores,
    colors_both, colors_out, colors_high, colors_low, crops_both, crops_out, crops_in, scores_both, back_out, back_in,
    local_sem, halo_send, halo_recv, sum_send, sum_recv, color_send, color_recv, crop_send, crop_recv, back_send, back_recv,
    mate_send, mate_recv, relay, relay_send, relay_recv,
):
    me = lax.axis_index("tile")
    chunks = channels // CHUNK
    edge = REACH * cols
    cells = rows * cols
    count = routes_ref.shape[1]
    classes = head_ref.shape[0]
    half, low_count = tiles // 2, tiles // (2 * HIGH)
    core = lax.rem(me, 2)
    low = lax.rem(me // 2, low_count)
    high = me // (2 * low_count)
    chip = me // 2

    local = [
        pltpu.make_async_copy(source, target, local_sem.at[n])
        for n, (source, target) in enumerate(
            ((feat_hbm, feat), (blocks_hbm, blocks_ref), (routes_hbm, routes_ref), (w_one_hbm, w_one), (image_hbm, image),
             (w_depth_hbm, w_depth_ref), (w_rates_hbm, w_rates), (w_pool_hbm, w_pool), (w_proj_hbm, w_proj),
             (color_hbm, color_ref), (head_hbm, head_ref), (table_hbm, table_ref), (first_hbm, first), (second_hbm, second))
        )
    ]
    for copy in local:
        copy.start()

    mate = me + 1 - 2 * core

    def low_peer(step):
        return (high * low_count + lax.rem(low + step, low_count)) * 2 + core

    def high_peer(step):
        return (lax.rem(high + step, HIGH) * low_count + low) * 2 + core

    has_next = me < tiles - 1
    has_prev = me > 0
    barrier = pltpu.get_barrier_semaphore()

    def greet(peer):
        pl.semaphore_signal(barrier, inc=1, device_id={"tile": peer}, device_id_type=pl.DeviceIdType.MESH)

    def chip_peer(step):
        return lax.rem(chip + step, half) * 2 + core

    def greet_chip(step, carry):
        greet(chip_peer(step))
        return carry

    outward = jnp.where(core == 1, me + 1, me - 1)
    has_outward = (outward >= 0) & (outward < tiles)

    slanted = jnp.where(core == 1, me + 3, me - 3)
    has_slanted = (slanted >= 0) & (slanted < tiles) if low_count == 2 else False
    forward = jnp.where(high < HIGH - 1, 2 * (HIGH - 1 - high) + 1, 0)
    relayed = jnp.where(core == 1, forward, 2 * high) if low_count == 2 else 0
    gives = low == core
    first_relayed = chunks - relayed

    @pl.when(has_outward)
    def _():
        greet(outward)

    if low_count == 2:
        @pl.when(has_slanted)
        def _():
            greet(slanted)

    greet(mate)
    lax.fori_loop(1, half, greet_chip, 0)
    local[0].wait()

    def sum_rows(n, totals):
        block = feat[pl.ds(pl.multiple_of(n * 16, 16), 16), :].astype(F32)
        return totals + block[0:8] + block[8:16]

    totals = lax.fori_loop(0, cells // 16, sum_rows, jnp.zeros((8, channels), F32))
    sums[0] = jnp.sum(totals, axis=0, keepdims=True)

    expected = half + has_outward.astype(jnp.int32)
    pl.semaphore_wait(barrier, expected + has_slanted.astype(jnp.int32) if low_count == 2 else expected)

    def send(source, target, send_sem, recv_sem, peer):
        return pltpu.make_async_remote_copy(
            src_ref=source, dst_ref=target, send_sem=send_sem, recv_sem=recv_sem,
            device_id={"tile": peer}, device_id_type=pl.DeviceIdType.MESH,
        )

    def halo_copy(side, c):
        lanes = pl.ds(pl.multiple_of(c * CHUNK, CHUNK), CHUNK)
        return send(
            feat_hbm.at[pl.ds(cells - edge if side == 0 else 0, edge), lanes], halo.at[side, :, lanes],
            halo_send.at[side, c], halo_recv.at[side, c],
            lax.rem(me + 1, tiles) if side == 0 else lax.rem(me + tiles - 1, tiles),
        )

    def relay_copy(side, c):
        lanes = pl.ds(pl.multiple_of(c * CHUNK, CHUNK), CHUNK)
        return send(
            feat_hbm.at[pl.ds(cells - edge if side == 0 else 0, edge), lanes], relay.at[c - first_relayed],
            halo_send.at[side, c], relay_recv.at[c - first_relayed], low_peer(1),
        )

    def pass_copy(side, c):
        lanes = pl.ds(pl.multiple_of(c * CHUNK, CHUNK), CHUNK)
        slot = c - first_relayed
        return send(relay.at[slot], halo.at[side, :, lanes], relay_send.at[slot], halo_recv.at[side, c], slanted)

    def relays(side, c):
        return (core == 1 - side) & gives & (c >= first_relayed)

    def send_direct(c):
        for side, present in ((0, has_next), (1, has_prev)):
            if low_count == 2:
                present = present & jnp.logical_not(relays(side, c))

            @pl.when(present)
            def _(side=side):
                halo_copy(side, c).start()

    def send_relay(c):
        if low_count == 2:
            for side in range(2):
                @pl.when(relays(side, c))
                def _(side=side):
                    relay_copy(side, c).start()

    def pass_halo(c):
        if low_count == 2:
            for side in range(2):
                @pl.when((core == 1 - side) & jnp.logical_not(gives) & (c >= first_relayed) & (c < chunks))
                def _(side=side):
                    relay_copy(side, c).wait_recv()
                    pass_copy(side, c).start()

    def steps(number, function):
        def body(step, carry):
            function(step)
            return carry

        lax.fori_loop(1, number, body, 0)

    def mate_copy(number, both):
        return send(both.at[core], both.at[core], mate_send.at[number], mate_recv.at[number], mate)

    def color_high(step):
        rows_of = pl.ds(pl.multiple_of(lax.rem(high + step, HIGH) * (low_count * 16), 16), low_count * 16)
        return send(colors_out.at[rows_of], colors_high.at[step - 1], color_send.at[step], color_recv.at[step], high_peer(step))

    def color_low(step):
        rows_of = pl.ds(pl.multiple_of((high * low_count + lax.rem(low + step, low_count)) * 16, 16), 16)
        slot = HIGH + step
        return send(colors_out.at[rows_of], colors_low.at[step - 1], color_send.at[slot], color_recv.at[slot], low_peer(step))

    def crop_rows(block, to_chip):
        return pl.ds(pl.multiple_of((block * half + to_chip) * 16, 16), 16)

    def crop_copy(block, step):
        return send(
            crops_out.at[crop_rows(block, lax.rem(chip + step, half))], crops_in.at[block, step - 1],
            crop_send.at[block, step], crop_recv.at[block, step], chip_peer(step),
        )

    item = back_pick.shape[0] // half

    def back_rows(to_chip):
        return pl.ds(pl.multiple_of(to_chip * item, 16), item)

    def back_copy(m, step):
        return send(
            back_out.at[m, back_rows(lax.rem(chip + step, half))], back_in.at[m, step - 1],
            back_send.at[m, step], back_recv.at[m, step], chip_peer(step),
        )

    def sum_low(step):
        return send(sums.at[0], sums_in.at[step - 1], sum_send.at[step], sum_recv.at[step], low_peer(step))

    def sum_high(step):
        slot = low_count + step
        return send(sums.at[1], sums_in.at[slot - 2], sum_send.at[slot], sum_recv.at[slot], high_peer(step))

    def sum_mate():
        return send(sums.at[2], sums_in.at[low_count + HIGH - 2], sum_send.at[0], sum_recv.at[0], mate)

    def add_sums(start, number, total):
        return lax.fori_loop(0, number, lambda n, value: value + sums_in[start + n], total)

    steps(low_count, lambda step: sum_low(step).start())
    send_direct(0)
    for c in range(1, AHEAD):
        send_direct(c)
    for c in range(RELAY_AHEAD):
        send_relay(c)

    tall = 768
    local[3].wait()

    @pl.loop(0, cells // tall)
    def _(m):
        span = pl.ds(pl.multiple_of(m * tall, tall), tall)
        acc[0, span, :] = jnp.dot(feat[span, :], w_one[...], preferred_element_type=F32)

    @pl.when(jnp.logical_not(has_prev))
    def _():
        grown[0:edge, :] = jnp.zeros((edge, CHUNK), F32)

    @pl.when(jnp.logical_not(has_next))
    def _():
        grown[edge + cells :, :] = jnp.zeros((edge, CHUNK), F32)

    def widen(source, start, count, lanes):
        @pl.loop(0, count // 48)
        def _(n):
            grown[pl.ds(pl.multiple_of(start + n * 48, 8), 48), :] = source[
                pl.ds(pl.multiple_of(n * 48, 16), 48), lanes
            ].astype(F32)

    local[1].wait()
    local[2].wait()
    experts = routes_ref[...].astype(F32)
    square = (count, count)
    down, over = lax.broadcasted_iota(jnp.int32, square, 0), lax.broadcasted_iota(jnp.int32, square, 1)
    spread = jnp.broadcast_to(experts, square)

    def stand(row):
        return jnp.sum(jnp.where(down == over, jnp.broadcast_to(row, square), 0.0), axis=1, keepdims=True)

    upright = stand(experts)
    rank = jnp.sum(jnp.where((upright == spread) & (down < over), 1.0, 0.0), axis=0, keepdims=True)
    strip_blocks = rows // CELLS
    block_row, block_col = blocks_ref[0:1, :].astype(F32), blocks_ref[1:2, :].astype(F32)
    strip_row = (blocks_ref[0:1, :] // strip_blocks).astype(F32)
    strip_col = stand(strip_row)
    beside = jnp.broadcast_to(strip_row, square) == strip_col
    first_strip = lax.convert_element_type(chip * 2, F32)

    def listed_at(strip, place):
        within = strip - first_strip
        return jnp.where((within >= 0) & (within < 2), within * 8 + place, -1.0)

    own_row_index = listed_at(strip_row, jnp.sum(jnp.where(beside & (down < over), 1.0, 0.0), axis=0, keepdims=True))
    own_col_index = listed_at(strip_col, jnp.sum(jnp.where(beside & (over < down), 1.0, 0.0), axis=1, keepdims=True))
    slot_col = upright * CAP + jnp.sum(jnp.where((upright == spread) & (over < down), 1.0, 0.0), axis=1, keepdims=True)
    local_row = block_row - lax.convert_element_type(me * strip_blocks, F32)

    def own_values(index, values):
        shape = (index.shape[0], count)
        hit = jnp.broadcast_to(own_row_index, shape) == (index + core * 8).astype(F32)
        return jnp.max(jnp.where(hit, jnp.broadcast_to(values, shape), -1e6), axis=1, keepdims=True)

    own_row = lax.broadcasted_iota(jnp.int32, (128, 1), 0)
    own_base = own_values(own_row >> 4, local_row * (CELLS * cols) + block_col * CELLS)
    wanted_cell = own_base + (((own_row >> 2) & 3) * cols + (own_row & 3)).astype(F32)
    cell_at = lax.broadcasted_iota(jnp.int32, (128, cells), 1).astype(F32)
    own_pick[...] = (cell_at == wanted_cell).astype(F32).astype(BF16)

    own_lane = lax.broadcasted_iota(jnp.int32, (1, 256), 1)

    def own_slots(index):
        hit = own_col_index == index.astype(F32)
        return jnp.max(jnp.where(hit, jnp.broadcast_to(slot_col, (count, 256)), -1.0), axis=0, keepdims=True)

    own_slot = own_slots(own_lane >> 4)
    @pl.loop(0, CAP * half // 8)
    def _(n):
        row = lax.broadcasted_iota(jnp.int32, (128, 1), 0) + n * 128
        index = row >> 4
        tile = (index % half) * 2 + core
        hit = (own_slot == (tile * CAP + index // half).astype(F32)) & ((own_lane & 15) == (row & 15))
        crop_pick[pl.ds(pl.multiple_of(n * 128, 128), 128), :] = hit.astype(F32).astype(BF16)

    def to_expert(expert):
        return jnp.where(experts == lax.convert_element_type(expert, F32), rank, -1.0)

    to_first, to_second = to_expert(2 * chip), to_expert(2 * chip + 1)

    @pl.loop(0, half)
    def _(n):
        tile = n * 2 + core
        span = item // QUARTERS
        line = lax.broadcasted_iota(jnp.int32, (item, 1), 0)
        quarter = sum((line >= q * span).astype(jnp.int32) for q in range(1, QUARTERS))
        line = line - quarter * span
        place = sum((line >= p * classes).astype(jnp.int32) for p in range(1, span // classes)) + jnp.zeros_like(line)
        kind = line - place * classes
        listed = lax.broadcasted_iota(jnp.int32, (item, count), 1)
        wanted = listed == tile * (span // classes) + place
        given = lax.broadcasted_iota(jnp.int32, (item, 128), 1)
        right_place = ((given & 7) == kind) & ((given >> 5) == quarter)
        for s, values in enumerate((to_first, to_second)):
            slot = jnp.max(jnp.where(wanted, jnp.broadcast_to(values, (item, count)), -1.0), axis=1, keepdims=True)
            pick = (((given >> 3) & 3).astype(F32) == slot) & right_place
            back_pick[back_rows(n), s * 128 : s * 128 + 128] = pick.astype(F32).astype(BF16)

    steps(low_count, lambda step: sum_low(step).wait_recv())
    sums[1] = add_sums(0, low_count - 1, sums[0])
    steps(HIGH, lambda step: sum_high(step).start())

    local[4].wait()
    parts_high = image.shape[0]
    across = parts_high // 3
    group = 2 * 3 * BLK
    line = lax.broadcasted_iota(jnp.int32, (group, 1), 0)
    line_own = (line >= 3 * BLK).astype(jnp.int32)
    line_channel = (line - line_own * (3 * BLK)) // BLK
    lane = lax.broadcasted_iota(jnp.int32, (1, BLK * BLK), 1)
    source = lax.broadcasted_iota(jnp.int32, (1, parts_high), 1).astype(F32)
    keep = (line & (BLK - 1)) == (lane & (BLK - 1))
    tall_rows = image.shape[1]
    image_row = lax.broadcasted_iota(jnp.int32, (tall_rows, 1), 0)
    image_lane = (lax.broadcasted_iota(jnp.int32, (1, tall_rows), 1) // BLK).astype(F32)
    fold = ((image_row & (BLK - 1)) == (lane >> 5)).astype(F32).astype(BF16)
    own_colors[...] = jnp.zeros(own_colors.shape, F32)

    for n in range(OWN // 2):
        index = line_own + 2 * n
        at = own_values(index, local_row)
        wanted = own_values(index, block_col) * BLK + (line_channel * across + (line & (BLK - 1))).astype(F32)
        chosen = (source == wanted).astype(F32).astype(BF16)
        columns = jnp.dot(chosen, image[...], preferred_element_type=F32)
        columns = jnp.where(image_lane == at, columns, 0.0).astype(BF16)
        strips = jnp.where(keep, jnp.dot(columns, fold, preferred_element_type=F32), 0.0)
        for p in range(6):
            to = (2 * n + p // 3) * 4 + p % 3
            own_colors[to : to + 1, :] = jnp.sum(strips[p * BLK : (p + 1) * BLK], axis=0, keepdims=True)

    colors_both[core] = own_colors[...].astype(BF16)
    mate_copy(0, colors_both).start()

    local[5].wait()
    local[6].wait()

    def one_chunk(c, carry):
        @pl.when(c < chunks - AHEAD)
        def _():
            send_direct(c + AHEAD)

        @pl.when(c < chunks - RELAY_AHEAD)
        def _():
            send_relay(c + RELAY_AHEAD)

        @pl.when(c == 2)
        def _():
            mate_copy(0, colors_both).wait_recv()
            lane_of = own_lane[:, 0:32]
            for s in range(2):
                lane_slot = own_slots((own_lane & 31) // 4 + 8 * s)[:, 0:32]

                @pl.loop(0, half)
                def _(n, s=s, lane_slot=lane_slot):
                    row = lax.broadcasted_iota(jnp.int32, (16, 1), 0)
                    hit = (lane_slot == ((n * 2 + core) * CAP + (row >> 2)).astype(F32)) & ((lane_of & 3) == (row & 3))
                    found = jnp.dot(hit.astype(F32).astype(BF16), colors_both[s], preferred_element_type=F32)
                    rows_of = pl.ds(pl.multiple_of(n * 16, 16), 16)
                    if s == 0:
                        colors_out[rows_of, :] = found.astype(BF16)
                    else:
                        colors_out[rows_of, :] = (colors_out[rows_of, :].astype(F32) + found).astype(BF16)

            steps(HIGH, lambda step: color_high(step).start())

        @pl.when(c == 1)
        def _():
            steps(HIGH, lambda step: sum_high(step).wait_recv())
            sums[2] = add_sums(low_count - 1, HIGH - 1, sums[1])
            sum_mate().start()

        @pl.when(c == 3)
        def _():
            sum_mate().wait_recv()
            local[7].wait()
            local[8].wait()
            pooled = add_sums(low_count + HIGH - 2, 1, sums[2]) / (cells * tiles)
            context = jnp.maximum(exact_row_dot(pooled, w_pool[...]), 0.0)
            context_ref[...] = context
            offset_ref[...] = exact_row_dot(context, w_proj[4 * width :, :])

        @pl.when(c == chunks - 2)
        def _():
            steps(HIGH, lambda step: color_high(step).wait_recv())
            rows_of = pl.ds(pl.multiple_of(high * (low_count * 16), 16), low_count * 16)

            def add(n, total):
                return total + colors_high[n].astype(F32)

            colors_out[rows_of, :] = lax.fori_loop(0, HIGH - 1, add, colors_out[rows_of, :].astype(F32)).astype(BF16)
            steps(low_count, lambda step: color_low(step).start())

        @pl.when(c == chunks - 1)
        def _():
            @pl.loop(0, cells // tall)
            def _(m):
                span = pl.ds(pl.multiple_of(m * tall, tall), tall)
                branch = jnp.maximum(acc[0, span, :], 0.0).astype(BF16)
                acc[0, span, :] = offset_ref[...] + jnp.dot(branch, w_proj[0:width, :], preferred_element_type=F32)

        for at, (start, stop) in ((chunks // 2, (0, chunks // 2)), (chunks - 1, (chunks // 2, chunks - 1))):
            @pl.when(c == at)
            def _(start=start * CHUNK, stop=stop * CHUNK):
                for k in range(3):
                    @pl.loop(0, cells // tall)
                    def _(m, k=k):
                        span = pl.ds(pl.multiple_of(m * tall, tall), tall)
                        part = jnp.dot(depth[k, span, start:stop], w_rates[k, start:stop, :], preferred_element_type=F32)
                        acc[k + 1, span, :] = part if start == 0 else acc[k + 1, span, :] + part

        lanes = pl.ds(pl.multiple_of(c * CHUNK, CHUNK), CHUNK)
        widen(feat, edge, cells, lanes)

        def take(side, present):
            @pl.when(present)
            def _():
                halo_copy(side, c).wait_recv()
                widen(halo.at[side], 0 if side == 0 else edge + cells, edge, lanes)

        def map_rows(late):
            for part in range(CHUNK // 128):
                inner = slice(part * 128, part * 128 + 128)
                outer = pl.ds(pl.multiple_of(c * CHUNK + part * 128, 128), 128)
                for k, d in enumerate(RATES):
                    taps = [
                        jnp.broadcast_to(w_depth_ref[t, k : k + 1, outer].astype(F32), (8, 128)) for t in range(9)
                    ]

                    def weigh(parts, column, taps=taps):
                        total = None
                        for i in range(3):
                            tap = jnp.concatenate([taps[3 * i + column]] * (parts[i].shape[0] // 8), axis=0)
                            term = parts[i] * tap
                            total = term if total is None else total + term
                        return total

                    def two_rows(pair, d=d, weigh=weigh, inner=inner, outer=outer, k=k):
                        results = []
                        for r in range(2):
                            parts = []
                            for i in (-1, 0, 1):
                                start = pl.multiple_of((REACH + i * d + r) * cols + pair * (2 * cols), 8)
                                parts.append(grown[pl.ds(start, cols), inner])
                            low = -(-(cols - d) // 8) * 8
                            high = (d // 8) * 8
                            middle = weigh(parts, 1)
                            left = weigh([p[:low] for p in parts], 0)
                            right = weigh([p[high:] for p in parts], 2)
                            fill = jnp.zeros((d, 128), F32)
                            left = jnp.concatenate([fill, left[: cols - d]], axis=0)
                            right = jnp.concatenate([right[d - high :], fill], axis=0)
                            results.append(jnp.maximum(middle + left + right, 0.0))
                        depth[k, pl.ds(pl.multiple_of(pair * (2 * cols), 16), 2 * cols), outer] = jnp.concatenate(
                            results, axis=0
                        ).astype(BF16)

                    pairs = d // 2 if late else (rows - d) // 2
                    after = core == 1 if late else core == 0
                    first_pair = jnp.where(after, rows // 2 - pairs, 0)
                    unroll = max(u for u in (3, 4, 5) if pairs % u == 0 or pairs % u == 1)
                    for n in range(pairs % unroll):
                        two_rows(first_pair + n)
                    first_pair += pairs % unroll

                    @pl.loop(0, pairs // unroll)
                    def _(n, two_rows=two_rows, first_pair=first_pair, unroll=unroll):
                        for u in range(unroll):
                            two_rows(first_pair + n * unroll + u)

        take(1, has_next & (core == 0))
        take(0, has_prev & (core == 1))
        map_rows(False)
        pass_halo(c + 1)
        take(0, has_prev & (core == 0))
        take(1, has_next & (core == 1))
        map_rows(True)
        return carry

    lax.fori_loop(0, chunks, one_chunk, 0)

    @pl.loop(0, cells // tall)
    def _(m):
        span = pl.ds(pl.multiple_of(m * tall, tall), tall)
        blended = acc[0, span, :]
        for k in range(1, 4):
            branch = acc[k, span, :] + jnp.dot(
                depth[k - 1, span, channels - CHUNK :], w_rates[k - 1, channels - CHUNK :, :], preferred_element_type=F32
            )
            branch = jnp.maximum(branch, 0.0).astype(BF16)
            blended += jnp.dot(branch, w_proj[k * width : (k + 1) * width, :], preferred_element_type=F32)
        aspp_ref[span, :] = jnp.maximum(blended, 0.0).astype(BF16)

    leaving = [
        pltpu.make_async_copy(source, target, out_sem.at[n])
        for n, (source, target) in enumerate(((aspp_ref, aspp_hbm), (context_ref, context_hbm), (refined_ref, refined_hbm)))
    ]
    leaving[0].start()
    leaving[1].start()
    crops_both[core] = jnp.dot(own_pick[...], aspp_ref[...], preferred_element_type=F32).astype(BF16)
    mate_copy(1, crops_both).start()
    steps(low_count, lambda step: color_low(step).wait_recv())

    def add_low(n, total):
        return total + colors_low[n].astype(F32)

    mine_ref[...] = lax.fori_loop(
        0, low_count - 1, add_low, colors_out[pl.ds(pl.multiple_of(chip * 16, 16), 16), :].astype(F32)
    )
    side, pixels = BLK, BLK * BLK
    wide = lax.broadcasted_iota(jnp.int32, (3 * CAP, pixels), 1)
    row_at, col_at = wide >> 5, wide & (side - 1)
    received = mine_ref[...]
    colors = jnp.concatenate([received[4 * n : 4 * n + 3] for n in range(CAP)], axis=0)
    local[11].wait()
    pieces = []
    for i in (-1, 0, 1):
        for j in (-1, 0, 1):
            moved = colors if i == 0 and j == 0 else pltpu.roll(colors, (-(side * i + j)) % pixels, 1)
            inside = (row_at + i >= 0) & (row_at + i < side) & (col_at + j >= 0) & (col_at + j < side)
            pieces.append(jnp.where(inside, moved, 0.0))
    pieces.append(jnp.zeros((128 - 9 * 3 * CAP, pixels), F32))
    spread_colors = jnp.concatenate(pieces, axis=0).T.astype(BF16)
    table_ref[:, 0:128] = (table_ref[:, 0:128].astype(F32) + spread_colors.astype(F32)).astype(BF16)

    mate_copy(1, crops_both).wait_recv()

    @pl.loop(0, CAP)
    def _(block):
        @pl.loop(0, half // 8)
        def _(n):
            rows_of = pl.ds(pl.multiple_of((block * (half // 8) + n) * 128, 128), 128)
            found = jnp.dot(crop_pick[rows_of, :], crops_both[...].reshape(256, width), preferred_element_type=F32)
            crops_out[rows_of, :] = found.astype(BF16)

        steps(half, lambda step: crop_copy(block, step).start())

    blank = jnp.zeros((side, 3 * width), BF16)
    for block in range(CAP):
        grids[block, 0:side, :] = blank
        grids[block, side + pixels :, :] = blank
    for n in (9, 10, 12, 13):
        local[n].wait()
    tap_row = lax.broadcasted_iota(jnp.int32, (COLOR_ROWS, 27), 0)
    pixel_tap = lax.broadcasted_iota(jnp.int32, (COLOR_ROWS, 27), 1)
    tap_of = sum((pixel_tap >= 3 * n).astype(jnp.int32) for n in range(1, 9))
    for block in range(CAP):
        wanted = tap_of * (3 * CAP) + 3 * block + pixel_tap - 3 * tap_of
        spread_taps = (tap_row == wanted).astype(F32).astype(BF16)
        taps_ref[block, 0:COLOR_ROWS, :] = jnp.dot(spread_taps, color_ref[...], preferred_element_type=F32).astype(BF16)
    scores[...] = jnp.zeros(scores.shape, F32)
    tall = pixels // PARTS
    col = lax.broadcasted_iota(jnp.int32, (tall, width), 0) & (side - 1)

    def open_block(block):
        steps(half, lambda step: crop_copy(block, step).wait_recv())

        def add_crop(n, total):
            return total + crops_in[block, n].astype(F32)

        crop = lax.fori_loop(0, half - 1, add_crop, crops_out[crop_rows(block, chip), :].astype(F32)).astype(BF16)
        for tap in range(9):
            part = jnp.dot(crop, first[tap * width : (tap + 1) * width, :], preferred_element_type=F32)
            taps_ref[block, COLOR_ROWS + tap * 16 : COLOR_ROWS + tap * 16 + 16, :] = part.astype(BF16)

    def first_conv(block):
        @pl.loop(0, PARTS)
        def _(m):
            at = pl.multiple_of(m * tall, tall)
            total = jnp.dot(table_ref[pl.ds(at, tall), :], taps_ref[block], preferred_element_type=F32)
            total = jnp.maximum(total, 0.0)
            before = jnp.where(col == 0, 0.0, pltpu.roll(total, 1, 0))
            after = jnp.where(col == side - 1, 0.0, pltpu.roll(total, tall - 1, 0))
            inner = pl.ds(pl.multiple_of(side + at, side), tall)
            grids[block, inner, 0:width] = before.astype(BF16)
            grids[block, inner, width : 2 * width] = total.astype(BF16)
            grids[block, inner, 2 * width :] = after.astype(BF16)

    def second_conv(pair, m):
        at = m * tall
        total = None
        for i in range(3):
            rows_of = slice(at + side * i, at + side * i + tall)
            both = jnp.concatenate([grids[2 * pair, rows_of, :], grids[2 * pair + 1, rows_of, :]], axis=0)
            term = jnp.dot(both, second[3 * width * i : 3 * width * (i + 1), :], preferred_element_type=F32)
            total = term if total is None else total + term
        total = jnp.maximum(total, 0.0).astype(BF16)
        found = lax.dot_general(head_ref[...], total, (((1,), (1,)), ((), ())), preferred_element_type=F32)
        wide_part = tall // QUARTERS
        for b in range(2):
            for q in range(QUARTERS):
                start = pl.multiple_of(q * (8 * CAP) + (2 * pair + b) * 8, 8)
                left = b * tall + q * wide_part
                scores[m, pl.ds(start, classes), :] = found[:, left : left + wide_part]

    def back_swap(m):
        scores_both[m, core] = scores[m].astype(BF16)
        mate_copy(2 + m, scores_both.at[m]).start()

    def back_spread(m):
        mate_copy(2 + m, scores_both.at[m]).wait_recv()

        @pl.loop(0, half // 2)
        def _(n):
            rows_of = pl.ds(pl.multiple_of(n * (2 * item), 16), 2 * item)
            found = jnp.dot(back_pick[rows_of, 0:128], scores_both[m, 0], preferred_element_type=F32)
            found += jnp.dot(back_pick[rows_of, 128:256], scores_both[m, 1], preferred_element_type=F32)
            back_out[m, rows_of, :] = found.astype(BF16)
            for t in range(2):
                step = lax.rem(2 * n + t - chip + half, half)

                @pl.when(step > 0)
                def _(step=step):
                    back_copy(m, step).start()


    def back_finish(m):
        steps(half, lambda step: back_copy(m, step).wait_recv())

        def add_back(n, total):
            return total + back_in[m, n].astype(F32)

        result = lax.fori_loop(0, half - 1, add_back, back_out[m, back_rows(chip), :].astype(F32))
        span = item // QUARTERS
        wide_part = pixels // (PARTS * QUARTERS)
        for q in range(QUARTERS):
            for p in range(span // classes):
                start = q * span + p * classes
                left = (m * QUARTERS + q) * wide_part
                refined_ref[:, p, left : left + wide_part] = result[start : start + classes].astype(BF16)

    @pl.loop(0, CAP // 2)
    def _(pair):
        @pl.loop(0, 2)
        def _(n):
            open_block(2 * pair + n)
            first_conv(2 * pair + n)

        second_conv(pair, 0)

    for m in range(1, PARTS):
        back_swap(m - 1)
        second_conv(0, m)
        back_spread(m - 1)

        @pl.loop(1, CAP // 2)
        def _(pair, m=m):
            second_conv(pair, m)

    back_swap(PARTS - 1)
    back_spread(PARTS - 1)
    steps(low_count, lambda step: sum_low(step).wait_send())
    steps(HIGH, lambda step: sum_high(step).wait_send())
    sum_mate().wait_send()
    steps(HIGH, lambda step: color_high(step).wait_send())
    steps(low_count, lambda step: color_low(step).wait_send())
    for number, both in enumerate((colors_both, crops_both)):
        mate_copy(number, both).wait_send()

    def drain_crops(block, carry):
        steps(half, lambda step: crop_copy(block, step).wait_send())
        return carry

    lax.fori_loop(0, CAP, drain_crops, 0)

    def drain_halo(c, carry):
        @pl.when(has_next)
        def _():
            halo_copy(0, c).wait_send()

        @pl.when(has_prev)
        def _():
            halo_copy(1, c).wait_send()

        return carry

    lax.fori_loop(0, chunks, drain_halo, 0)
    if low_count == 2:
        def drain_relay(c, carry):
            pass_copy(0, first_relayed + c).wait_send()
            return carry

        lax.fori_loop(0, jnp.where(gives, 0, relayed), drain_relay, 0)

    for m in range(PARTS):
        back_finish(m)
    leaving[2].start()

    for m in range(PARTS):
        steps(half, lambda step, m=m: back_copy(m, step).wait_send())
        mate_copy(2 + m, scores_both.at[m]).wait_send()
    for copy in leaving:
        copy.wait()


def upsample_taps():
    pixels = np.arange(BLK, dtype=np.float32)
    source = np.clip((pixels + 0.5) / 8.0 - 0.5, 0.0, CELLS - 1.0)
    table = np.maximum(1.0 - np.abs(source[:, None] - np.arange(CELLS, dtype=np.float32)[None, :]), 0.0)
    moved = []
    for i in (-1, 0, 1):
        shifted = np.zeros_like(table)
        for p in range(BLK):
            if 0 <= p + i < BLK:
                shifted[p] = table[p + i]
        moved.append(shifted)
    moved = np.stack(moved)
    table = np.einsum("ipa,jqb->pqijab", moved, moved).reshape(BLK * BLK, 9 * CELLS * CELLS)
    return np.pad(table, ((0, 0), (COLOR_ROWS, 0)))


def pyramid(tiles, rows, cols, features, image, blocks, routes, w_one, w_rates, w_depth, w_pool, w_proj,
            w_first, w_color, w_second, w_head):
    channels, width = w_one.shape
    cells = rows * cols
    per = CAP * CELLS * CELLS
    chunks = channels // CHUNK
    edge = REACH * cols
    places = routes.shape[0] // tiles
    classes = w_head.shape[0]
    pixels = BLK * BLK
    item = places * classes * QUARTERS
    low_count = tiles // (2 * HIGH)
    part = pixels // (PARTS * QUARTERS)
    away = pl.BlockSpec(memory_space=pl.ANY)
    dma = pltpu.SemaphoreType.DMA
    image = image.transpose(0, 2, 1).reshape(-1, image.shape[1])
    first, second = w_first.reshape(9 * width, width), w_second.reshape(9 * width, width)
    operands = (
        features.reshape(cells, channels), w_one, w_rates, w_depth.transpose(1, 0, 2), w_pool, w_proj, image, first, second,
        w_color, w_head, jnp.asarray(upsample_taps(), BF16), blocks.T, routes.T,
    )

    links = low_count + HIGH
    half = tiles // 2
    return pl.pallas_call(
        functools.partial(pyramid_kernel, tiles, rows, cols, channels, width),
        out_shape=(
            jax.ShapeDtypeStruct((cells, width), BF16),
            jax.ShapeDtypeStruct((1, width), F32),
            jax.ShapeDtypeStruct((classes, places, pixels), BF16),
        ),
        in_specs=[away] * len(operands),
        out_specs=(away, away, away),
        scratch_shapes=[
            pltpu.VMEM((cells, width), BF16),
            pltpu.VMEM((1, width), F32),
            pltpu.VMEM((classes, places, pixels), BF16),
            dma((3,)),
            *(pltpu.VMEM(operand.shape, operand.dtype) for operand in operands),
            pltpu.VMEM((2, edge, channels), BF16),
            pltpu.VMEM((cells + 2 * edge, CHUNK), F32),
            pltpu.VMEM((3, cells, channels), BF16),
            pltpu.VMEM((4, cells, width), F32),
            pltpu.VMEM((3, 1, channels), F32),
            pltpu.VMEM((links - 1, 1, channels), F32),
            pltpu.VMEM((32, pixels), F32),
            pltpu.VMEM((128, cells), BF16),
            pltpu.VMEM((half * per, 256), BF16),
            pltpu.VMEM((half * item, 256), BF16),
            pltpu.VMEM((16, pixels), F32),
            pltpu.VMEM((1, width), F32),
            pltpu.VMEM((CAP, COLOR_ROWS + 144, width), BF16),
            pltpu.VMEM((CAP, pixels + 2 * BLK, 3 * width), BF16),
            pltpu.VMEM((PARTS, QUARTERS * CAP * 8, part), F32),
            pltpu.VMEM((2, 32, pixels), BF16),
            pltpu.VMEM((half * 16, pixels), BF16),
            pltpu.VMEM((HIGH - 1, low_count * 16, pixels), BF16),
            pltpu.VMEM((low_count - 1, 16, pixels), BF16),
            pltpu.VMEM((2, 128, width), BF16),
            pltpu.VMEM((half * per, width), BF16),
            pltpu.VMEM((CAP, half - 1, 16, width), BF16),
            pltpu.VMEM((PARTS, 2, QUARTERS * CAP * 8, part), BF16),
            pltpu.VMEM((PARTS, half * item, part), BF16),
            pltpu.VMEM((PARTS, half - 1, item, part), BF16),
            dma((len(operands),)),
            dma((2, chunks)),
            dma((2, chunks)),
            *(dma((links,)) for _ in range(4)),
            *(dma((CAP, half)) for _ in range(2)),
            *(dma((PARTS, half)) for _ in range(2)),
            *(dma((2 + PARTS,)) for _ in range(2)),
            pltpu.VMEM((2 * HIGH - 1, edge, CHUNK), BF16),
            *(dma((2 * HIGH - 1,)) for _ in range(2)),
        ],
        compiler_params=pltpu.CompilerParams(collective_id=0, has_side_effects=True, vmem_limit_bytes=60 << 20),
        name="pyramid",
    )(*operands)


def settle_kernel(*refs):
    half = len(refs) // 2
    for source, target in zip(refs[:half], refs[half:]):
        target[...] = source[...]


def settle(*arrays):
    return pl.pallas_call(
        settle_kernel,
        out_shape=tuple(jax.ShapeDtypeStruct(a.shape, a.dtype) for a in arrays),
        name="settle",
    )(*arrays)


def shards(
    tiles,
    features,
    aerial_image,
    blocks,
    routes,
    w_one,
    w_depth,
    w_rates,
    w_pool,
    w_proj,
    w_first,
    w_color,
    w_second,
    w_head,
):
    rows, cols, channels = features.shape
    width = w_one.shape[1]
    aspp, context, refined = pyramid(
        tiles, rows, cols, features, aerial_image, blocks, routes, w_one, w_rates, w_depth, w_pool, w_proj,
        w_first[0], w_color[0], w_second[0], w_head[0],
    )
    aspp, context, refined = settle(aspp, context, refined)
    return aspp.reshape(rows, cols, width), context.reshape(width), refined.transpose(1, 0, 2)


def solution(mesh):
    return jax.shard_map(
        functools.partial(shards, mesh.shape["tile"]),
        mesh=mesh,
        in_specs=(
            P(("groups", "tile"), None, None),
            P(None, ("groups", "tile"), None),
            P("groups", None),
            P("groups", None),
            P(),
            P(),
            P(),
            P(),
            P(),
            P("tile", None, None, None),
            P("tile", None, None),
            P("tile", None, None, None),
            P("tile", None, None),
        ),
        out_specs=(
            P(("groups", "tile"), None, None),
            P("groups"),
            P(("groups", "tile"), None, None),
        ),
        check_vma=False,
    )
```

```python
import functools

import jax
import jax.numpy as jnp
import numpy as np
from jax import lax
from jax.experimental import pallas as pl
from jax.experimental.pallas import tpu as pltpu
from jax.sharding import PartitionSpec as P

BLK = 32
CAP = 4
CELLS = 4
RATES = (6, 12, 18)
REACH = 18
CHUNK = 256
HIGH = 4
QUARTERS = 4
COLOR_ROWS = 112
AHEAD = 4
RELAY_AHEAD = 6
PARTS = 2
OWN = 6
F32 = jnp.float32
BF16 = jnp.bfloat16


def split_three(value):
    high = value.astype(BF16)
    rest = value - high.astype(F32)
    mid = rest.astype(BF16)
    low = (rest - mid.astype(F32)).astype(BF16)
    return high, mid, low


def exact_row_dot(row, weights):
    high, mid, low = split_three(row)
    stacked = jnp.concatenate(
        [high.astype(F32), mid.astype(F32), low.astype(F32), jnp.zeros((13, row.shape[1]), F32)], axis=0
    ).astype(BF16)
    product = jnp.dot(stacked, weights, preferred_element_type=F32)
    return product[0:1] + product[1:2] + product[2:3]


def pyramid_kernel(
    tiles, rows, cols, channels, width,
    feat_hbm, w_one_hbm, w_rates_hbm, w_depth_hbm, w_pool_hbm, w_proj_hbm, image_hbm, first_hbm, second_hbm,
    color_hbm, head_hbm, table_hbm, blocks_hbm, routes_hbm,
    aspp_hbm, context_hbm, refined_hbm,
    aspp_ref, context_ref, refined_ref, out_sem,
    feat, w_one, w_rates, w_depth_ref, w_pool, w_proj, image, first, second, color_ref, head_ref, table_ref, blocks_ref, routes_ref,
    halo, grown, depth, acc, sums, sums_in, own_colors, own_pick, crop_pick, back_pick, mine_ref, offset_ref,
    taps_ref, grids, scores,
    colors_both, colors_out, colors_high, colors_low, crops_both, crops_out, crops_in, scores_both, back_out, back_in,
    local_sem, halo_send, halo_recv, sum_send, sum_recv, color_send, color_recv, crop_send, crop_recv, back_send, back_recv,
    mate_send, mate_recv, relay, relay_send, relay_recv,
):
    me = lax.axis_index("tile")
    chunks = channels // CHUNK
    edge = REACH * cols
    cells = rows * cols
    count = routes_ref.shape[1]
    classes = head_ref.shape[0]
    half, low_count = tiles // 2, tiles // (2 * HIGH)
    core = lax.rem(me, 2)
    low = lax.rem(me // 2, low_count)
    high = me // (2 * low_count)
    chip = me // 2

    local = [
        pltpu.make_async_copy(source, target, local_sem.at[n])
        for n, (source, target) in enumerate(
            ((feat_hbm, feat), (blocks_hbm, blocks_ref), (routes_hbm, routes_ref), (w_one_hbm, w_one), (image_hbm, image),
             (w_depth_hbm, w_depth_ref), (w_rates_hbm, w_rates), (w_pool_hbm, w_pool), (w_proj_hbm, w_proj),
             (color_hbm, color_ref), (head_hbm, head_ref), (table_hbm, table_ref), (first_hbm, first), (second_hbm, second))
        )
    ]
    for copy in local:
        copy.start()

    mate = me + 1 - 2 * core

    def low_peer(step):
        return (high * low_count + lax.rem(low + step, low_count)) * 2 + core

    def high_peer(step):
        return (lax.rem(high + step, HIGH) * low_count + low) * 2 + core

    has_next = me < tiles - 1
    has_prev = me > 0
    barrier = pltpu.get_barrier_semaphore()

    def greet(peer):
        pl.semaphore_signal(barrier, inc=1, device_id={"tile": peer}, device_id_type=pl.DeviceIdType.MESH)

    def chip_peer(step):
        return lax.rem(chip + step, half) * 2 + core

    def greet_chip(step, carry):
        greet(chip_peer(step))
        return carry

    outward = jnp.where(core == 1, me + 1, me - 1)
    has_outward = (outward >= 0) & (outward < tiles)

    slanted = jnp.where(core == 1, me + 3, me - 3)
    has_slanted = (slanted >= 0) & (slanted < tiles) if low_count == 2 else False
    forward = jnp.where(high < HIGH - 1, 2 * (HIGH - 1 - high) + 1, 0)
    relayed = jnp.where(core == 1, forward, 2 * high) if low_count == 2 else 0
    gives = low == core
    first_relayed = chunks - relayed

    @pl.when(has_outward)
    def _():
        greet(outward)

    if low_count == 2:
        @pl.when(has_slanted)
        def _():
            greet(slanted)

    greet(mate)
    lax.fori_loop(1, half, greet_chip, 0)
    local[0].wait()

    def sum_rows(n, totals):
        block = feat[pl.ds(pl.multiple_of(n * 16, 16), 16), :].astype(F32)
        return totals + block[0:8] + block[8:16]

    totals = lax.fori_loop(0, cells // 16, sum_rows, jnp.zeros((8, channels), F32))
    sums[0] = jnp.sum(totals, axis=0, keepdims=True)

    expected = half + has_outward.astype(jnp.int32)
    pl.semaphore_wait(barrier, expected + has_slanted.astype(jnp.int32) if low_count == 2 else expected)

    def send(source, target, send_sem, recv_sem, peer):
        return pltpu.make_async_remote_copy(
            src_ref=source, dst_ref=target, send_sem=send_sem, recv_sem=recv_sem,
            device_id={"tile": peer}, device_id_type=pl.DeviceIdType.MESH,
        )

    def halo_copy(side, c):
        lanes = pl.ds(pl.multiple_of(c * CHUNK, CHUNK), CHUNK)
        return send(
            feat_hbm.at[pl.ds(cells - edge if side == 0 else 0, edge), lanes], halo.at[side, :, lanes],
            halo_send.at[side, c], halo_recv.at[side, c],
            lax.rem(me + 1, tiles) if side == 0 else lax.rem(me + tiles - 1, tiles),
        )

    def relay_copy(side, c):
        lanes = pl.ds(pl.multiple_of(c * CHUNK, CHUNK), CHUNK)
        return send(
            feat_hbm.at[pl.ds(cells - edge if side == 0 else 0, edge), lanes], relay.at[c - first_relayed],
            halo_send.at[side, c], relay_recv.at[c - first_relayed], low_peer(1),
        )

    def pass_copy(side, c):
        lanes = pl.ds(pl.multiple_of(c * CHUNK, CHUNK), CHUNK)
        slot = c - first_relayed
        return send(relay.at[slot], halo.at[side, :, lanes], relay_send.at[slot], halo_recv.at[side, c], slanted)

    def relays(side, c):
        return (core == 1 - side) & gives & (c >= first_relayed)

    def send_direct(c):
        for side, present in ((0, has_next), (1, has_prev)):
            if low_count == 2:
                present = present & jnp.logical_not(relays(side, c))

            @pl.when(present)
            def _(side=side):
                halo_copy(side, c).start()

    def send_relay(c):
        if low_count == 2:
            for side in range(2):
                @pl.when(relays(side, c))
                def _(side=side):
                    relay_copy(side, c).start()

    def pass_halo(c):
        if low_count == 2:
            for side in range(2):
                @pl.when((core == 1 - side) & jnp.logical_not(gives) & (c >= first_relayed) & (c < chunks))
                def _(side=side):
                    relay_copy(side, c).wait_recv()
                    pass_copy(side, c).start()

    def steps(number, function):
        def body(step, carry):
            function(step)
            return carry

        lax.fori_loop(1, number, body, 0)

    def mate_copy(number, both):
        return send(both.at[core], both.at[core], mate_send.at[number], mate_recv.at[number], mate)

    def color_high(step):
        rows_of = pl.ds(pl.multiple_of(lax.rem(high + step, HIGH) * (low_count * 16), 16), low_count * 16)
        return send(colors_out.at[rows_of], colors_high.at[step - 1], color_send.at[step], color_recv.at[step], high_peer(step))

    def color_low(step):
        rows_of = pl.ds(pl.multiple_of((high * low_count + lax.rem(low + step, low_count)) * 16, 16), 16)
        slot = HIGH + step
        return send(colors_out.at[rows_of], colors_low.at[step - 1], color_send.at[slot], color_recv.at[slot], low_peer(step))

    def crop_rows(block, to_chip):
        return pl.ds(pl.multiple_of((block * half + to_chip) * 16, 16), 16)

    def crop_copy(block, step):
        return send(
            crops_out.at[crop_rows(block, lax.rem(chip + step, half))], crops_in.at[block, step - 1],
            crop_send.at[block, step], crop_recv.at[block, step], chip_peer(step),
        )

    item = back_pick.shape[0] // half

    def back_rows(to_chip):
        return pl.ds(pl.multiple_of(to_chip * item, 16), item)

    def back_copy(m, step):
        return send(
            back_out.at[m, back_rows(lax.rem(chip + step, half))], back_in.at[m, step - 1],
            back_send.at[m, step], back_recv.at[m, step], chip_peer(step),
        )

    def sum_low(step):
        return send(sums.at[0], sums_in.at[step - 1], sum_send.at[step], sum_recv.at[step], low_peer(step))

    def sum_high(step):
        slot = low_count + step
        return send(sums.at[1], sums_in.at[slot - 2], sum_send.at[slot], sum_recv.at[slot], high_peer(step))

    def sum_mate():
        return send(sums.at[2], sums_in.at[low_count + HIGH - 2], sum_send.at[0], sum_recv.at[0], mate)

    def add_sums(start, number, total):
        return lax.fori_loop(0, number, lambda n, value: value + sums_in[start + n], total)

    steps(low_count, lambda step: sum_low(step).start())
    send_direct(0)
    for c in range(1, AHEAD):
        send_direct(c)
    for c in range(RELAY_AHEAD):
        send_relay(c)

    tall = 768
    local[3].wait()

    @pl.loop(0, cells // tall)
    def _(m):
        span = pl.ds(pl.multiple_of(m * tall, tall), tall)
        acc[0, span, :] = jnp.dot(feat[span, :], w_one[...], preferred_element_type=F32)

    @pl.when(jnp.logical_not(has_prev))
    def _():
        grown[0:edge, :] = jnp.zeros((edge, CHUNK), F32)

    @pl.when(jnp.logical_not(has_next))
    def _():
        grown[edge + cells :, :] = jnp.zeros((edge, CHUNK), F32)

    def widen(source, start, count, lanes):
        @pl.loop(0, count // 48)
        def _(n):
            grown[pl.ds(pl.multiple_of(start + n * 48, 8), 48), :] = source[
                pl.ds(pl.multiple_of(n * 48, 16), 48), lanes
            ].astype(F32)

    local[1].wait()
    local[2].wait()
    experts = routes_ref[...].astype(F32)
    square = (count, count)
    down, over = lax.broadcasted_iota(jnp.int32, square, 0), lax.broadcasted_iota(jnp.int32, square, 1)
    spread = jnp.broadcast_to(experts, square)

    def stand(row):
        return jnp.sum(jnp.where(down == over, jnp.broadcast_to(row, square), 0.0), axis=1, keepdims=True)

    upright = stand(experts)
    rank = jnp.sum(jnp.where((upright == spread) & (down < over), 1.0, 0.0), axis=0, keepdims=True)
    strip_blocks = rows // CELLS
    block_row, block_col = blocks_ref[0:1, :].astype(F32), blocks_ref[1:2, :].astype(F32)
    strip_row = (blocks_ref[0:1, :] // strip_blocks).astype(F32)
    strip_col = stand(strip_row)
    beside = jnp.broadcast_to(strip_row, square) == strip_col
    first_strip = lax.convert_element_type(chip * 2, F32)

    def listed_at(strip, place):
        within = strip - first_strip
        return jnp.where((within >= 0) & (within < 2), within * 8 + place, -1.0)

    own_row_index = listed_at(strip_row, jnp.sum(jnp.where(beside & (down < over), 1.0, 0.0), axis=0, keepdims=True))
    own_col_index = listed_at(strip_col, jnp.sum(jnp.where(beside & (over < down), 1.0, 0.0), axis=1, keepdims=True))
    slot_col = upright * CAP + jnp.sum(jnp.where((upright == spread) & (over < down), 1.0, 0.0), axis=1, keepdims=True)
    local_row = block_row - lax.convert_element_type(me * strip_blocks, F32)

    def own_values(index, values):
        shape = (index.shape[0], count)
        hit = jnp.broadcast_to(own_row_index, shape) == (index + core * 8).astype(F32)
        return jnp.max(jnp.where(hit, jnp.broadcast_to(values, shape), -1e6), axis=1, keepdims=True)

    own_row = lax.broadcasted_iota(jnp.int32, (128, 1), 0)
    own_base = own_values(own_row >> 4, local_row * (CELLS * cols) + block_col * CELLS)
    wanted_cell = own_base + (((own_row >> 2) & 3) * cols + (own_row & 3)).astype(F32)
    cell_at = lax.broadcasted_iota(jnp.int32, (128, cells), 1).astype(F32)
    own_pick[...] = (cell_at == wanted_cell).astype(F32).astype(BF16)

    own_lane = lax.broadcasted_iota(jnp.int32, (1, 256), 1)

    def own_slots(index):
        hit = own_col_index == index.astype(F32)
        return jnp.max(jnp.where(hit, jnp.broadcast_to(slot_col, (count, 256)), -1.0), axis=0, keepdims=True)

    own_slot = own_slots(own_lane >> 4)
    @pl.loop(0, CAP * half // 8)
    def _(n):
        row = lax.broadcasted_iota(jnp.int32, (128, 1), 0) + n * 128
        index = row >> 4
        tile = (index % half) * 2 + core
        hit = (own_slot == (tile * CAP + index // half).astype(F32)) & ((own_lane & 15) == (row & 15))
        crop_pick[pl.ds(pl.multiple_of(n * 128, 128), 128), :] = hit.astype(F32).astype(BF16)

    def to_expert(expert):
        return jnp.where(experts == lax.convert_element_type(expert, F32), rank, -1.0)

    to_first, to_second = to_expert(2 * chip), to_expert(2 * chip + 1)

    @pl.loop(0, half)
    def _(n):
        tile = n * 2 + core
        span = item // QUARTERS
        line = lax.broadcasted_iota(jnp.int32, (item, 1), 0)
        quarter = sum((line >= q * span).astype(jnp.int32) for q in range(1, QUARTERS))
        line = line - quarter * span
        place = sum((line >= p * classes).astype(jnp.int32) for p in range(1, span // classes)) + jnp.zeros_like(line)
        kind = line - place * classes
        listed = lax.broadcasted_iota(jnp.int32, (item, count), 1)
        wanted = listed == tile * (span // classes) + place
        given = lax.broadcasted_iota(jnp.int32, (item, 128), 1)
        right_place = ((given & 7) == kind) & ((given >> 5) == quarter)
        for s, values in enumerate((to_first, to_second)):
            slot = jnp.max(jnp.where(wanted, jnp.broadcast_to(values, (item, count)), -1.0), axis=1, keepdims=True)
            pick = (((given >> 3) & 3).astype(F32) == slot) & right_place
            back_pick[back_rows(n), s * 128 : s * 128 + 128] = pick.astype(F32).astype(BF16)

    steps(low_count, lambda step: sum_low(step).wait_recv())
    sums[1] = add_sums(0, low_count - 1, sums[0])
    steps(HIGH, lambda step: sum_high(step).start())

    local[4].wait()
    parts_high = image.shape[0]
    across = parts_high // 3
    group = 2 * 3 * BLK
    line = lax.broadcasted_iota(jnp.int32, (group, 1), 0)
    line_own = (line >= 3 * BLK).astype(jnp.int32)
    line_channel = (line - line_own * (3 * BLK)) // BLK
    lane = lax.broadcasted_iota(jnp.int32, (1, BLK * BLK), 1)
    source = lax.broadcasted_iota(jnp.int32, (1, parts_high), 1).astype(F32)
    keep = (line & (BLK - 1)) == (lane & (BLK - 1))
    tall_rows = image.shape[1]
    image_row = lax.broadcasted_iota(jnp.int32, (tall_rows, 1), 0)
    image_lane = (lax.broadcasted_iota(jnp.int32, (1, tall_rows), 1) // BLK).astype(F32)
    fold = ((image_row & (BLK - 1)) == (lane >> 5)).astype(F32).astype(BF16)
    own_colors[...] = jnp.zeros(own_colors.shape, F32)

    for n in range(OWN // 2):
        index = line_own + 2 * n
        at = own_values(index, local_row)
        wanted = own_values(index, block_col) * BLK + (line_channel * across + (line & (BLK - 1))).astype(F32)
        chosen = (source == wanted).astype(F32).astype(BF16)
        columns = jnp.dot(chosen, image[...], preferred_element_type=F32)
        columns = jnp.where(image_lane == at, columns, 0.0).astype(BF16)
        strips = jnp.where(keep, jnp.dot(columns, fold, preferred_element_type=F32), 0.0)
        for p in range(6):
            to = (2 * n + p // 3) * 4 + p % 3
            own_colors[to : to + 1, :] = jnp.sum(strips[p * BLK : (p + 1) * BLK], axis=0, keepdims=True)

    colors_both[core] = own_colors[...].astype(BF16)
    mate_copy(0, colors_both).start()

    local[5].wait()
    local[6].wait()

    def one_chunk(c, carry):
        @pl.when(c < chunks - AHEAD)
        def _():
            send_direct(c + AHEAD)

        @pl.when(c < chunks - RELAY_AHEAD)
        def _():
            send_relay(c + RELAY_AHEAD)

        @pl.when(c == 2)
        def _():
            mate_copy(0, colors_both).wait_recv()
            lane_of = own_lane[:, 0:32]
            for s in range(2):
                lane_slot = own_slots((own_lane & 31) // 4 + 8 * s)[:, 0:32]

                @pl.loop(0, half)
                def _(n, s=s, lane_slot=lane_slot):
                    row = lax.broadcasted_iota(jnp.int32, (16, 1), 0)
                    hit = (lane_slot == ((n * 2 + core) * CAP + (row >> 2)).astype(F32)) & ((lane_of & 3) == (row & 3))
                    found = jnp.dot(hit.astype(F32).astype(BF16), colors_both[s], preferred_element_type=F32)
                    rows_of = pl.ds(pl.multiple_of(n * 16, 16), 16)
                    if s == 0:
                        colors_out[rows_of, :] = found.astype(BF16)
                    else:
                        colors_out[rows_of, :] = (colors_out[rows_of, :].astype(F32) + found).astype(BF16)

            steps(HIGH, lambda step: color_high(step).start())

        @pl.when(c == 1)
        def _():
            steps(HIGH, lambda step: sum_high(step).wait_recv())
            sums[2] = add_sums(low_count - 1, HIGH - 1, sums[1])
            sum_mate().start()

        @pl.when(c == 3)
        def _():
            sum_mate().wait_recv()
            local[7].wait()
            local[8].wait()
            pooled = add_sums(low_count + HIGH - 2, 1, sums[2]) / (cells * tiles)
            context = jnp.maximum(exact_row_dot(pooled, w_pool[...]), 0.0)
            context_ref[...] = context
            offset_ref[...] = exact_row_dot(context, w_proj[4 * width :, :])

        @pl.when(c == chunks - 2)
        def _():
            steps(HIGH, lambda step: color_high(step).wait_recv())
            rows_of = pl.ds(pl.multiple_of(high * (low_count * 16), 16), low_count * 16)

            def add(n, total):
                return total + colors_high[n].astype(F32)

            colors_out[rows_of, :] = lax.fori_loop(0, HIGH - 1, add, colors_out[rows_of, :].astype(F32)).astype(BF16)
            steps(low_count, lambda step: color_low(step).start())

        @pl.when(c == chunks - 3)
        def _():
            @pl.loop(0, cells // tall)
            def _(m):
                span = pl.ds(pl.multiple_of(m * tall, tall), tall)
                branch = jnp.maximum(acc[0, span, :], 0.0).astype(BF16)
                acc[0, span, :] = offset_ref[...] + jnp.dot(branch, w_proj[0:width, :], preferred_element_type=F32)

        for at, (start, stop) in (
            (chunks // 2, (0, chunks // 2)), (chunks - 2, (chunks // 2, chunks - 2)), (chunks - 1, (chunks - 2, chunks - 1))
        ):
            @pl.when(c == at)
            def _(start=start * CHUNK, stop=stop * CHUNK):
                for k in range(3):
                    @pl.loop(0, cells // tall)
                    def _(m, k=k):
                        span = pl.ds(pl.multiple_of(m * tall, tall), tall)
                        part = jnp.dot(depth[k, span, start:stop], w_rates[k, start:stop, :], preferred_element_type=F32)
                        acc[k + 1, span, :] = part if start == 0 else acc[k + 1, span, :] + part

        lanes = pl.ds(pl.multiple_of(c * CHUNK, CHUNK), CHUNK)
        widen(feat, edge, cells, lanes)

        def take(side, present):
            @pl.when(present)
            def _():
                halo_copy(side, c).wait_recv()
                widen(halo.at[side], 0 if side == 0 else edge + cells, edge, lanes)

        def map_rows(late):
            for part in range(CHUNK // 128):
                inner = slice(part * 128, part * 128 + 128)
                outer = pl.ds(pl.multiple_of(c * CHUNK + part * 128, 128), 128)
                for k, d in enumerate(RATES):
                    taps = [
                        jnp.broadcast_to(w_depth_ref[t, k : k + 1, outer].astype(F32), (8, 128)) for t in range(9)
                    ]

                    def weigh(parts, column, taps=taps):
                        total = None
                        for i in range(3):
                            tap = jnp.concatenate([taps[3 * i + column]] * (parts[i].shape[0] // 8), axis=0)
                            term = parts[i] * tap
                            total = term if total is None else total + term
                        return total

                    def two_rows(pair, d=d, weigh=weigh, inner=inner, outer=outer, k=k):
                        results = []
                        for r in range(2):
                            parts = []
                            for i in (-1, 0, 1):
                                start = pl.multiple_of((REACH + i * d + r) * cols + pair * (2 * cols), 8)
                                parts.append(grown[pl.ds(start, cols), inner])
                            low = -(-(cols - d) // 8) * 8
                            high = (d // 8) * 8
                            middle = weigh(parts, 1)
                            left = weigh([p[:low] for p in parts], 0)
                            right = weigh([p[high:] for p in parts], 2)
                            fill = jnp.zeros((d, 128), F32)
                            left = jnp.concatenate([fill, left[: cols - d]], axis=0)
                            right = jnp.concatenate([right[d - high :], fill], axis=0)
                            results.append(jnp.maximum(middle + left + right, 0.0))
                        depth[k, pl.ds(pl.multiple_of(pair * (2 * cols), 16), 2 * cols), outer] = jnp.concatenate(
                            results, axis=0
                        ).astype(BF16)

                    pairs = d // 2 if late else (rows - d) // 2
                    after = core == 1 if late else core == 0
                    first_pair = jnp.where(after, rows // 2 - pairs, 0)
                    unroll = max(u for u in (3, 4, 5) if pairs % u == 0 or pairs % u == 1)
                    for n in range(pairs % unroll):
                        two_rows(first_pair + n)
                    first_pair += pairs % unroll

                    @pl.loop(0, pairs // unroll)
                    def _(n, two_rows=two_rows, first_pair=first_pair, unroll=unroll):
                        for u in range(unroll):
                            two_rows(first_pair + n * unroll + u)

        take(1, has_next & (core == 0))
        take(0, has_prev & (core == 1))
        map_rows(False)
        pass_halo(c + 1)
        take(0, has_prev & (core == 0))
        take(1, has_next & (core == 1))
        map_rows(True)
        return carry

    lax.fori_loop(0, chunks, one_chunk, 0)

    @pl.loop(0, cells // tall)
    def _(m):
        span = pl.ds(pl.multiple_of(m * tall, tall), tall)
        blended = acc[0, span, :]
        for k in range(1, 4):
            branch = acc[k, span, :] + jnp.dot(
                depth[k - 1, span, channels - CHUNK :], w_rates[k - 1, channels - CHUNK :, :], preferred_element_type=F32
            )
            branch = jnp.maximum(branch, 0.0).astype(BF16)
            blended += jnp.dot(branch, w_proj[k * width : (k + 1) * width, :], preferred_element_type=F32)
        aspp_ref[span, :] = jnp.maximum(blended, 0.0).astype(BF16)

    leaving = [
        pltpu.make_async_copy(source, target, out_sem.at[n])
        for n, (source, target) in enumerate(((aspp_ref, aspp_hbm), (context_ref, context_hbm), (refined_ref, refined_hbm)))
    ]
    leaving[0].start()
    leaving[1].start()
    crops_both[core] = jnp.dot(own_pick[...], aspp_ref[...], preferred_element_type=F32).astype(BF16)
    mate_copy(1, crops_both).start()
    steps(low_count, lambda step: color_low(step).wait_recv())

    def add_low(n, total):
        return total + colors_low[n].astype(F32)

    mine_ref[...] = lax.fori_loop(
        0, low_count - 1, add_low, colors_out[pl.ds(pl.multiple_of(chip * 16, 16), 16), :].astype(F32)
    )
    side, pixels = BLK, BLK * BLK
    wide = lax.broadcasted_iota(jnp.int32, (3 * CAP, pixels), 1)
    row_at, col_at = wide >> 5, wide & (side - 1)
    received = mine_ref[...]
    colors = jnp.concatenate([received[4 * n : 4 * n + 3] for n in range(CAP)], axis=0)
    local[11].wait()
    pieces = []
    for i in (-1, 0, 1):
        for j in (-1, 0, 1):
            moved = colors if i == 0 and j == 0 else pltpu.roll(colors, (-(side * i + j)) % pixels, 1)
            inside = (row_at + i >= 0) & (row_at + i < side) & (col_at + j >= 0) & (col_at + j < side)
            pieces.append(jnp.where(inside, moved, 0.0))
    pieces.append(jnp.zeros((128 - 9 * 3 * CAP, pixels), F32))
    spread_colors = jnp.concatenate(pieces, axis=0).T.astype(BF16)
    table_ref[:, 0:128] = (table_ref[:, 0:128].astype(F32) + spread_colors.astype(F32)).astype(BF16)

    mate_copy(1, crops_both).wait_recv()

    @pl.loop(0, CAP)
    def _(block):
        @pl.loop(0, half // 8)
        def _(n):
            rows_of = pl.ds(pl.multiple_of((block * (half // 8) + n) * 128, 128), 128)
            found = jnp.dot(crop_pick[rows_of, :], crops_both[...].reshape(256, width), preferred_element_type=F32)
            crops_out[rows_of, :] = found.astype(BF16)

        steps(half, lambda step: crop_copy(block, step).start())

    blank = jnp.zeros((side, 3 * width), BF16)
    for block in range(CAP):
        grids[block, 0:side, :] = blank
        grids[block, side + pixels :, :] = blank
    for n in (9, 10, 12, 13):
        local[n].wait()
    tap_row = lax.broadcasted_iota(jnp.int32, (COLOR_ROWS, 27), 0)
    pixel_tap = lax.broadcasted_iota(jnp.int32, (COLOR_ROWS, 27), 1)
    tap_of = sum((pixel_tap >= 3 * n).astype(jnp.int32) for n in range(1, 9))
    for block in range(CAP):
        wanted = tap_of * (3 * CAP) + 3 * block + pixel_tap - 3 * tap_of
        spread_taps = (tap_row == wanted).astype(F32).astype(BF16)
        taps_ref[block, 0:COLOR_ROWS, :] = jnp.dot(spread_taps, color_ref[...], preferred_element_type=F32).astype(BF16)
    scores[...] = jnp.zeros(scores.shape, F32)
    tall = pixels // PARTS
    col = lax.broadcasted_iota(jnp.int32, (pixels, width), 0) & (side - 1)

    def open_block(block):
        steps(half, lambda step: crop_copy(block, step).wait_recv())

        def add_crop(n, total):
            return total + crops_in[block, n].astype(F32)

        crop = lax.fori_loop(0, half - 1, add_crop, crops_out[crop_rows(block, chip), :].astype(F32)).astype(BF16)
        for tap in range(9):
            part = jnp.dot(crop, first[tap * width : (tap + 1) * width, :], preferred_element_type=F32)
            taps_ref[block, COLOR_ROWS + tap * 16 : COLOR_ROWS + tap * 16 + 16, :] = part.astype(BF16)

    def first_conv(block):
        total = jnp.dot(table_ref[...], taps_ref[block], preferred_element_type=F32)
        total = jnp.maximum(total, 0.0)
        before = jnp.where(col == 0, 0.0, pltpu.roll(total, 1, 0))
        after = jnp.where(col == side - 1, 0.0, pltpu.roll(total, pixels - 1, 0))
        inner = slice(side, side + pixels)
        grids[block, inner, 0:width] = before.astype(BF16)
        grids[block, inner, width : 2 * width] = total.astype(BF16)
        grids[block, inner, 2 * width :] = after.astype(BF16)

    def second_conv(pair, m):
        at = m * tall
        total = None
        for i in range(3):
            rows_of = slice(at + side * i, at + side * i + tall)
            both = jnp.concatenate([grids[2 * pair, rows_of, :], grids[2 * pair + 1, rows_of, :]], axis=0)
            term = jnp.dot(both, second[3 * width * i : 3 * width * (i + 1), :], preferred_element_type=F32)
            total = term if total is None else total + term
        total = jnp.maximum(total, 0.0).astype(BF16)
        found = lax.dot_general(head_ref[...], total, (((1,), (1,)), ((), ())), preferred_element_type=F32)
        wide_part = tall // QUARTERS
        for b in range(2):
            for q in range(QUARTERS):
                start = pl.multiple_of(q * (8 * CAP) + (2 * pair + b) * 8, 8)
                left = b * tall + q * wide_part
                scores[m, pl.ds(start, classes), :] = found[:, left : left + wide_part]

    def back_swap(m):
        scores_both[m, core] = scores[m].astype(BF16)
        mate_copy(2 + m, scores_both.at[m]).start()

    def back_spread(m):
        mate_copy(2 + m, scores_both.at[m]).wait_recv()

        @pl.loop(0, half // 2)
        def _(n):
            rows_of = pl.ds(pl.multiple_of(n * (2 * item), 16), 2 * item)
            found = jnp.dot(back_pick[rows_of, 0:128], scores_both[m, 0], preferred_element_type=F32)
            found += jnp.dot(back_pick[rows_of, 128:256], scores_both[m, 1], preferred_element_type=F32)
            back_out[m, rows_of, :] = found.astype(BF16)
            for t in range(2):
                step = lax.rem(2 * n + t - chip + half, half)

                @pl.when(step > 0)
                def _(step=step):
                    back_copy(m, step).start()


    def back_finish(m):
        steps(half, lambda step: back_copy(m, step).wait_recv())

        def add_back(n, total):
            return total + back_in[m, n].astype(F32)

        result = lax.fori_loop(0, half - 1, add_back, back_out[m, back_rows(chip), :].astype(F32))
        span = item // QUARTERS
        wide_part = pixels // (PARTS * QUARTERS)
        for q in range(QUARTERS):
            for p in range(span // classes):
                start = q * span + p * classes
                left = (m * QUARTERS + q) * wide_part
                refined_ref[:, p, left : left + wide_part] = result[start : start + classes].astype(BF16)

    @pl.loop(0, CAP // 2)
    def _(pair):
        @pl.loop(0, 2)
        def _(n):
            open_block(2 * pair + n)
            first_conv(2 * pair + n)

        second_conv(pair, 0)

    for m in range(1, PARTS):
        back_swap(m - 1)
        second_conv(0, m)
        back_spread(m - 1)

        @pl.loop(1, CAP // 2)
        def _(pair, m=m):
            second_conv(pair, m)

    back_swap(PARTS - 1)
    back_spread(PARTS - 1)
    steps(low_count, lambda step: sum_low(step).wait_send())
    steps(HIGH, lambda step: sum_high(step).wait_send())
    sum_mate().wait_send()
    steps(HIGH, lambda step: color_high(step).wait_send())
    steps(low_count, lambda step: color_low(step).wait_send())
    for number, both in enumerate((colors_both, crops_both)):
        mate_copy(number, both).wait_send()

    def drain_crops(block, carry):
        steps(half, lambda step: crop_copy(block, step).wait_send())
        return carry

    lax.fori_loop(0, CAP, drain_crops, 0)

    def drain_halo(c, carry):
        @pl.when(has_next)
        def _():
            halo_copy(0, c).wait_send()

        @pl.when(has_prev)
        def _():
            halo_copy(1, c).wait_send()

        return carry

    lax.fori_loop(0, chunks, drain_halo, 0)
    if low_count == 2:
        def drain_relay(c, carry):
            pass_copy(0, first_relayed + c).wait_send()
            return carry

        lax.fori_loop(0, jnp.where(gives, 0, relayed), drain_relay, 0)

    for m in range(PARTS):
        back_finish(m)
    leaving[2].start()

    for m in range(PARTS):
        steps(half, lambda step, m=m: back_copy(m, step).wait_send())
        mate_copy(2 + m, scores_both.at[m]).wait_send()
    for copy in leaving:
        copy.wait()


def upsample_taps():
    pixels = np.arange(BLK, dtype=np.float32)
    source = np.clip((pixels + 0.5) / 8.0 - 0.5, 0.0, CELLS - 1.0)
    table = np.maximum(1.0 - np.abs(source[:, None] - np.arange(CELLS, dtype=np.float32)[None, :]), 0.0)
    moved = []
    for i in (-1, 0, 1):
        shifted = np.zeros_like(table)
        for p in range(BLK):
            if 0 <= p + i < BLK:
                shifted[p] = table[p + i]
        moved.append(shifted)
    moved = np.stack(moved)
    table = np.einsum("ipa,jqb->pqijab", moved, moved).reshape(BLK * BLK, 9 * CELLS * CELLS)
    return np.pad(table, ((0, 0), (COLOR_ROWS, 0)))


def pyramid(tiles, rows, cols, features, image, blocks, routes, w_one, w_rates, w_depth, w_pool, w_proj,
            w_first, w_color, w_second, w_head):
    channels, width = w_one.shape
    cells = rows * cols
    per = CAP * CELLS * CELLS
    chunks = channels // CHUNK
    edge = REACH * cols
    places = routes.shape[0] // tiles
    classes = w_head.shape[0]
    pixels = BLK * BLK
    item = places * classes * QUARTERS
    low_count = tiles // (2 * HIGH)
    part = pixels // (PARTS * QUARTERS)
    away = pl.BlockSpec(memory_space=pl.ANY)
    dma = pltpu.SemaphoreType.DMA
    image = image.transpose(0, 2, 1).reshape(-1, image.shape[1])
    first, second = w_first.reshape(9 * width, width), w_second.reshape(9 * width, width)
    operands = (
        features.reshape(cells, channels), w_one, w_rates, w_depth.transpose(1, 0, 2), w_pool, w_proj, image, first, second,
        w_color, w_head, jnp.asarray(upsample_taps(), BF16), blocks.T, routes.T,
    )

    links = low_count + HIGH
    half = tiles // 2
    return pl.pallas_call(
        functools.partial(pyramid_kernel, tiles, rows, cols, channels, width),
        out_shape=(
            jax.ShapeDtypeStruct((cells, width), BF16),
            jax.ShapeDtypeStruct((1, width), F32),
            jax.ShapeDtypeStruct((classes, places, pixels), BF16),
        ),
        in_specs=[away] * len(operands),
        out_specs=(away, away, away),
        scratch_shapes=[
            pltpu.VMEM((cells, width), BF16),
            pltpu.VMEM((1, width), F32),
            pltpu.VMEM((classes, places, pixels), BF16),
            dma((3,)),
            *(pltpu.VMEM(operand.shape, operand.dtype) for operand in operands),
            pltpu.VMEM((2, edge, channels), BF16),
            pltpu.VMEM((cells + 2 * edge, CHUNK), F32),
            pltpu.VMEM((3, cells, channels), BF16),
            pltpu.VMEM((4, cells, width), F32),
            pltpu.VMEM((3, 1, channels), F32),
            pltpu.VMEM((links - 1, 1, channels), F32),
            pltpu.VMEM((32, pixels), F32),
            pltpu.VMEM((128, cells), BF16),
            pltpu.VMEM((half * per, 256), BF16),
            pltpu.VMEM((half * item, 256), BF16),
            pltpu.VMEM((16, pixels), F32),
            pltpu.VMEM((1, width), F32),
            pltpu.VMEM((CAP, COLOR_ROWS + 144, width), BF16),
            pltpu.VMEM((CAP, pixels + 2 * BLK, 3 * width), BF16),
            pltpu.VMEM((PARTS, QUARTERS * CAP * 8, part), F32),
            pltpu.VMEM((2, 32, pixels), BF16),
            pltpu.VMEM((half * 16, pixels), BF16),
            pltpu.VMEM((HIGH - 1, low_count * 16, pixels), BF16),
            pltpu.VMEM((low_count - 1, 16, pixels), BF16),
            pltpu.VMEM((2, 128, width), BF16),
            pltpu.VMEM((half * per, width), BF16),
            pltpu.VMEM((CAP, half - 1, 16, width), BF16),
            pltpu.VMEM((PARTS, 2, QUARTERS * CAP * 8, part), BF16),
            pltpu.VMEM((PARTS, half * item, part), BF16),
            pltpu.VMEM((PARTS, half - 1, item, part), BF16),
            dma((len(operands),)),
            dma((2, chunks)),
            dma((2, chunks)),
            *(dma((links,)) for _ in range(4)),
            *(dma((CAP, half)) for _ in range(2)),
            *(dma((PARTS, half)) for _ in range(2)),
            *(dma((2 + PARTS,)) for _ in range(2)),
            pltpu.VMEM((2 * HIGH - 1, edge, CHUNK), BF16),
            *(dma((2 * HIGH - 1,)) for _ in range(2)),
        ],
        compiler_params=pltpu.CompilerParams(collective_id=0, has_side_effects=True, vmem_limit_bytes=60 << 20),
        name="pyramid",
    )(*operands)


def settle_kernel(*refs):
    half = len(refs) // 2
    for source, target in zip(refs[:half], refs[half:]):
        target[...] = source[...]


def settle(*arrays):
    return pl.pallas_call(
        settle_kernel,
        out_shape=tuple(jax.ShapeDtypeStruct(a.shape, a.dtype) for a in arrays),
        name="settle",
    )(*arrays)


def shards(
    tiles,
    features,
    aerial_image,
    blocks,
    routes,
    w_one,
    w_depth,
    w_rates,
    w_pool,
    w_proj,
    w_first,
    w_color,
    w_second,
    w_head,
):
    rows, cols, channels = features.shape
    width = w_one.shape[1]
    aspp, context, refined = pyramid(
        tiles, rows, cols, features, aerial_image, blocks, routes, w_one, w_rates, w_depth, w_pool, w_proj,
        w_first[0], w_color[0], w_second[0], w_head[0],
    )
    aspp, context, refined = settle(aspp, context, refined)
    return aspp.reshape(rows, cols, width), context.reshape(width), refined.transpose(1, 0, 2)


def solution(mesh):
    return jax.shard_map(
        functools.partial(shards, mesh.shape["tile"]),
        mesh=mesh,
        in_specs=(
            P(("groups", "tile"), None, None),
            P(None, ("groups", "tile"), None),
            P("groups", None),
            P("groups", None),
            P(),
            P(),
            P(),
            P(),
            P(),
            P("tile", None, None, None),
            P("tile", None, None),
            P("tile", None, None, None),
            P("tile", None, None),
        ),
        out_specs=(
            P(("groups", "tile"), None, None),
            P("groups"),
            P(("groups", "tile"), None, None),
        ),
        check_vma=False,
    )
```

```python
import functools

import jax
import jax.numpy as jnp
import numpy as np
from jax import lax
from jax.experimental import pallas as pl
from jax.experimental.pallas import tpu as pltpu
from jax.sharding import PartitionSpec as P

BLK = 32
CAP = 4
CELLS = 4
RATES = (6, 12, 18)
REACH = 18
CHUNK = 256
HIGH = 4
QUARTERS = 4
COLOR_ROWS = 112
AHEAD = 4
RELAY_AHEAD = 6
PARTS = 2
OWN = 6
F32 = jnp.float32
BF16 = jnp.bfloat16


def split_three(value):
    high = value.astype(BF16)
    rest = value - high.astype(F32)
    mid = rest.astype(BF16)
    low = (rest - mid.astype(F32)).astype(BF16)
    return high, mid, low


def exact_row_dot(row, weights):
    high, mid, low = split_three(row)
    stacked = jnp.concatenate(
        [high.astype(F32), mid.astype(F32), low.astype(F32), jnp.zeros((13, row.shape[1]), F32)], axis=0
    ).astype(BF16)
    product = jnp.dot(stacked, weights, preferred_element_type=F32)
    return product[0:1] + product[1:2] + product[2:3]


def pyramid_kernel(
    tiles, rows, cols, channels, width,
    feat_hbm, w_one_hbm, w_rates_hbm, w_depth_hbm, w_pool_hbm, w_proj_hbm, image_hbm, first_hbm, second_hbm,
    color_hbm, head_hbm, table_hbm, blocks_hbm, routes_hbm,
    aspp_hbm, context_hbm, refined_hbm,
    aspp_ref, context_ref, refined_ref, out_sem,
    feat, w_one, w_rates, w_depth_ref, w_pool, w_proj, image, first, second, color_ref, head_ref, table_ref, blocks_ref, routes_ref,
    halo, grown, depth, acc, sums, sums_in, own_colors, own_pick, crop_pick, back_pick, mine_ref, offset_ref,
    taps_ref, grids, scores,
    colors_both, colors_out, colors_high, colors_low, crops_both, crops_out, crops_in, scores_both, back_out, back_in,
    local_sem, halo_send, halo_recv, sum_send, sum_recv, color_send, color_recv, crop_send, crop_recv, back_send, back_recv,
    mate_send, mate_recv, relay, relay_send, relay_recv,
):
    me = lax.axis_index("tile")
    chunks = channels // CHUNK
    edge = REACH * cols
    cells = rows * cols
    count = routes_ref.shape[1]
    classes = head_ref.shape[0]
    half, low_count = tiles // 2, tiles // (2 * HIGH)
    core = lax.rem(me, 2)
    low = lax.rem(me // 2, low_count)
    high = me // (2 * low_count)
    chip = me // 2

    local = [
        pltpu.make_async_copy(source, target, local_sem.at[n])
        for n, (source, target) in enumerate(
            ((feat_hbm, feat), (blocks_hbm, blocks_ref), (routes_hbm, routes_ref), (w_one_hbm, w_one), (image_hbm, image),
             (w_depth_hbm, w_depth_ref), (w_rates_hbm, w_rates), (w_pool_hbm, w_pool), (w_proj_hbm, w_proj),
             (color_hbm, color_ref), (head_hbm, head_ref), (table_hbm, table_ref), (first_hbm, first), (second_hbm, second))
        )
    ]
    for copy in local:
        copy.start()

    mate = me + 1 - 2 * core

    def low_peer(step):
        return (high * low_count + lax.rem(low + step, low_count)) * 2 + core

    def high_peer(step):
        return (lax.rem(high + step, HIGH) * low_count + low) * 2 + core

    has_next = me < tiles - 1
    has_prev = me > 0
    barrier = pltpu.get_barrier_semaphore()

    def greet(peer):
        pl.semaphore_signal(barrier, inc=1, device_id={"tile": peer}, device_id_type=pl.DeviceIdType.MESH)

    def chip_peer(step):
        return lax.rem(chip + step, half) * 2 + core

    def greet_chip(step, carry):
        greet(chip_peer(step))
        return carry

    outward = jnp.where(core == 1, me + 1, me - 1)
    has_outward = (outward >= 0) & (outward < tiles)

    slanted = jnp.where(core == 1, me + 3, me - 3)
    has_slanted = (slanted >= 0) & (slanted < tiles) if low_count == 2 else False
    forward = jnp.where(high < HIGH - 1, 2 * (HIGH - 1 - high) + 1, 0)
    relayed = jnp.where(core == 1, forward, 2 * high) if low_count == 2 else 0
    gives = low == core
    first_relayed = chunks - relayed

    @pl.when(has_outward)
    def _():
        greet(outward)

    if low_count == 2:
        @pl.when(has_slanted)
        def _():
            greet(slanted)

    greet(mate)
    lax.fori_loop(1, half, greet_chip, 0)
    local[0].wait()

    def sum_rows(n, totals):
        block = feat[pl.ds(pl.multiple_of(n * 16, 16), 16), :].astype(F32)
        return totals + block[0:8] + block[8:16]

    totals = lax.fori_loop(0, cells // 16, sum_rows, jnp.zeros((8, channels), F32))
    sums[0] = jnp.sum(totals, axis=0, keepdims=True)

    expected = half + has_outward.astype(jnp.int32)
    pl.semaphore_wait(barrier, expected + has_slanted.astype(jnp.int32) if low_count == 2 else expected)

    def send(source, target, send_sem, recv_sem, peer):
        return pltpu.make_async_remote_copy(
            src_ref=source, dst_ref=target, send_sem=send_sem, recv_sem=recv_sem,
            device_id={"tile": peer}, device_id_type=pl.DeviceIdType.MESH,
        )

    def halo_copy(side, c):
        lanes = pl.ds(pl.multiple_of(c * CHUNK, CHUNK), CHUNK)
        return send(
            feat_hbm.at[pl.ds(cells - edge if side == 0 else 0, edge), lanes], halo.at[side, :, lanes],
            halo_send.at[side, c], halo_recv.at[side, c],
            lax.rem(me + 1, tiles) if side == 0 else lax.rem(me + tiles - 1, tiles),
        )

    def relay_copy(side, c):
        lanes = pl.ds(pl.multiple_of(c * CHUNK, CHUNK), CHUNK)
        return send(
            feat_hbm.at[pl.ds(cells - edge if side == 0 else 0, edge), lanes], relay.at[c - first_relayed],
            halo_send.at[side, c], relay_recv.at[c - first_relayed], low_peer(1),
        )

    def pass_copy(side, c):
        lanes = pl.ds(pl.multiple_of(c * CHUNK, CHUNK), CHUNK)
        slot = c - first_relayed
        return send(relay.at[slot], halo.at[side, :, lanes], relay_send.at[slot], halo_recv.at[side, c], slanted)

    def relays(side, c):
        return (core == 1 - side) & gives & (c >= first_relayed)

    def send_direct(c):
        for side, present in ((0, has_next), (1, has_prev)):
            if low_count == 2:
                present = present & jnp.logical_not(relays(side, c))

            @pl.when(present)
            def _(side=side):
                halo_copy(side, c).start()

    def send_relay(c):
        if low_count == 2:
            for side in range(2):
                @pl.when(relays(side, c))
                def _(side=side):
                    relay_copy(side, c).start()

    def pass_halo(c):
        if low_count == 2:
            for side in range(2):
                @pl.when((core == 1 - side) & jnp.logical_not(gives) & (c >= first_relayed) & (c < chunks))
                def _(side=side):
                    relay_copy(side, c).wait_recv()
                    pass_copy(side, c).start()

    def steps(number, function):
        def body(step, carry):
            function(step)
            return carry

        lax.fori_loop(1, number, body, 0)

    def mate_copy(number, both):
        return send(both.at[core], both.at[core], mate_send.at[number], mate_recv.at[number], mate)

    def color_high(step):
        rows_of = pl.ds(pl.multiple_of(lax.rem(high + step, HIGH) * (low_count * 16), 16), low_count * 16)
        return send(colors_out.at[rows_of], colors_high.at[step - 1], color_send.at[step], color_recv.at[step], high_peer(step))

    def color_low(step):
        rows_of = pl.ds(pl.multiple_of((high * low_count + lax.rem(low + step, low_count)) * 16, 16), 16)
        slot = HIGH + step
        return send(colors_out.at[rows_of], colors_low.at[step - 1], color_send.at[slot], color_recv.at[slot], low_peer(step))

    def crop_rows(block, to_chip):
        return pl.ds(pl.multiple_of((block * half + to_chip) * 16, 16), 16)

    def crop_copy(block, step):
        return send(
            crops_out.at[crop_rows(block, lax.rem(chip + step, half))], crops_in.at[block, step - 1],
            crop_send.at[block, step], crop_recv.at[block, step], chip_peer(step),
        )

    item = back_pick.shape[0] // half

    def back_rows(to_chip):
        return pl.ds(pl.multiple_of(to_chip * item, 16), item)

    def back_copy(m, step):
        return send(
            back_out.at[m, back_rows(lax.rem(chip + step, half))], back_in.at[m, step - 1],
            back_send.at[m, step], back_recv.at[m, step], chip_peer(step),
        )

    def sum_low(step):
        return send(sums.at[0], sums_in.at[step - 1], sum_send.at[step], sum_recv.at[step], low_peer(step))

    def sum_high(step):
        slot = low_count + step
        return send(sums.at[1], sums_in.at[slot - 2], sum_send.at[slot], sum_recv.at[slot], high_peer(step))

    def sum_mate():
        return send(sums.at[2], sums_in.at[low_count + HIGH - 2], sum_send.at[0], sum_recv.at[0], mate)

    def add_sums(start, number, total):
        return lax.fori_loop(0, number, lambda n, value: value + sums_in[start + n], total)

    steps(low_count, lambda step: sum_low(step).start())
    send_direct(0)
    for c in range(1, AHEAD):
        send_direct(c)
    for c in range(RELAY_AHEAD):
        send_relay(c)

    tall = 768
    local[3].wait()

    @pl.loop(0, cells // tall)
    def _(m):
        span = pl.ds(pl.multiple_of(m * tall, tall), tall)
        acc[0, span, :] = jnp.dot(feat[span, :], w_one[...], preferred_element_type=F32)

    @pl.when(jnp.logical_not(has_prev))
    def _():
        grown[0:edge, :] = jnp.zeros((edge, CHUNK), F32)

    @pl.when(jnp.logical_not(has_next))
    def _():
        grown[edge + cells :, :] = jnp.zeros((edge, CHUNK), F32)

    def widen(source, start, count, lanes):
        @pl.loop(0, count // 48)
        def _(n):
            grown[pl.ds(pl.multiple_of(start + n * 48, 8), 48), :] = source[
                pl.ds(pl.multiple_of(n * 48, 16), 48), lanes
            ].astype(F32)

    local[1].wait()
    local[2].wait()
    experts = routes_ref[...].astype(F32)
    square = (count, count)
    down, over = lax.broadcasted_iota(jnp.int32, square, 0), lax.broadcasted_iota(jnp.int32, square, 1)
    spread = jnp.broadcast_to(experts, square)

    def stand(row):
        return jnp.sum(jnp.where(down == over, jnp.broadcast_to(row, square), 0.0), axis=1, keepdims=True)

    upright = stand(experts)
    rank = jnp.sum(jnp.where((upright == spread) & (down < over), 1.0, 0.0), axis=0, keepdims=True)
    strip_blocks = rows // CELLS
    block_row, block_col = blocks_ref[0:1, :].astype(F32), blocks_ref[1:2, :].astype(F32)
    strip_row = (blocks_ref[0:1, :] // strip_blocks).astype(F32)
    strip_col = stand(strip_row)
    beside = jnp.broadcast_to(strip_row, square) == strip_col
    first_strip = lax.convert_element_type(chip * 2, F32)

    def listed_at(strip, place):
        within = strip - first_strip
        return jnp.where((within >= 0) & (within < 2), within * 8 + place, -1.0)

    own_row_index = listed_at(strip_row, jnp.sum(jnp.where(beside & (down < over), 1.0, 0.0), axis=0, keepdims=True))
    own_col_index = listed_at(strip_col, jnp.sum(jnp.where(beside & (over < down), 1.0, 0.0), axis=1, keepdims=True))
    slot_col = upright * CAP + jnp.sum(jnp.where((upright == spread) & (over < down), 1.0, 0.0), axis=1, keepdims=True)
    local_row = block_row - lax.convert_element_type(me * strip_blocks, F32)

    def own_values(index, values):
        shape = (index.shape[0], count)
        hit = jnp.broadcast_to(own_row_index, shape) == (index + core * 8).astype(F32)
        return jnp.max(jnp.where(hit, jnp.broadcast_to(values, shape), -1e6), axis=1, keepdims=True)

    own_row = lax.broadcasted_iota(jnp.int32, (128, 1), 0)
    own_base = own_values(own_row >> 4, local_row * (CELLS * cols) + block_col * CELLS)
    wanted_cell = own_base + (((own_row >> 2) & 3) * cols + (own_row & 3)).astype(F32)
    cell_at = lax.broadcasted_iota(jnp.int32, (128, cells), 1).astype(F32)
    own_pick[...] = (cell_at == wanted_cell).astype(F32).astype(BF16)

    own_lane = lax.broadcasted_iota(jnp.int32, (1, 256), 1)

    def own_slots(index):
        hit = own_col_index == index.astype(F32)
        return jnp.max(jnp.where(hit, jnp.broadcast_to(slot_col, (count, 256)), -1.0), axis=0, keepdims=True)

    own_slot = own_slots(own_lane >> 4)
    @pl.loop(0, CAP * half // 8)
    def _(n):
        row = lax.broadcasted_iota(jnp.int32, (128, 1), 0) + n * 128
        index = row >> 4
        tile = (index % half) * 2 + core
        hit = (own_slot == (tile * CAP + index // half).astype(F32)) & ((own_lane & 15) == (row & 15))
        crop_pick[pl.ds(pl.multiple_of(n * 128, 128), 128), :] = hit.astype(F32).astype(BF16)

    def to_expert(expert):
        return jnp.where(experts == lax.convert_element_type(expert, F32), rank, -1.0)

    to_first, to_second = to_expert(2 * chip), to_expert(2 * chip + 1)

    @pl.loop(0, half)
    def _(n):
        tile = n * 2 + core
        span = item // QUARTERS
        line = lax.broadcasted_iota(jnp.int32, (item, 1), 0)
        quarter = sum((line >= q * span).astype(jnp.int32) for q in range(1, QUARTERS))
        line = line - quarter * span
        place = sum((line >= p * classes).astype(jnp.int32) for p in range(1, span // classes)) + jnp.zeros_like(line)
        kind = line - place * classes
        listed = lax.broadcasted_iota(jnp.int32, (item, count), 1)
        wanted = listed == tile * (span // classes) + place
        given = lax.broadcasted_iota(jnp.int32, (item, 128), 1)
        right_place = ((given & 7) == kind) & ((given >> 5) == quarter)
        for s, values in enumerate((to_first, to_second)):
            slot = jnp.max(jnp.where(wanted, jnp.broadcast_to(values, (item, count)), -1.0), axis=1, keepdims=True)
            pick = (((given >> 3) & 3).astype(F32) == slot) & right_place
            back_pick[back_rows(n), s * 128 : s * 128 + 128] = pick.astype(F32).astype(BF16)

    steps(low_count, lambda step: sum_low(step).wait_recv())
    sums[1] = add_sums(0, low_count - 1, sums[0])
    steps(HIGH, lambda step: sum_high(step).start())

    local[4].wait()
    parts_high = image.shape[0]
    across = parts_high // 3
    group = 2 * 3 * BLK
    line = lax.broadcasted_iota(jnp.int32, (group, 1), 0)
    line_own = (line >= 3 * BLK).astype(jnp.int32)
    line_channel = (line - line_own * (3 * BLK)) // BLK
    lane = lax.broadcasted_iota(jnp.int32, (1, BLK * BLK), 1)
    source = lax.broadcasted_iota(jnp.int32, (1, parts_high), 1).astype(F32)
    keep = (line & (BLK - 1)) == (lane & (BLK - 1))
    tall_rows = image.shape[1]
    image_row = lax.broadcasted_iota(jnp.int32, (tall_rows, 1), 0)
    image_lane = (lax.broadcasted_iota(jnp.int32, (1, tall_rows), 1) // BLK).astype(F32)
    fold = ((image_row & (BLK - 1)) == (lane >> 5)).astype(F32).astype(BF16)
    own_colors[...] = jnp.zeros(own_colors.shape, F32)

    for n in range(OWN // 2):
        index = line_own + 2 * n
        at = own_values(index, local_row)
        wanted = own_values(index, block_col) * BLK + (line_channel * across + (line & (BLK - 1))).astype(F32)
        chosen = (source == wanted).astype(F32).astype(BF16)
        columns = jnp.dot(chosen, image[...], preferred_element_type=F32)
        columns = jnp.where(image_lane == at, columns, 0.0).astype(BF16)
        strips = jnp.where(keep, jnp.dot(columns, fold, preferred_element_type=F32), 0.0)
        for p in range(6):
            to = (2 * n + p // 3) * 4 + p % 3
            own_colors[to : to + 1, :] = jnp.sum(strips[p * BLK : (p + 1) * BLK], axis=0, keepdims=True)

    colors_both[core] = own_colors[...].astype(BF16)
    mate_copy(0, colors_both).start()

    local[5].wait()
    local[6].wait()

    def one_chunk(c, carry):
        @pl.when(c < chunks - AHEAD)
        def _():
            send_direct(c + AHEAD)

        @pl.when(c < chunks - RELAY_AHEAD)
        def _():
            send_relay(c + RELAY_AHEAD)

        @pl.when(c == 2)
        def _():
            mate_copy(0, colors_both).wait_recv()
            lane_of = own_lane[:, 0:32]
            for s in range(2):
                lane_slot = own_slots((own_lane & 31) // 4 + 8 * s)[:, 0:32]

                @pl.loop(0, half)
                def _(n, s=s, lane_slot=lane_slot):
                    row = lax.broadcasted_iota(jnp.int32, (16, 1), 0)
                    hit = (lane_slot == ((n * 2 + core) * CAP + (row >> 2)).astype(F32)) & ((lane_of & 3) == (row & 3))
                    found = jnp.dot(hit.astype(F32).astype(BF16), colors_both[s], preferred_element_type=F32)
                    rows_of = pl.ds(pl.multiple_of(n * 16, 16), 16)
                    if s == 0:
                        colors_out[rows_of, :] = found.astype(BF16)
                    else:
                        colors_out[rows_of, :] = (colors_out[rows_of, :].astype(F32) + found).astype(BF16)

            steps(HIGH, lambda step: color_high(step).start())

        @pl.when(c == 1)
        def _():
            steps(HIGH, lambda step: sum_high(step).wait_recv())
            sums[2] = add_sums(low_count - 1, HIGH - 1, sums[1])
            sum_mate().start()

        @pl.when(c == 3)
        def _():
            sum_mate().wait_recv()
            local[7].wait()
            local[8].wait()
            pooled = add_sums(low_count + HIGH - 2, 1, sums[2]) / (cells * tiles)
            context = jnp.maximum(exact_row_dot(pooled, w_pool[...]), 0.0)
            context_ref[...] = context
            offset_ref[...] = exact_row_dot(context, w_proj[4 * width :, :])

        @pl.when(c == chunks - 2)
        def _():
            steps(HIGH, lambda step: color_high(step).wait_recv())
            rows_of = pl.ds(pl.multiple_of(high * (low_count * 16), 16), low_count * 16)

            def add(n, total):
                return total + colors_high[n].astype(F32)

            colors_out[rows_of, :] = lax.fori_loop(0, HIGH - 1, add, colors_out[rows_of, :].astype(F32)).astype(BF16)
            steps(low_count, lambda step: color_low(step).start())

        @pl.when(c == chunks - 3)
        def _():
            @pl.loop(0, cells // tall)
            def _(m):
                span = pl.ds(pl.multiple_of(m * tall, tall), tall)
                branch = jnp.maximum(acc[0, span, :], 0.0).astype(BF16)
                acc[0, span, :] = offset_ref[...] + jnp.dot(branch, w_proj[0:width, :], preferred_element_type=F32)

        for at, (start, stop) in (
            (chunks // 2, (0, chunks // 2)), (chunks - 2, (chunks // 2, chunks - 2)), (chunks - 1, (chunks - 2, chunks - 1))
        ):
            @pl.when(c == at)
            def _(start=start * CHUNK, stop=stop * CHUNK):
                for k in range(3):
                    @pl.loop(0, cells // tall)
                    def _(m, k=k):
                        span = pl.ds(pl.multiple_of(m * tall, tall), tall)
                        part = jnp.dot(depth[k, span, start:stop], w_rates[k, start:stop, :], preferred_element_type=F32)
                        acc[k + 1, span, :] = part if start == 0 else acc[k + 1, span, :] + part

        lanes = pl.ds(pl.multiple_of(c * CHUNK, CHUNK), CHUNK)
        widen(feat, edge, cells, lanes)

        def take(side, present):
            @pl.when(present)
            def _():
                halo_copy(side, c).wait_recv()
                widen(halo.at[side], 0 if side == 0 else edge + cells, edge, lanes)

        def map_rows(late):
            for part in range(CHUNK // 128):
                inner = slice(part * 128, part * 128 + 128)
                outer = pl.ds(pl.multiple_of(c * CHUNK + part * 128, 128), 128)
                for k, d in enumerate(RATES):
                    taps = [
                        jnp.broadcast_to(w_depth_ref[t, k : k + 1, outer].astype(F32), (8, 128)) for t in range(9)
                    ]

                    def weigh(parts, column, taps=taps):
                        total = None
                        for i in range(3):
                            tap = jnp.concatenate([taps[3 * i + column]] * (parts[i].shape[0] // 8), axis=0)
                            term = parts[i] * tap
                            total = term if total is None else total + term
                        return total

                    def two_rows(pair, d=d, weigh=weigh, inner=inner, outer=outer, k=k):
                        results = []
                        for r in range(2):
                            parts = []
                            for i in (-1, 0, 1):
                                start = pl.multiple_of((REACH + i * d + r) * cols + pair * (2 * cols), 8)
                                parts.append(grown[pl.ds(start, cols), inner])
                            low = -(-(cols - d) // 8) * 8
                            high = (d // 8) * 8
                            middle = weigh(parts, 1)
                            left = weigh([p[:low] for p in parts], 0)
                            right = weigh([p[high:] for p in parts], 2)
                            fill = jnp.zeros((d, 128), F32)
                            left = jnp.concatenate([fill, left[: cols - d]], axis=0)
                            right = jnp.concatenate([right[d - high :], fill], axis=0)
                            results.append(jnp.maximum(middle + left + right, 0.0))
                        depth[k, pl.ds(pl.multiple_of(pair * (2 * cols), 16), 2 * cols), outer] = jnp.concatenate(
                            results, axis=0
                        ).astype(BF16)

                    pairs = d // 2 if late else (rows - d) // 2
                    after = core == 1 if late else core == 0
                    first_pair = jnp.where(after, rows // 2 - pairs, 0)
                    unroll = max(u for u in (3, 4, 5) if pairs % u == 0 or pairs % u == 1)
                    for n in range(pairs % unroll):
                        two_rows(first_pair + n)
                    first_pair += pairs % unroll

                    @pl.loop(0, pairs // unroll)
                    def _(n, two_rows=two_rows, first_pair=first_pair, unroll=unroll):
                        for u in range(unroll):
                            two_rows(first_pair + n * unroll + u)

        take(1, has_next & (core == 0))
        take(0, has_prev & (core == 1))
        map_rows(False)
        pass_halo(c + 1)
        take(0, has_prev & (core == 0))
        take(1, has_next & (core == 1))
        map_rows(True)
        return carry

    lax.fori_loop(0, chunks, one_chunk, 0)

    @pl.loop(0, cells // tall)
    def _(m):
        span = pl.ds(pl.multiple_of(m * tall, tall), tall)
        blended = acc[0, span, :]
        for k in range(1, 4):
            branch = acc[k, span, :] + jnp.dot(
                depth[k - 1, span, channels - CHUNK :], w_rates[k - 1, channels - CHUNK :, :], preferred_element_type=F32
            )
            branch = jnp.maximum(branch, 0.0).astype(BF16)
            blended += jnp.dot(branch, w_proj[k * width : (k + 1) * width, :], preferred_element_type=F32)
        aspp_ref[span, :] = jnp.maximum(blended, 0.0).astype(BF16)

    leaving = [
        pltpu.make_async_copy(source, target, out_sem.at[n])
        for n, (source, target) in enumerate(((aspp_ref, aspp_hbm), (context_ref, context_hbm), (refined_ref, refined_hbm)))
    ]
    leaving[0].start()
    leaving[1].start()
    crops_both[core] = jnp.dot(own_pick[...], aspp_ref[...], preferred_element_type=F32).astype(BF16)
    mate_copy(1, crops_both).start()
    steps(low_count, lambda step: color_low(step).wait_recv())

    def add_low(n, total):
        return total + colors_low[n].astype(F32)

    mine_ref[...] = lax.fori_loop(
        0, low_count - 1, add_low, colors_out[pl.ds(pl.multiple_of(chip * 16, 16), 16), :].astype(F32)
    )
    side, pixels = BLK, BLK * BLK
    wide = lax.broadcasted_iota(jnp.int32, (3 * CAP, pixels), 1)
    row_at, col_at = wide >> 5, wide & (side - 1)
    received = mine_ref[...]
    colors = jnp.concatenate([received[4 * n : 4 * n + 3] for n in range(CAP)], axis=0)
    local[11].wait()
    pieces = []
    for i in (-1, 0, 1):
        for j in (-1, 0, 1):
            moved = colors if i == 0 and j == 0 else pltpu.roll(colors, (-(side * i + j)) % pixels, 1)
            inside = (row_at + i >= 0) & (row_at + i < side) & (col_at + j >= 0) & (col_at + j < side)
            pieces.append(jnp.where(inside, moved, 0.0))
    pieces.append(jnp.zeros((128 - 9 * 3 * CAP, pixels), F32))
    spread_colors = jnp.concatenate(pieces, axis=0).T.astype(BF16)
    table_ref[:, 0:128] = (table_ref[:, 0:128].astype(F32) + spread_colors.astype(F32)).astype(BF16)

    mate_copy(1, crops_both).wait_recv()

    @pl.loop(0, CAP)
    def _(block):
        @pl.loop(0, half // 8)
        def _(n):
            rows_of = pl.ds(pl.multiple_of((block * (half // 8) + n) * 128, 128), 128)
            found = jnp.dot(crop_pick[rows_of, :], crops_both[...].reshape(256, width), preferred_element_type=F32)
            crops_out[rows_of, :] = found.astype(BF16)

        steps(half, lambda step: crop_copy(block, half - step).start())

    blank = jnp.zeros((side, 3 * width), BF16)
    for block in range(CAP):
        grids[block, 0:side, :] = blank
        grids[block, side + pixels :, :] = blank
    for n in (9, 10, 12, 13):
        local[n].wait()
    tap_row = lax.broadcasted_iota(jnp.int32, (COLOR_ROWS, 27), 0)
    pixel_tap = lax.broadcasted_iota(jnp.int32, (COLOR_ROWS, 27), 1)
    tap_of = sum((pixel_tap >= 3 * n).astype(jnp.int32) for n in range(1, 9))
    for block in range(CAP):
        wanted = tap_of * (3 * CAP) + 3 * block + pixel_tap - 3 * tap_of
        spread_taps = (tap_row == wanted).astype(F32).astype(BF16)
        taps_ref[block, 0:COLOR_ROWS, :] = jnp.dot(spread_taps, color_ref[...], preferred_element_type=F32).astype(BF16)
    scores[...] = jnp.zeros(scores.shape, F32)
    tall = pixels // PARTS
    col = lax.broadcasted_iota(jnp.int32, (pixels, width), 0) & (side - 1)

    def open_block(block):
        steps(half, lambda step: crop_copy(block, step).wait_recv())

        def add_crop(n, total):
            return total + crops_in[block, n].astype(F32)

        crop = lax.fori_loop(0, half - 1, add_crop, crops_out[crop_rows(block, chip), :].astype(F32)).astype(BF16)
        for tap in range(9):
            part = jnp.dot(crop, first[tap * width : (tap + 1) * width, :], preferred_element_type=F32)
            taps_ref[block, COLOR_ROWS + tap * 16 : COLOR_ROWS + tap * 16 + 16, :] = part.astype(BF16)

    def first_conv(block):
        total = jnp.dot(table_ref[...], taps_ref[block], preferred_element_type=F32)
        total = jnp.maximum(total, 0.0)
        before = jnp.where(col == 0, 0.0, pltpu.roll(total, 1, 0))
        after = jnp.where(col == side - 1, 0.0, pltpu.roll(total, pixels - 1, 0))
        inner = slice(side, side + pixels)
        grids[block, inner, 0:width] = before.astype(BF16)
        grids[block, inner, width : 2 * width] = total.astype(BF16)
        grids[block, inner, 2 * width :] = after.astype(BF16)

    def second_conv(pair, m):
        at = m * tall
        total = None
        for i in range(3):
            rows_of = slice(at + side * i, at + side * i + tall)
            both = jnp.concatenate([grids[2 * pair, rows_of, :], grids[2 * pair + 1, rows_of, :]], axis=0)
            term = jnp.dot(both, second[3 * width * i : 3 * width * (i + 1), :], preferred_element_type=F32)
            total = term if total is None else total + term
        total = jnp.maximum(total, 0.0).astype(BF16)
        found = lax.dot_general(head_ref[...], total, (((1,), (1,)), ((), ())), preferred_element_type=F32)
        wide_part = tall // QUARTERS
        for b in range(2):
            for q in range(QUARTERS):
                start = pl.multiple_of(q * (8 * CAP) + (2 * pair + b) * 8, 8)
                left = b * tall + q * wide_part
                scores[m, pl.ds(start, classes), :] = found[:, left : left + wide_part]

    def back_swap(m):
        scores_both[m, core] = scores[m].astype(BF16)
        mate_copy(2 + m, scores_both.at[m]).start()

    def back_spread(m):
        mate_copy(2 + m, scores_both.at[m]).wait_recv()

        @pl.loop(0, half // 2)
        def _(n):
            rows_of = pl.ds(pl.multiple_of(n * (2 * item), 16), 2 * item)
            found = jnp.dot(back_pick[rows_of, 0:128], scores_both[m, 0], preferred_element_type=F32)
            found += jnp.dot(back_pick[rows_of, 128:256], scores_both[m, 1], preferred_element_type=F32)
            back_out[m, rows_of, :] = found.astype(BF16)
            for t in range(2):
                step = lax.rem(2 * n + t - chip + half, half)

                @pl.when(step > 0)
                def _(step=step):
                    back_copy(m, step).start()


    def back_finish(m):
        steps(half, lambda step: back_copy(m, step).wait_recv())

        def add_back(n, total):
            return total + back_in[m, n].astype(F32)

        result = lax.fori_loop(0, half - 1, add_back, back_out[m, back_rows(chip), :].astype(F32))
        span = item // QUARTERS
        wide_part = pixels // (PARTS * QUARTERS)
        for q in range(QUARTERS):
            for p in range(span // classes):
                start = q * span + p * classes
                left = (m * QUARTERS + q) * wide_part
                refined_ref[:, p, left : left + wide_part] = result[start : start + classes].astype(BF16)

    @pl.loop(0, CAP // 2)
    def _(pair):
        @pl.loop(0, 2)
        def _(n):
            open_block(2 * pair + n)
            first_conv(2 * pair + n)

        second_conv(pair, 0)

    for m in range(1, PARTS):
        back_swap(m - 1)
        second_conv(0, m)
        back_spread(m - 1)

        @pl.loop(1, CAP // 2)
        def _(pair, m=m):
            second_conv(pair, m)

    back_swap(PARTS - 1)
    back_spread(PARTS - 1)
    steps(low_count, lambda step: sum_low(step).wait_send())
    steps(HIGH, lambda step: sum_high(step).wait_send())
    sum_mate().wait_send()
    steps(HIGH, lambda step: color_high(step).wait_send())
    steps(low_count, lambda step: color_low(step).wait_send())
    for number, both in enumerate((colors_both, crops_both)):
        mate_copy(number, both).wait_send()

    def drain_crops(block, carry):
        steps(half, lambda step: crop_copy(block, step).wait_send())
        return carry

    lax.fori_loop(0, CAP, drain_crops, 0)

    def drain_halo(c, carry):
        @pl.when(has_next)
        def _():
            halo_copy(0, c).wait_send()

        @pl.when(has_prev)
        def _():
            halo_copy(1, c).wait_send()

        return carry

    lax.fori_loop(0, chunks, drain_halo, 0)
    if low_count == 2:
        def drain_relay(c, carry):
            pass_copy(0, first_relayed + c).wait_send()
            return carry

        lax.fori_loop(0, jnp.where(gives, 0, relayed), drain_relay, 0)

    for m in range(PARTS):
        back_finish(m)
    leaving[2].start()

    for m in range(PARTS):
        steps(half, lambda step, m=m: back_copy(m, step).wait_send())
        mate_copy(2 + m, scores_both.at[m]).wait_send()
    for copy in leaving:
        copy.wait()


def upsample_taps():
    pixels = np.arange(BLK, dtype=np.float32)
    source = np.clip((pixels + 0.5) / 8.0 - 0.5, 0.0, CELLS - 1.0)
    table = np.maximum(1.0 - np.abs(source[:, None] - np.arange(CELLS, dtype=np.float32)[None, :]), 0.0)
    moved = []
    for i in (-1, 0, 1):
        shifted = np.zeros_like(table)
        for p in range(BLK):
            if 0 <= p + i < BLK:
                shifted[p] = table[p + i]
        moved.append(shifted)
    moved = np.stack(moved)
    table = np.einsum("ipa,jqb->pqijab", moved, moved).reshape(BLK * BLK, 9 * CELLS * CELLS)
    return np.pad(table, ((0, 0), (COLOR_ROWS, 0)))


def pyramid(tiles, rows, cols, features, image, blocks, routes, w_one, w_rates, w_depth, w_pool, w_proj,
            w_first, w_color, w_second, w_head):
    channels, width = w_one.shape
    cells = rows * cols
    per = CAP * CELLS * CELLS
    chunks = channels // CHUNK
    edge = REACH * cols
    places = routes.shape[0] // tiles
    classes = w_head.shape[0]
    pixels = BLK * BLK
    item = places * classes * QUARTERS
    low_count = tiles // (2 * HIGH)
    part = pixels // (PARTS * QUARTERS)
    away = pl.BlockSpec(memory_space=pl.ANY)
    dma = pltpu.SemaphoreType.DMA
    image = image.transpose(0, 2, 1).reshape(-1, image.shape[1])
    first, second = w_first.reshape(9 * width, width), w_second.reshape(9 * width, width)
    operands = (
        features.reshape(cells, channels), w_one, w_rates, w_depth.transpose(1, 0, 2), w_pool, w_proj, image, first, second,
        w_color, w_head, jnp.asarray(upsample_taps(), BF16), blocks.T, routes.T,
    )

    links = low_count + HIGH
    half = tiles // 2
    return pl.pallas_call(
        functools.partial(pyramid_kernel, tiles, rows, cols, channels, width),
        out_shape=(
            jax.ShapeDtypeStruct((cells, width), BF16),
            jax.ShapeDtypeStruct((1, width), F32),
            jax.ShapeDtypeStruct((classes, places, pixels), BF16),
        ),
        in_specs=[away] * len(operands),
        out_specs=(away, away, away),
        scratch_shapes=[
            pltpu.VMEM((cells, width), BF16),
            pltpu.VMEM((1, width), F32),
            pltpu.VMEM((classes, places, pixels), BF16),
            dma((3,)),
            *(pltpu.VMEM(operand.shape, operand.dtype) for operand in operands),
            pltpu.VMEM((2, edge, channels), BF16),
            pltpu.VMEM((cells + 2 * edge, CHUNK), F32),
            pltpu.VMEM((3, cells, channels), BF16),
            pltpu.VMEM((4, cells, width), F32),
            pltpu.VMEM((3, 1, channels), F32),
            pltpu.VMEM((links - 1, 1, channels), F32),
            pltpu.VMEM((32, pixels), F32),
            pltpu.VMEM((128, cells), BF16),
            pltpu.VMEM((half * per, 256), BF16),
            pltpu.VMEM((half * item, 256), BF16),
            pltpu.VMEM((16, pixels), F32),
            pltpu.VMEM((1, width), F32),
            pltpu.VMEM((CAP, COLOR_ROWS + 144, width), BF16),
            pltpu.VMEM((CAP, pixels + 2 * BLK, 3 * width), BF16),
            pltpu.VMEM((PARTS, QUARTERS * CAP * 8, part), F32),
            pltpu.VMEM((2, 32, pixels), BF16),
            pltpu.VMEM((half * 16, pixels), BF16),
            pltpu.VMEM((HIGH - 1, low_count * 16, pixels), BF16),
            pltpu.VMEM((low_count - 1, 16, pixels), BF16),
            pltpu.VMEM((2, 128, width), BF16),
            pltpu.VMEM((half * per, width), BF16),
            pltpu.VMEM((CAP, half - 1, 16, width), BF16),
            pltpu.VMEM((PARTS, 2, QUARTERS * CAP * 8, part), BF16),
            pltpu.VMEM((PARTS, half * item, part), BF16),
            pltpu.VMEM((PARTS, half - 1, item, part), BF16),
            dma((len(operands),)),
            dma((2, chunks)),
            dma((2, chunks)),
            *(dma((links,)) for _ in range(4)),
            *(dma((CAP, half)) for _ in range(2)),
            *(dma((PARTS, half)) for _ in range(2)),
            *(dma((2 + PARTS,)) for _ in range(2)),
            pltpu.VMEM((2 * HIGH - 1, edge, CHUNK), BF16),
            *(dma((2 * HIGH - 1,)) for _ in range(2)),
        ],
        compiler_params=pltpu.CompilerParams(collective_id=0, has_side_effects=True, vmem_limit_bytes=60 << 20),
        name="pyramid",
    )(*operands)


def settle_kernel(*refs):
    half = len(refs) // 2
    for source, target in zip(refs[:half], refs[half:]):
        target[...] = source[...]


def settle(*arrays):
    return pl.pallas_call(
        settle_kernel,
        out_shape=tuple(jax.ShapeDtypeStruct(a.shape, a.dtype) for a in arrays),
        name="settle",
    )(*arrays)


def shards(
    tiles,
    features,
    aerial_image,
    blocks,
    routes,
    w_one,
    w_depth,
    w_rates,
    w_pool,
    w_proj,
    w_first,
    w_color,
    w_second,
    w_head,
):
    rows, cols, channels = features.shape
    width = w_one.shape[1]
    aspp, context, refined = pyramid(
        tiles, rows, cols, features, aerial_image, blocks, routes, w_one, w_rates, w_depth, w_pool, w_proj,
        w_first[0], w_color[0], w_second[0], w_head[0],
    )
    aspp, context, refined = settle(aspp, context, refined)
    return aspp.reshape(rows, cols, width), context.reshape(width), refined.transpose(1, 0, 2)


def solution(mesh):
    return jax.shard_map(
        functools.partial(shards, mesh.shape["tile"]),
        mesh=mesh,
        in_specs=(
            P(("groups", "tile"), None, None),
            P(None, ("groups", "tile"), None),
            P("groups", None),
            P("groups", None),
            P(),
            P(),
            P(),
            P(),
            P(),
            P("tile", None, None, None),
            P("tile", None, None),
            P("tile", None, None, None),
            P("tile", None, None),
        ),
        out_specs=(
            P(("groups", "tile"), None, None),
            P("groups"),
            P(("groups", "tile"), None, None),
        ),
        check_vma=False,
    )
```

```python
import functools

import jax
import jax.numpy as jnp
import numpy as np
from jax import lax
from jax.experimental import pallas as pl
from jax.experimental.pallas import tpu as pltpu
from jax.sharding import PartitionSpec as P

BLK = 32
CAP = 4
CELLS = 4
RATES = (6, 12, 18)
REACH = 18
CHUNK = 256
HIGH = 4
QUARTERS = 4
COLOR_ROWS = 112
AHEAD = 4
RELAY_AHEAD = 6
PARTS = 2
OWN = 6
F32 = jnp.float32
BF16 = jnp.bfloat16


def split_three(value):
    high = value.astype(BF16)
    rest = value - high.astype(F32)
    mid = rest.astype(BF16)
    low = (rest - mid.astype(F32)).astype(BF16)
    return high, mid, low


def exact_row_dot(row, weights):
    high, mid, low = split_three(row)
    stacked = jnp.concatenate(
        [high.astype(F32), mid.astype(F32), low.astype(F32), jnp.zeros((13, row.shape[1]), F32)], axis=0
    ).astype(BF16)
    product = jnp.dot(stacked, weights, preferred_element_type=F32)
    return product[0:1] + product[1:2] + product[2:3]


def pyramid_kernel(
    tiles, rows, cols, channels, width,
    feat_hbm, w_one_hbm, w_rates_hbm, w_depth_hbm, w_pool_hbm, w_proj_hbm, image_hbm, first_hbm, second_hbm,
    color_hbm, head_hbm, table_hbm, blocks_hbm, routes_hbm,
    aspp_hbm, context_hbm, refined_hbm,
    aspp_ref, context_ref, refined_ref, out_sem,
    feat, w_one, w_rates, w_depth_ref, w_pool, w_proj, image, first, second, color_ref, head_ref, table_ref, blocks_ref, routes_ref,
    halo, grown, depth, acc, sums, sums_in, own_colors, own_pick, crop_pick, back_pick, mine_ref, offset_ref,
    taps_ref, grids, scores,
    colors_both, colors_out, colors_high, colors_low, crops_both, crops_out, crops_in, scores_both, back_out, back_in,
    local_sem, halo_send, halo_recv, sum_send, sum_recv, color_send, color_recv, crop_send, crop_recv, back_send, back_recv,
    mate_send, mate_recv, relay, relay_send, relay_recv,
):
    me = lax.axis_index("tile")
    chunks = channels // CHUNK
    edge = REACH * cols
    cells = rows * cols
    count = routes_ref.shape[1]
    classes = head_ref.shape[0]
    half, low_count = tiles // 2, tiles // (2 * HIGH)
    core = lax.rem(me, 2)
    low = lax.rem(me // 2, low_count)
    high = me // (2 * low_count)
    chip = me // 2

    local = [
        pltpu.make_async_copy(source, target, local_sem.at[n])
        for n, (source, target) in enumerate(
            ((feat_hbm, feat), (blocks_hbm, blocks_ref), (routes_hbm, routes_ref), (w_one_hbm, w_one), (image_hbm, image),
             (w_depth_hbm, w_depth_ref), (w_rates_hbm, w_rates), (w_pool_hbm, w_pool), (w_proj_hbm, w_proj),
             (color_hbm, color_ref), (head_hbm, head_ref), (table_hbm, table_ref), (first_hbm, first), (second_hbm, second))
        )
    ]
    for copy in local:
        copy.start()

    mate = me + 1 - 2 * core

    def low_peer(step):
        return (high * low_count + lax.rem(low + step, low_count)) * 2 + core

    def high_peer(step):
        return (lax.rem(high + step, HIGH) * low_count + low) * 2 + core

    has_next = me < tiles - 1
    has_prev = me > 0
    barrier = pltpu.get_barrier_semaphore()

    def greet(peer):
        pl.semaphore_signal(barrier, inc=1, device_id={"tile": peer}, device_id_type=pl.DeviceIdType.MESH)

    def chip_peer(step):
        return lax.rem(chip + step, half) * 2 + core

    def greet_chip(step, carry):
        greet(chip_peer(step))
        return carry

    outward = jnp.where(core == 1, me + 1, me - 1)
    has_outward = (outward >= 0) & (outward < tiles)

    slanted = jnp.where(core == 1, me + 3, me - 3)
    has_slanted = (slanted >= 0) & (slanted < tiles) if low_count == 2 else False
    forward = jnp.where(high < HIGH - 1, 2 * (HIGH - 1 - high) + 1, 0)
    relayed = jnp.where(core == 1, forward, 2 * high) if low_count == 2 else 0
    gives = low == core
    first_relayed = chunks - relayed

    @pl.when(has_outward)
    def _():
        greet(outward)

    if low_count == 2:
        @pl.when(has_slanted)
        def _():
            greet(slanted)

    greet(mate)
    lax.fori_loop(1, half, greet_chip, 0)
    local[0].wait()

    def sum_rows(n, totals):
        block = feat[pl.ds(pl.multiple_of(n * 16, 16), 16), :].astype(F32)
        return totals + block[0:8] + block[8:16]

    totals = lax.fori_loop(0, cells // 16, sum_rows, jnp.zeros((8, channels), F32))
    sums[0] = jnp.sum(totals, axis=0, keepdims=True)

    expected = half + has_outward.astype(jnp.int32)
    pl.semaphore_wait(barrier, expected + has_slanted.astype(jnp.int32) if low_count == 2 else expected)

    def send(source, target, send_sem, recv_sem, peer):
        return pltpu.make_async_remote_copy(
            src_ref=source, dst_ref=target, send_sem=send_sem, recv_sem=recv_sem,
            device_id={"tile": peer}, device_id_type=pl.DeviceIdType.MESH,
        )

    def halo_copy(side, c):
        lanes = pl.ds(pl.multiple_of(c * CHUNK, CHUNK), CHUNK)
        return send(
            feat_hbm.at[pl.ds(cells - edge if side == 0 else 0, edge), lanes], halo.at[side, :, lanes],
            halo_send.at[side, c], halo_recv.at[side, c],
            lax.rem(me + 1, tiles) if side == 0 else lax.rem(me + tiles - 1, tiles),
        )

    def relay_copy(side, c):
        lanes = pl.ds(pl.multiple_of(c * CHUNK, CHUNK), CHUNK)
        return send(
            feat_hbm.at[pl.ds(cells - edge if side == 0 else 0, edge), lanes], relay.at[c - first_relayed],
            halo_send.at[side, c], relay_recv.at[c - first_relayed], low_peer(1),
        )

    def pass_copy(side, c):
        lanes = pl.ds(pl.multiple_of(c * CHUNK, CHUNK), CHUNK)
        slot = c - first_relayed
        return send(relay.at[slot], halo.at[side, :, lanes], relay_send.at[slot], halo_recv.at[side, c], slanted)

    def relays(side, c):
        return (core == 1 - side) & gives & (c >= first_relayed)

    def send_direct(c):
        for side, present in ((0, has_next), (1, has_prev)):
            if low_count == 2:
                present = present & jnp.logical_not(relays(side, c))

            @pl.when(present)
            def _(side=side):
                halo_copy(side, c).start()

    def send_relay(c):
        if low_count == 2:
            for side in range(2):
                @pl.when(relays(side, c))
                def _(side=side):
                    relay_copy(side, c).start()

    def pass_halo(c):
        if low_count == 2:
            for side in range(2):
                @pl.when((core == 1 - side) & jnp.logical_not(gives) & (c >= first_relayed) & (c < chunks))
                def _(side=side):
                    relay_copy(side, c).wait_recv()
                    pass_copy(side, c).start()

    def steps(number, function):
        def body(step, carry):
            function(step)
            return carry

        lax.fori_loop(1, number, body, 0)

    def mate_copy(number, both):
        return send(both.at[core], both.at[core], mate_send.at[number], mate_recv.at[number], mate)

    def color_high(step):
        rows_of = pl.ds(pl.multiple_of(lax.rem(high + step, HIGH) * (low_count * 16), 16), low_count * 16)
        return send(colors_out.at[rows_of], colors_high.at[step - 1], color_send.at[step], color_recv.at[step], high_peer(step))

    def color_low(step):
        rows_of = pl.ds(pl.multiple_of((high * low_count + lax.rem(low + step, low_count)) * 16, 16), 16)
        slot = HIGH + step
        return send(colors_out.at[rows_of], colors_low.at[step - 1], color_send.at[slot], color_recv.at[slot], low_peer(step))

    def crop_rows(block, to_chip):
        return pl.ds(pl.multiple_of((block * half + to_chip) * 16, 16), 16)

    def crop_copy(block, step):
        return send(
            crops_out.at[crop_rows(block, lax.rem(chip + step, half))], crops_in.at[block, step - 1],
            crop_send.at[block, step], crop_recv.at[block, step], chip_peer(step),
        )

    item = back_pick.shape[0] // half

    def back_rows(to_chip):
        return pl.ds(pl.multiple_of(to_chip * item, 16), item)

    def back_copy(m, step):
        return send(
            back_out.at[m, back_rows(lax.rem(chip + step, half))], back_in.at[m, step - 1],
            back_send.at[m, step], back_recv.at[m, step], chip_peer(step),
        )

    def sum_low(step):
        return send(sums.at[0], sums_in.at[step - 1], sum_send.at[step], sum_recv.at[step], low_peer(step))

    def sum_high(step):
        slot = low_count + step
        return send(sums.at[1], sums_in.at[slot - 2], sum_send.at[slot], sum_recv.at[slot], high_peer(step))

    def sum_mate():
        return send(sums.at[2], sums_in.at[low_count + HIGH - 2], sum_send.at[0], sum_recv.at[0], mate)

    def add_sums(start, number, total):
        return lax.fori_loop(0, number, lambda n, value: value + sums_in[start + n], total)

    steps(low_count, lambda step: sum_low(step).start())
    send_direct(0)
    for c in range(1, AHEAD):
        send_direct(c)
    for c in range(RELAY_AHEAD):
        send_relay(c)

    tall = 768
    local[3].wait()

    @pl.loop(0, cells // tall)
    def _(m):
        span = pl.ds(pl.multiple_of(m * tall, tall), tall)
        acc[0, span, :] = jnp.dot(feat[span, :], w_one[...], preferred_element_type=F32)

    @pl.when(jnp.logical_not(has_prev))
    def _():
        grown[0:edge, :] = jnp.zeros((edge, CHUNK), F32)

    @pl.when(jnp.logical_not(has_next))
    def _():
        grown[edge + cells :, :] = jnp.zeros((edge, CHUNK), F32)

    def widen(source, start, count, lanes):
        @pl.loop(0, count // 48)
        def _(n):
            grown[pl.ds(pl.multiple_of(start + n * 48, 8), 48), :] = source[
                pl.ds(pl.multiple_of(n * 48, 16), 48), lanes
            ].astype(F32)

    local[1].wait()
    local[2].wait()
    experts = routes_ref[...].astype(F32)
    square = (count, count)
    down, over = lax.broadcasted_iota(jnp.int32, square, 0), lax.broadcasted_iota(jnp.int32, square, 1)
    spread = jnp.broadcast_to(experts, square)

    def stand(row):
        return jnp.sum(jnp.where(down == over, jnp.broadcast_to(row, square), 0.0), axis=1, keepdims=True)

    upright = stand(experts)
    rank = jnp.sum(jnp.where((upright == spread) & (down < over), 1.0, 0.0), axis=0, keepdims=True)
    strip_blocks = rows // CELLS
    block_row, block_col = blocks_ref[0:1, :].astype(F32), blocks_ref[1:2, :].astype(F32)
    strip_row = (blocks_ref[0:1, :] // strip_blocks).astype(F32)
    strip_col = stand(strip_row)
    beside = jnp.broadcast_to(strip_row, square) == strip_col
    first_strip = lax.convert_element_type(chip * 2, F32)

    def listed_at(strip, place):
        within = strip - first_strip
        return jnp.where((within >= 0) & (within < 2), within * 8 + place, -1.0)

    own_row_index = listed_at(strip_row, jnp.sum(jnp.where(beside & (down < over), 1.0, 0.0), axis=0, keepdims=True))
    own_col_index = listed_at(strip_col, jnp.sum(jnp.where(beside & (over < down), 1.0, 0.0), axis=1, keepdims=True))
    slot_col = upright * CAP + jnp.sum(jnp.where((upright == spread) & (over < down), 1.0, 0.0), axis=1, keepdims=True)
    local_row = block_row - lax.convert_element_type(me * strip_blocks, F32)

    def own_values(index, values):
        shape = (index.shape[0], count)
        hit = jnp.broadcast_to(own_row_index, shape) == (index + core * 8).astype(F32)
        return jnp.max(jnp.where(hit, jnp.broadcast_to(values, shape), -1e6), axis=1, keepdims=True)

    own_row = lax.broadcasted_iota(jnp.int32, (128, 1), 0)
    own_base = own_values(own_row >> 4, local_row * (CELLS * cols) + block_col * CELLS)
    wanted_cell = own_base + (((own_row >> 2) & 3) * cols + (own_row & 3)).astype(F32)
    cell_at = lax.broadcasted_iota(jnp.int32, (128, cells), 1).astype(F32)
    own_pick[...] = (cell_at == wanted_cell).astype(F32).astype(BF16)

    own_lane = lax.broadcasted_iota(jnp.int32, (1, 256), 1)

    def own_slots(index):
        hit = own_col_index == index.astype(F32)
        return jnp.max(jnp.where(hit, jnp.broadcast_to(slot_col, (count, 256)), -1.0), axis=0, keepdims=True)

    own_slot = own_slots(own_lane >> 4)
    @pl.loop(0, CAP * half // 8)
    def _(n):
        row = lax.broadcasted_iota(jnp.int32, (128, 1), 0) + n * 128
        index = row >> 4
        tile = (index % half) * 2 + core
        hit = (own_slot == (tile * CAP + index // half).astype(F32)) & ((own_lane & 15) == (row & 15))
        crop_pick[pl.ds(pl.multiple_of(n * 128, 128), 128), :] = hit.astype(F32).astype(BF16)

    def to_expert(expert):
        return jnp.where(experts == lax.convert_element_type(expert, F32), rank, -1.0)

    to_first, to_second = to_expert(2 * chip), to_expert(2 * chip + 1)

    @pl.loop(0, half)
    def _(n):
        tile = n * 2 + core
        span = item // QUARTERS
        line = lax.broadcasted_iota(jnp.int32, (item, 1), 0)
        quarter = sum((line >= q * span).astype(jnp.int32) for q in range(1, QUARTERS))
        line = line - quarter * span
        place = sum((line >= p * classes).astype(jnp.int32) for p in range(1, span // classes)) + jnp.zeros_like(line)
        kind = line - place * classes
        listed = lax.broadcasted_iota(jnp.int32, (item, count), 1)
        wanted = listed == tile * (span // classes) + place
        given = lax.broadcasted_iota(jnp.int32, (item, 128), 1)
        right_place = ((given & 7) == kind) & ((given >> 5) == quarter)
        for s, values in enumerate((to_first, to_second)):
            slot = jnp.max(jnp.where(wanted, jnp.broadcast_to(values, (item, count)), -1.0), axis=1, keepdims=True)
            pick = (((given >> 3) & 3).astype(F32) == slot) & right_place
            back_pick[back_rows(n), s * 128 : s * 128 + 128] = pick.astype(F32).astype(BF16)

    steps(low_count, lambda step: sum_low(step).wait_recv())
    sums[1] = add_sums(0, low_count - 1, sums[0])
    steps(HIGH, lambda step: sum_high(step).start())

    local[4].wait()
    parts_high = image.shape[0]
    across = parts_high // 3
    group = 2 * 3 * BLK
    line = lax.broadcasted_iota(jnp.int32, (group, 1), 0)
    line_own = (line >= 3 * BLK).astype(jnp.int32)
    line_channel = (line - line_own * (3 * BLK)) // BLK
    lane = lax.broadcasted_iota(jnp.int32, (1, BLK * BLK), 1)
    source = lax.broadcasted_iota(jnp.int32, (1, parts_high), 1).astype(F32)
    keep = (line & (BLK - 1)) == (lane & (BLK - 1))
    tall_rows = image.shape[1]
    image_row = lax.broadcasted_iota(jnp.int32, (tall_rows, 1), 0)
    image_lane = (lax.broadcasted_iota(jnp.int32, (1, tall_rows), 1) // BLK).astype(F32)
    fold = ((image_row & (BLK - 1)) == (lane >> 5)).astype(F32).astype(BF16)
    own_colors[...] = jnp.zeros(own_colors.shape, F32)

    for n in range(OWN // 2):
        index = line_own + 2 * n
        at = own_values(index, local_row)
        wanted = own_values(index, block_col) * BLK + (line_channel * across + (line & (BLK - 1))).astype(F32)
        chosen = (source == wanted).astype(F32).astype(BF16)
        columns = jnp.dot(chosen, image[...], preferred_element_type=F32)
        columns = jnp.where(image_lane == at, columns, 0.0).astype(BF16)
        strips = jnp.where(keep, jnp.dot(columns, fold, preferred_element_type=F32), 0.0)
        for p in range(6):
            to = (2 * n + p // 3) * 4 + p % 3
            own_colors[to : to + 1, :] = jnp.sum(strips[p * BLK : (p + 1) * BLK], axis=0, keepdims=True)

    colors_both[core] = own_colors[...].astype(BF16)
    mate_copy(0, colors_both).start()

    local[5].wait()
    local[6].wait()

    def one_chunk(c, carry):
        @pl.when(c < chunks - AHEAD)
        def _():
            send_direct(c + AHEAD)

        @pl.when(c < chunks - RELAY_AHEAD)
        def _():
            send_relay(c + RELAY_AHEAD)

        @pl.when(c == 2)
        def _():
            mate_copy(0, colors_both).wait_recv()
            lane_of = own_lane[:, 0:32]
            for s in range(2):
                lane_slot = own_slots((own_lane & 31) // 4 + 8 * s)[:, 0:32]

                @pl.loop(0, half)
                def _(n, s=s, lane_slot=lane_slot):
                    row = lax.broadcasted_iota(jnp.int32, (16, 1), 0)
                    hit = (lane_slot == ((n * 2 + core) * CAP + (row >> 2)).astype(F32)) & ((lane_of & 3) == (row & 3))
                    found = jnp.dot(hit.astype(F32).astype(BF16), colors_both[s], preferred_element_type=F32)
                    rows_of = pl.ds(pl.multiple_of(n * 16, 16), 16)
                    if s == 0:
                        colors_out[rows_of, :] = found.astype(BF16)
                    else:
                        colors_out[rows_of, :] = (colors_out[rows_of, :].astype(F32) + found).astype(BF16)

            steps(HIGH, lambda step: color_high(step).start())

        @pl.when(c == 1)
        def _():
            steps(HIGH, lambda step: sum_high(step).wait_recv())
            sums[2] = add_sums(low_count - 1, HIGH - 1, sums[1])
            sum_mate().start()

        @pl.when(c == 3)
        def _():
            sum_mate().wait_recv()
            local[7].wait()
            local[8].wait()
            pooled = add_sums(low_count + HIGH - 2, 1, sums[2]) / (cells * tiles)
            context = jnp.maximum(exact_row_dot(pooled, w_pool[...]), 0.0)
            context_ref[...] = context
            offset_ref[...] = exact_row_dot(context, w_proj[4 * width :, :])

        @pl.when(c == chunks - 2)
        def _():
            steps(HIGH, lambda step: color_high(step).wait_recv())
            rows_of = pl.ds(pl.multiple_of(high * (low_count * 16), 16), low_count * 16)

            def add(n, total):
                return total + colors_high[n].astype(F32)

            colors_out[rows_of, :] = lax.fori_loop(0, HIGH - 1, add, colors_out[rows_of, :].astype(F32)).astype(BF16)
            steps(low_count, lambda step: color_low(step).start())

        @pl.when(c == chunks - 3)
        def _():
            @pl.loop(0, cells // tall)
            def _(m):
                span = pl.ds(pl.multiple_of(m * tall, tall), tall)
                branch = jnp.maximum(acc[0, span, :], 0.0).astype(BF16)
                acc[0, span, :] = offset_ref[...] + jnp.dot(branch, w_proj[0:width, :], preferred_element_type=F32)

        for at, (start, stop) in (
            (chunks // 2, (0, chunks // 2)), (chunks - 2, (chunks // 2, chunks - 2)), (chunks - 1, (chunks - 2, chunks - 1))
        ):
            @pl.when(c == at)
            def _(start=start * CHUNK, stop=stop * CHUNK):
                for k in range(3):
                    @pl.loop(0, cells // tall)
                    def _(m, k=k):
                        span = pl.ds(pl.multiple_of(m * tall, tall), tall)
                        part = jnp.dot(depth[k, span, start:stop], w_rates[k, start:stop, :], preferred_element_type=F32)
                        acc[k + 1, span, :] = part if start == 0 else acc[k + 1, span, :] + part

        lanes = pl.ds(pl.multiple_of(c * CHUNK, CHUNK), CHUNK)
        widen(feat, edge, cells, lanes)

        def take(side, present):
            @pl.when(present)
            def _():
                halo_copy(side, c).wait_recv()
                widen(halo.at[side], 0 if side == 0 else edge + cells, edge, lanes)

        def map_rows(late):
            for part in range(CHUNK // 128):
                inner = slice(part * 128, part * 128 + 128)
                outer = pl.ds(pl.multiple_of(c * CHUNK + part * 128, 128), 128)
                for k, d in enumerate(RATES):
                    taps = [
                        jnp.broadcast_to(w_depth_ref[t, k : k + 1, outer].astype(F32), (8, 128)) for t in range(9)
                    ]

                    def weigh(parts, column, taps=taps):
                        total = None
                        for i in range(3):
                            tap = jnp.concatenate([taps[3 * i + column]] * (parts[i].shape[0] // 8), axis=0)
                            term = parts[i] * tap
                            total = term if total is None else total + term
                        return total

                    def two_rows(pair, d=d, weigh=weigh, inner=inner, outer=outer, k=k):
                        results = []
                        for r in range(2):
                            parts = []
                            for i in (-1, 0, 1):
                                start = pl.multiple_of((REACH + i * d + r) * cols + pair * (2 * cols), 8)
                                parts.append(grown[pl.ds(start, cols), inner])
                            low = -(-(cols - d) // 8) * 8
                            high = (d // 8) * 8
                            middle = weigh(parts, 1)
                            left = weigh([p[:low] for p in parts], 0)
                            right = weigh([p[high:] for p in parts], 2)
                            fill = jnp.zeros((d, 128), F32)
                            left = jnp.concatenate([fill, left[: cols - d]], axis=0)
                            right = jnp.concatenate([right[d - high :], fill], axis=0)
                            results.append(jnp.maximum(middle + left + right, 0.0))
                        depth[k, pl.ds(pl.multiple_of(pair * (2 * cols), 16), 2 * cols), outer] = jnp.concatenate(
                            results, axis=0
                        ).astype(BF16)

                    pairs = d // 2 if late else (rows - d) // 2
                    after = core == 1 if late else core == 0
                    first_pair = jnp.where(after, rows // 2 - pairs, 0)
                    unroll = max(u for u in (3, 4, 5) if pairs % u == 0 or pairs % u == 1)
                    for n in range(pairs % unroll):
                        two_rows(first_pair + n)
                    first_pair += pairs % unroll

                    @pl.loop(0, pairs // unroll)
                    def _(n, two_rows=two_rows, first_pair=first_pair, unroll=unroll):
                        for u in range(unroll):
                            two_rows(first_pair + n * unroll + u)

        take(1, has_next & (core == 0))
        take(0, has_prev & (core == 1))
        map_rows(False)
        pass_halo(c + 1)
        take(0, has_prev & (core == 0))
        take(1, has_next & (core == 1))
        map_rows(True)
        return carry

    lax.fori_loop(0, chunks, one_chunk, 0)

    @pl.loop(0, cells // tall)
    def _(m):
        span = pl.ds(pl.multiple_of(m * tall, tall), tall)
        blended = acc[0, span, :]
        for k in range(1, 4):
            branch = acc[k, span, :] + jnp.dot(
                depth[k - 1, span, channels - CHUNK :], w_rates[k - 1, channels - CHUNK :, :], preferred_element_type=F32
            )
            branch = jnp.maximum(branch, 0.0).astype(BF16)
            blended += jnp.dot(branch, w_proj[k * width : (k + 1) * width, :], preferred_element_type=F32)
        aspp_ref[span, :] = jnp.maximum(blended, 0.0).astype(BF16)

    leaving = [
        pltpu.make_async_copy(source, target, out_sem.at[n])
        for n, (source, target) in enumerate(((aspp_ref, aspp_hbm), (context_ref, context_hbm), (refined_ref, refined_hbm)))
    ]
    leaving[0].start()
    leaving[1].start()
    crops_both[core] = jnp.dot(own_pick[...], aspp_ref[...], preferred_element_type=F32).astype(BF16)
    mate_copy(1, crops_both).start()
    steps(low_count, lambda step: color_low(step).wait_recv())

    def add_low(n, total):
        return total + colors_low[n].astype(F32)

    mine_ref[...] = lax.fori_loop(
        0, low_count - 1, add_low, colors_out[pl.ds(pl.multiple_of(chip * 16, 16), 16), :].astype(F32)
    )
    side, pixels = BLK, BLK * BLK
    wide = lax.broadcasted_iota(jnp.int32, (3 * CAP, pixels), 1)
    row_at, col_at = wide >> 5, wide & (side - 1)
    received = mine_ref[...]
    colors = jnp.concatenate([received[4 * n : 4 * n + 3] for n in range(CAP)], axis=0)
    local[11].wait()
    pieces = []
    for i in (-1, 0, 1):
        for j in (-1, 0, 1):
            moved = colors if i == 0 and j == 0 else pltpu.roll(colors, (-(side * i + j)) % pixels, 1)
            inside = (row_at + i >= 0) & (row_at + i < side) & (col_at + j >= 0) & (col_at + j < side)
            pieces.append(jnp.where(inside, moved, 0.0))
    pieces.append(jnp.zeros((128 - 9 * 3 * CAP, pixels), F32))
    spread_colors = jnp.concatenate(pieces, axis=0).T.astype(BF16)
    table_ref[:, 0:128] = (table_ref[:, 0:128].astype(F32) + spread_colors.astype(F32)).astype(BF16)

    mate_copy(1, crops_both).wait_recv()

    @pl.loop(0, CAP)
    def _(block):
        @pl.loop(0, half // 8)
        def _(n):
            rows_of = pl.ds(pl.multiple_of((block * (half // 8) + n) * 128, 128), 128)
            found = jnp.dot(crop_pick[rows_of, :], crops_both[...].reshape(256, width), preferred_element_type=F32)
            crops_out[rows_of, :] = found.astype(BF16)

        steps(half, lambda step: crop_copy(block, half - step).start())

    blank = jnp.zeros((side, 3 * width), BF16)
    for block in range(CAP):
        grids[block, 0:side, :] = blank
        grids[block, side + pixels :, :] = blank
    for n in (9, 10, 12, 13):
        local[n].wait()
    tap_row = lax.broadcasted_iota(jnp.int32, (COLOR_ROWS, 27), 0)
    pixel_tap = lax.broadcasted_iota(jnp.int32, (COLOR_ROWS, 27), 1)
    tap_of = sum((pixel_tap >= 3 * n).astype(jnp.int32) for n in range(1, 9))
    for block in range(CAP):
        wanted = tap_of * (3 * CAP) + 3 * block + pixel_tap - 3 * tap_of
        spread_taps = (tap_row == wanted).astype(F32).astype(BF16)
        taps_ref[block, 0:COLOR_ROWS, :] = jnp.dot(spread_taps, color_ref[...], preferred_element_type=F32).astype(BF16)
    scores[...] = jnp.zeros(scores.shape, F32)
    tall = pixels // PARTS
    col = lax.broadcasted_iota(jnp.int32, (pixels, width), 0) & (side - 1)

    def open_block(block):
        steps(half, lambda step: crop_copy(block, step).wait_recv())

        def add_crop(n, total):
            return total + crops_in[block, n].astype(F32)

        crop = lax.fori_loop(0, half - 1, add_crop, crops_out[crop_rows(block, chip), :].astype(F32)).astype(BF16)
        for tap in range(9):
            part = jnp.dot(crop, first[tap * width : (tap + 1) * width, :], preferred_element_type=F32)
            taps_ref[block, COLOR_ROWS + tap * 16 : COLOR_ROWS + tap * 16 + 16, :] = part.astype(BF16)

    def first_conv(block):
        total = jnp.dot(table_ref[...], taps_ref[block], preferred_element_type=F32)
        total = jnp.maximum(total, 0.0)
        before = jnp.where(col == 0, 0.0, pltpu.roll(total, 1, 0))
        after = jnp.where(col == side - 1, 0.0, pltpu.roll(total, pixels - 1, 0))
        inner = slice(side, side + pixels)
        grids[block, inner, 0:width] = before.astype(BF16)
        grids[block, inner, width : 2 * width] = total.astype(BF16)
        grids[block, inner, 2 * width :] = after.astype(BF16)

    def second_conv(pair, m):
        total = None
        for i in range(3):
            rows_of = pl.ds(pl.multiple_of(m * tall + side * i, side), tall)
            both = jnp.concatenate([grids[2 * pair, rows_of, :], grids[2 * pair + 1, rows_of, :]], axis=0)
            term = jnp.dot(both, second[3 * width * i : 3 * width * (i + 1), :], preferred_element_type=F32)
            total = term if total is None else total + term
        total = jnp.maximum(total, 0.0).astype(BF16)
        found = lax.dot_general(head_ref[...], total, (((1,), (1,)), ((), ())), preferred_element_type=F32)
        wide_part = tall // QUARTERS
        for b in range(2):
            for q in range(QUARTERS):
                start = pl.multiple_of(q * (8 * CAP) + (2 * pair + b) * 8, 8)
                left = b * tall + q * wide_part
                scores[m, pl.ds(start, classes), :] = found[:, left : left + wide_part]

    def back_swap(m):
        scores_both[m, core] = scores[m].astype(BF16)
        mate_copy(2 + m, scores_both.at[m]).start()

    def back_spread(m):
        mate_copy(2 + m, scores_both.at[m]).wait_recv()

        @pl.loop(0, half // 2)
        def _(n):
            rows_of = pl.ds(pl.multiple_of(n * (2 * item), 16), 2 * item)
            found = jnp.dot(back_pick[rows_of, 0:128], scores_both[m, 0], preferred_element_type=F32)
            found += jnp.dot(back_pick[rows_of, 128:256], scores_both[m, 1], preferred_element_type=F32)
            back_out[m, rows_of, :] = found.astype(BF16)
            for t in range(2):
                step = lax.rem(2 * n + t - chip + half, half)

                @pl.when(step > 0)
                def _(step=step):
                    back_copy(m, step).start()


    def back_finish(m):
        steps(half, lambda step: back_copy(m, step).wait_recv())

        def add_back(n, total):
            return total + back_in[m, n].astype(F32)

        result = lax.fori_loop(0, half - 1, add_back, back_out[m, back_rows(chip), :].astype(F32))
        span = item // QUARTERS
        wide_part = pixels // (PARTS * QUARTERS)
        for q in range(QUARTERS):
            for p in range(span // classes):
                start = q * span + p * classes
                left = (m * QUARTERS + q) * wide_part
                refined_ref[:, p, left : left + wide_part] = result[start : start + classes].astype(BF16)

    pairs = CAP // 2

    @pl.loop(0, PARTS * pairs)
    def _(unit):
        m, pair = unit // pairs, lax.rem(unit, pairs)

        @pl.when(m == 0)
        def _():
            @pl.loop(0, 2)
            def _(n):
                open_block(2 * pair + n)
                first_conv(2 * pair + n)

        second_conv(pair, m)

        @pl.when(pair == pairs - 1)
        def _():
            back_swap(m)

        @pl.when((unit >= pairs) & ((pair == 0) | (m == PARTS - 1)))
        def _():
            back_spread(jnp.where(pair == 0, m - 1, m))

    steps(low_count, lambda step: sum_low(step).wait_send())
    steps(HIGH, lambda step: sum_high(step).wait_send())
    sum_mate().wait_send()
    steps(HIGH, lambda step: color_high(step).wait_send())
    steps(low_count, lambda step: color_low(step).wait_send())
    for number, both in enumerate((colors_both, crops_both)):
        mate_copy(number, both).wait_send()

    def drain_crops(block, carry):
        steps(half, lambda step: crop_copy(block, step).wait_send())
        return carry

    lax.fori_loop(0, CAP, drain_crops, 0)

    def drain_halo(c, carry):
        @pl.when(has_next)
        def _():
            halo_copy(0, c).wait_send()

        @pl.when(has_prev)
        def _():
            halo_copy(1, c).wait_send()

        return carry

    lax.fori_loop(0, chunks, drain_halo, 0)
    if low_count == 2:
        def drain_relay(c, carry):
            pass_copy(0, first_relayed + c).wait_send()
            return carry

        lax.fori_loop(0, jnp.where(gives, 0, relayed), drain_relay, 0)

    for m in range(PARTS):
        back_finish(m)
    leaving[2].start()

    for m in range(PARTS):
        steps(half, lambda step, m=m: back_copy(m, step).wait_send())
        mate_copy(2 + m, scores_both.at[m]).wait_send()
    for copy in leaving:
        copy.wait()


def upsample_taps():
    pixels = np.arange(BLK, dtype=np.float32)
    source = np.clip((pixels + 0.5) / 8.0 - 0.5, 0.0, CELLS - 1.0)
    table = np.maximum(1.0 - np.abs(source[:, None] - np.arange(CELLS, dtype=np.float32)[None, :]), 0.0)
    moved = []
    for i in (-1, 0, 1):
        shifted = np.zeros_like(table)
        for p in range(BLK):
            if 0 <= p + i < BLK:
                shifted[p] = table[p + i]
        moved.append(shifted)
    moved = np.stack(moved)
    table = np.einsum("ipa,jqb->pqijab", moved, moved).reshape(BLK * BLK, 9 * CELLS * CELLS)
    return np.pad(table, ((0, 0), (COLOR_ROWS, 0)))


def pyramid(tiles, rows, cols, features, image, blocks, routes, w_one, w_rates, w_depth, w_pool, w_proj,
            w_first, w_color, w_second, w_head):
    channels, width = w_one.shape
    cells = rows * cols
    per = CAP * CELLS * CELLS
    chunks = channels // CHUNK
    edge = REACH * cols
    places = routes.shape[0] // tiles
    classes = w_head.shape[0]
    pixels = BLK * BLK
    item = places * classes * QUARTERS
    low_count = tiles // (2 * HIGH)
    part = pixels // (PARTS * QUARTERS)
    away = pl.BlockSpec(memory_space=pl.ANY)
    dma = pltpu.SemaphoreType.DMA
    image = image.transpose(0, 2, 1).reshape(-1, image.shape[1])
    first, second = w_first.reshape(9 * width, width), w_second.reshape(9 * width, width)
    operands = (
        features.reshape(cells, channels), w_one, w_rates, w_depth.transpose(1, 0, 2), w_pool, w_proj, image, first, second,
        w_color, w_head, jnp.asarray(upsample_taps(), BF16), blocks.T, routes.T,
    )

    links = low_count + HIGH
    half = tiles // 2
    return pl.pallas_call(
        functools.partial(pyramid_kernel, tiles, rows, cols, channels, width),
        out_shape=(
            jax.ShapeDtypeStruct((cells, width), BF16),
            jax.ShapeDtypeStruct((1, width), F32),
            jax.ShapeDtypeStruct((classes, places, pixels), BF16),
        ),
        in_specs=[away] * len(operands),
        out_specs=(away, away, away),
        scratch_shapes=[
            pltpu.VMEM((cells, width), BF16),
            pltpu.VMEM((1, width), F32),
            pltpu.VMEM((classes, places, pixels), BF16),
            dma((3,)),
            *(pltpu.VMEM(operand.shape, operand.dtype) for operand in operands),
            pltpu.VMEM((2, edge, channels), BF16),
            pltpu.VMEM((cells + 2 * edge, CHUNK), F32),
            pltpu.VMEM((3, cells, channels), BF16),
            pltpu.VMEM((4, cells, width), F32),
            pltpu.VMEM((3, 1, channels), F32),
            pltpu.VMEM((links - 1, 1, channels), F32),
            pltpu.VMEM((32, pixels), F32),
            pltpu.VMEM((128, cells), BF16),
            pltpu.VMEM((half * per, 256), BF16),
            pltpu.VMEM((half * item, 256), BF16),
            pltpu.VMEM((16, pixels), F32),
            pltpu.VMEM((1, width), F32),
            pltpu.VMEM((CAP, COLOR_ROWS + 144, width), BF16),
            pltpu.VMEM((CAP, pixels + 2 * BLK, 3 * width), BF16),
            pltpu.VMEM((PARTS, QUARTERS * CAP * 8, part), F32),
            pltpu.VMEM((2, 32, pixels), BF16),
            pltpu.VMEM((half * 16, pixels), BF16),
            pltpu.VMEM((HIGH - 1, low_count * 16, pixels), BF16),
            pltpu.VMEM((low_count - 1, 16, pixels), BF16),
            pltpu.VMEM((2, 128, width), BF16),
            pltpu.VMEM((half * per, width), BF16),
            pltpu.VMEM((CAP, half - 1, 16, width), BF16),
            pltpu.VMEM((PARTS, 2, QUARTERS * CAP * 8, part), BF16),
            pltpu.VMEM((PARTS, half * item, part), BF16),
            pltpu.VMEM((PARTS, half - 1, item, part), BF16),
            dma((len(operands),)),
            dma((2, chunks)),
            dma((2, chunks)),
            *(dma((links,)) for _ in range(4)),
            *(dma((CAP, half)) for _ in range(2)),
            *(dma((PARTS, half)) for _ in range(2)),
            *(dma((2 + PARTS,)) for _ in range(2)),
            pltpu.VMEM((2 * HIGH - 1, edge, CHUNK), BF16),
            *(dma((2 * HIGH - 1,)) for _ in range(2)),
        ],
        compiler_params=pltpu.CompilerParams(collective_id=0, has_side_effects=True, vmem_limit_bytes=60 << 20),
        name="pyramid",
    )(*operands)


def settle_kernel(*refs):
    half = len(refs) // 2
    for source, target in zip(refs[:half], refs[half:]):
        target[...] = source[...]


def settle(*arrays):
    return pl.pallas_call(
        settle_kernel,
        out_shape=tuple(jax.ShapeDtypeStruct(a.shape, a.dtype) for a in arrays),
        name="settle",
    )(*arrays)


def shards(
    tiles,
    features,
    aerial_image,
    blocks,
    routes,
    w_one,
    w_depth,
    w_rates,
    w_pool,
    w_proj,
    w_first,
    w_color,
    w_second,
    w_head,
):
    rows, cols, channels = features.shape
    width = w_one.shape[1]
    aspp, context, refined = pyramid(
        tiles, rows, cols, features, aerial_image, blocks, routes, w_one, w_rates, w_depth, w_pool, w_proj,
        w_first[0], w_color[0], w_second[0], w_head[0],
    )
    aspp, context, refined = settle(aspp, context, refined)
    return aspp.reshape(rows, cols, width), context.reshape(width), refined.transpose(1, 0, 2)


def solution(mesh):
    return jax.shard_map(
        functools.partial(shards, mesh.shape["tile"]),
        mesh=mesh,
        in_specs=(
            P(("groups", "tile"), None, None),
            P(None, ("groups", "tile"), None),
            P("groups", None),
            P("groups", None),
            P(),
            P(),
            P(),
            P(),
            P(),
            P("tile", None, None, None),
            P("tile", None, None),
            P("tile", None, None, None),
            P("tile", None, None),
        ),
        out_specs=(
            P(("groups", "tile"), None, None),
            P("groups"),
            P(("groups", "tile"), None, None),
        ),
        check_vma=False,
    )
```
